128 devices in a mesh: segment: 8 (over y, x_hi), tp: 16 (over x_lo, z, core).
Axes of the slice: x: 4 (x_hi: 2, x_lo: 2; x = x_hi * 2 + x_lo), y: 4, z: 4, core: 2. Of those that a mesh axis runs over, the one named last changes fastest.
Arguments:
- memory: bfloat16 [1024, 4096], P('segment', 'tp'), may hold values from -6 to 6
- norm_gain: float32 [4096], replicated, may hold values from 0.1 to 1.9
- queries: bfloat16 [8, 1024, 4096], P('segment', None, 'tp'), may hold values from -200 to 200
- key_weight: bfloat16 [8, 4096, 4096], P('segment', None, 'tp'), may hold values from -0.09375 to 0.09375
- value_weight: bfloat16 [8, 4096, 4096], P('segment', None, 'tp'), may hold values from -0.09375 to 0.09375
- context_grad: bfloat16 [8, 1024, 4096], P('segment', None, 'tp'), may hold values from -6 to 6
Outputs:
- context: bfloat16 [8, 1024, 4096], P('segment', None, 'tp')
- query_grad: bfloat16 [8, 1024, 4096], P('segment', None, 'tp')
- key_weight_grad: float32 [8, 4096, 4096], P('segment', None, 'tp')
- value_weight_grad: float32 [8, 4096, 4096], P('segment', None, 'tp')
- encoder_output_gradient: float32 [1024, 4096], P('segment', 'tp')
The draws below stay inside these ranges and needn't reach their ends.
All inputs are finite; a program needn't handle non-finite values.
Results may differ from the reference program's by a relative error of at most 0.015.
The reference program's roundings to bfloat16 on the way (of `normed`, `attend_low` and `grad_scores`) count: a program that leaves them out, or rounds other values in their place, can miss the bound.
Values may be sent and summed in bfloat16 or wider, within the bound.
No kernel may reach another device: no remote copies, remote signals or barrier semaphores. Data moves between devices by JAX's collectives and lax.ppermute only.
A program may use at most 128 MiB of HBM per device.

```python
import jax
import jax.numpy as jnp
from jax import lax

D = 4096
HD = 256
HEADS = 16
TGT = 1024
SRC = 1024
SECTIONS = 8
N_SEGMENT = 8


def draw_queries(key, part):
    base = jax.random.truncated_normal(jax.random.fold_in(key, 11), -6.0, 6.0, (N_SEGMENT, TGT, D), jnp.float32)
    return base.astype(jnp.bfloat16)


def block_levels(rng, dims, split, low, largest):
    gain = 1.0
    for axis_at, blocks in split:
        heights = jax.random.uniform(jax.random.fold_in(jax.random.fold_in(rng, 6), axis_at), (blocks,), jnp.float32, low / len(split), largest / len(split))
        gain = gain * jnp.repeat(jnp.exp(heights), dims[axis_at] // blocks).reshape((-1,) + (1,) * (len(dims) - 1 - axis_at))
    return gain


def centred(own_key, dims, scale, limit, shards=(), dtype=jnp.bfloat16):
    factor_of = block_levels(own_key, dims, shards, -0.22, 0.18) if shards else 1.0
    result = jax.random.normal(own_key, dims, jnp.float32) * scale * factor_of
    return jnp.minimum(jnp.maximum(result, -limit), limit).astype(dtype)


def setup_inputs(seed: int = 0) -> dict:
    arg_keys = jax.random.split(jax.random.key(seed), 7)
    memory = centred(arg_keys[0], (SRC, D), 1.0, 6.0, ((0, 8), (1, 16)))
    norm_gain = jnp.clip(1.0 + 0.18 * jax.random.normal(arg_keys[1], (D,), jnp.float32), 0.1, 1.9)
    queries = draw_queries(jax.random.fold_in(arg_keys[6], 71), 0)
    key_weight = centred(arg_keys[3], (SECTIONS, D, D), D ** -0.5, 0.09375, ((0, 8), (2, 16)))
    value_weight = centred(arg_keys[4], (SECTIONS, D, D), D ** -0.5, 0.09375, ((0, 8), (2, 16)))
    context_grad = centred(arg_keys[5], (SECTIONS, TGT, D), 1.0, 6.0, ((0, 8), (2, 16)))
    return dict(memory=memory, norm_gain=norm_gain, queries=queries, key_weight=key_weight, value_weight=value_weight, context_grad=context_grad)


def section_pass(normed, items):
    query_rows, key_mat, value_mat, dctx = items
    key_rows = jnp.dot(normed, key_mat, preferred_element_type=jnp.float32).astype(jnp.bfloat16)
    value_rows = jnp.dot(normed, value_mat, preferred_element_type=jnp.float32).astype(jnp.bfloat16)
    scale = HD ** (-0.5)
    qh = query_rows.reshape(TGT, HEADS, HD).astype(jnp.float32)
    kh = key_rows.reshape(SRC, HEADS, HD).astype(jnp.float32)
    vh = value_rows.reshape(SRC, HEADS, HD).astype(jnp.float32)
    dch = dctx.reshape(TGT, HEADS, HD).astype(jnp.float32)
    scores = jnp.einsum('qhd,khd->hqk', qh, kh) * scale
    maxima = lax.optimization_barrier(jnp.max(scores, axis=-1, keepdims=True))
    exponent = jnp.exp(scores - maxima)
    attend = exponent / lax.optimization_barrier(jnp.sum(exponent, axis=-1, keepdims=True))
    attend_low = attend.astype(jnp.bfloat16)
    context = jnp.einsum('hqk,khd->qhd', attend_low.astype(jnp.float32), vh).astype(jnp.bfloat16)
    grad_attend = jnp.einsum('qhd,khd->hqk', dch, vh)
    row_dots = lax.optimization_barrier(jnp.sum(grad_attend * attend, axis=-1, keepdims=True))
    grad_scores = (attend * (grad_attend - row_dots) * scale).astype(jnp.bfloat16).astype(jnp.float32)
    query_grad = jnp.einsum('hqk,khd->qhd', grad_scores, kh).astype(jnp.bfloat16)
    grad_keys = jnp.einsum('hqk,qhd->khd', grad_scores, qh).astype(jnp.bfloat16).reshape(SRC, D)
    grad_values = jnp.einsum('hqk,qhd->khd', attend_low.astype(jnp.float32), dch).astype(jnp.bfloat16).reshape(SRC, D)
    key_grad = jnp.dot(normed.T, grad_keys, preferred_element_type=jnp.float32)
    value_grad = jnp.dot(normed.T, grad_values, preferred_element_type=jnp.float32)
    grad_normed = jnp.dot(grad_keys, key_mat.T, preferred_element_type=jnp.float32)
    grad_normed = grad_normed + jnp.dot(grad_values, value_mat.T, preferred_element_type=jnp.float32)
    return (context.reshape(TGT, D), query_grad.reshape(TGT, D), key_grad, value_grad, grad_normed)

def reference(memory, norm_gain, queries, key_weight, value_weight, context_grad):
    encoder_states = memory.astype(jnp.float32)
    row_inverse_scale = lax.rsqrt(lax.optimization_barrier(jnp.mean(encoder_states * encoder_states, axis=1)) + 1e-06)
    normed = (encoder_states * row_inverse_scale[:, None] * norm_gain).astype(jnp.bfloat16)
    context, query_grad, key_grad, value_grad, grad_parts = lax.map(lambda items: section_pass(normed, items), (queries, key_weight, value_weight, context_grad))
    grad_normed = lax.optimization_barrier(jnp.sum(grad_parts, axis=0))
    upper_term = grad_normed * norm_gain
    centered_normalized = encoder_states * row_inverse_scale[:, None]
    row_average = lax.optimization_barrier(jnp.mean(upper_term * centered_normalized, axis=1))
    encoder_output_gradient = row_inverse_scale[:, None] * (upper_term - centered_normalized * row_average[:, None])
    return (context, query_grad, key_grad, value_grad, encoder_output_gradient)
```

```python
import functools

import jax
import jax.numpy as jnp
from jax import lax
from jax.experimental import pallas as pl
from jax.experimental.pallas import tpu as pltpu
from jax.sharding import Mesh
from jax.sharding import PartitionSpec as P

HD = 256
AXES = ("y", "xh", "xl", "z", "c")
CHIPS = ("y", "xh", "xl", "z")
EPS = 1e-06
F32 = jnp.float32
BF16 = jnp.bfloat16
VMEM_LIMIT = 56 * 2**20


def params():
    return pltpu.CompilerParams(vmem_limit_bytes=VMEM_LIMIT)


def nn(a, b):
    return lax.dot_general(a, b, (((1,), (0,)), ((), ())), preferred_element_type=F32)


def nt(a, b):
    return lax.dot_general(a, b, (((1,), (1,)), ((), ())), preferred_element_type=F32)


def tn(a, b):
    return lax.dot_general(a, b, (((0,), (0,)), ((), ())), preferred_element_type=F32)


def project_body(blocks, x_ref, gain_ref, ko_ref, vo_ref, ks_ref, vs_ref,
                 own_ref, sib_ref, normed_ref, scale_ref, held, acc_own, acc_sib, squares):
    i = pl.program_id(0)
    rows, width = held.shape[1:]

    @pl.when(i == 0)
    def _():
        squares[...] = jnp.zeros_like(squares)
        acc_own[...] = jnp.zeros_like(acc_own)
        acc_sib[...] = jnp.zeros_like(acc_sib)

    @pl.when(i < blocks)
    def _():
        block = x_ref[:, 0].reshape(rows, width)
        held[i] = block
        wide = block.astype(F32)
        squares[...] += jnp.sum(wide * wide, axis=1, keepdims=True)

    @pl.when(i == blocks)
    def _():
        scale_ref[...] = lax.rsqrt(squares[...] / (blocks * width) + EPS)

    @pl.when(i >= blocks)
    def _():
        block = (held[i - blocks].astype(F32) * scale_ref[...] * gain_ref[0]).astype(BF16)
        normed_ref[0] = block
        acc_own[:, :HD] += nn(block, ko_ref[...])
        acc_own[:, HD:] += nn(block, vo_ref[...])
        acc_sib[:, :HD] += nn(block, ks_ref[...])
        acc_sib[:, HD:] += nn(block, vs_ref[...])

    @pl.when(i == 2 * blocks - 1)
    def _():
        own_ref[...] = acc_own[...].astype(BF16)
        sib_ref[...] = acc_sib[...].astype(BF16)


def project(x, gain, key_own, value_own, key_sib, value_sib):
    segs, blocks, part, width = x.shape
    rows = segs * part
    late = lambda i: jnp.maximum(i - blocks, 0)
    weight = pl.BlockSpec((width, HD), lambda i: (late(i), 0))
    whole = pl.BlockSpec((rows, 2 * HD), lambda i: (0, 0))
    return pl.pallas_call(
        functools.partial(project_body, blocks),
        grid=(2 * blocks,),
        in_specs=[
            pl.BlockSpec((segs, 1, part, width), lambda i: (0, jnp.minimum(i, blocks - 1), 0, 0)),
            pl.BlockSpec((1, 1, width), lambda i: (late(i), 0, 0)),
            weight, weight, weight, weight,
        ],
        out_specs=[
            whole, whole,
            pl.BlockSpec((1, rows, width), lambda i: (late(i), 0, 0)),
            pl.BlockSpec((rows, 1), lambda i: (0, 0)),
        ],
        out_shape=[
            jax.ShapeDtypeStruct((rows, 2 * HD), BF16),
            jax.ShapeDtypeStruct((rows, 2 * HD), BF16),
            jax.ShapeDtypeStruct((blocks, rows, width), BF16),
            jax.ShapeDtypeStruct((rows, 1), F32),
        ],
        scratch_shapes=[
            pltpu.VMEM((blocks, rows, width), BF16),
            pltpu.VMEM((rows, 2 * HD), F32),
            pltpu.VMEM((rows, 2 * HD), F32),
            pltpu.VMEM((rows, 1), F32),
        ],
        compiler_params=params(),
        cost_estimate=pl.CostEstimate(flops=2 * rows * blocks * width * 4 * HD, bytes_accessed=16 * 2**20, transcendentals=0),
        name="project",
    )(x, gain.reshape(blocks, 1, width), key_own, value_own, key_sib, value_sib)


def attend_body(q_ref, dc_ref, near_ref, far_ref, ctx_ref, qg_ref, gnear_ref, gfar_ref,
                keys, values, gkeys, gvalues):
    i = pl.program_id(0)
    half = near_ref.shape[0]
    scale = HD ** (-0.5)

    @pl.when(i == 0)
    def _():
        keys[:half] = near_ref[:, :HD]
        keys[half:] = far_ref[:, :HD]
        values[:half] = near_ref[:, HD:]
        values[half:] = far_ref[:, HD:]
        gkeys[...] = jnp.zeros_like(gkeys)
        gvalues[...] = jnp.zeros_like(gvalues)

    q, dc, k, v = q_ref[...], dc_ref[...], keys[...], values[...]
    scores = nt(q, k) * scale
    expo = jnp.exp(scores - jnp.max(scores, axis=-1, keepdims=True))
    attend = expo / jnp.sum(expo, axis=-1, keepdims=True)
    low = attend.astype(BF16)
    ctx_ref[...] = nn(low, v).astype(BF16)
    gattend = nt(dc, v)
    dots = jnp.sum(gattend * attend, axis=-1, keepdims=True)
    gscores = (attend * (gattend - dots) * scale).astype(BF16)
    qg_ref[...] = nn(gscores, k).astype(BF16)
    gkeys[...] += tn(gscores, q)
    gvalues[...] += tn(low, dc)

    @pl.when(i == pl.num_programs(0) - 1)
    def _():
        gnear_ref[:, :HD] = gkeys[:half].astype(BF16)
        gnear_ref[:, HD:] = gvalues[:half].astype(BF16)
        gfar_ref[:, :HD] = gkeys[half:].astype(BF16)
        gfar_ref[:, HD:] = gvalues[half:].astype(BF16)


def attention(q, dc, near, far, tile=256):
    targets, half = q.shape[0], near.shape[0]
    tiled = pl.BlockSpec((tile, HD), lambda i: (i, 0))
    whole = pl.BlockSpec((half, 2 * HD), lambda i: (0, 0))
    return pl.pallas_call(
        attend_body,
        grid=(targets // tile,),
        in_specs=[tiled, tiled, whole, whole],
        out_specs=[tiled, tiled, whole, whole],
        out_shape=[jax.ShapeDtypeStruct((targets, HD), BF16)] * 2
        + [jax.ShapeDtypeStruct((half, 2 * HD), BF16)] * 2,
        scratch_shapes=[pltpu.VMEM((2 * half, HD), BF16)] * 2 + [pltpu.VMEM((2 * half, HD), F32)] * 2,
        compiler_params=params(),
        cost_estimate=pl.CostEstimate(flops=12 * targets * 2 * half * HD, bytes_accessed=8 * 2**20, transcendentals=targets * 2 * half),
        name="attention",
    )(q, dc, near, far)


def back_body(own_ref, sib_ref, ko_ref, vo_ref, ks_ref, vs_ref, out_ref):
    total = nt(own_ref[:, :HD], ko_ref[...])
    total += nt(own_ref[:, HD:], vo_ref[...])
    total += nt(sib_ref[:, :HD], ks_ref[...])
    total += nt(sib_ref[:, HD:], vs_ref[...])
    out_ref[:, 0] = total.astype(BF16).reshape(out_ref.shape[0], *out_ref.shape[2:])


def back(own, sib, key_own, value_own, key_sib, value_sib, segs, blocks):
    rows = own.shape[0]
    width = key_own.shape[0] // blocks
    weight = pl.BlockSpec((width, HD), lambda i: (i, 0))
    whole = pl.BlockSpec((rows, 2 * HD), lambda i: (0, 0))
    return pl.pallas_call(
        back_body,
        grid=(blocks,),
        in_specs=[whole, whole, weight, weight, weight, weight],
        out_specs=pl.BlockSpec((segs, 1, rows // segs, width), lambda i: (0, i, 0, 0)),
        out_shape=jax.ShapeDtypeStruct((segs, blocks, rows // segs, width), BF16),
        compiler_params=params(),
        cost_estimate=pl.CostEstimate(flops=2 * rows * blocks * width * 4 * HD, bytes_accessed=14 * 2**20, transcendentals=0),
        name="back",
    )(own, sib, key_own, value_own, key_sib, value_sib)


def weights_body(near_ref, far_ref, gnear_ref, gfar_ref, gk_ref, gv_ref):
    total = tn(near_ref[0], gnear_ref[...]) + tn(far_ref[0], gfar_ref[...])
    gk_ref[...] = total[:, :HD]
    gv_ref[...] = total[:, HD:]


def weight_grads(near, far, gnear, gfar):
    blocks, rows, width = near.shape
    block = pl.BlockSpec((1, rows, width), lambda i: (i, 0, 0))
    whole = pl.BlockSpec((rows, 2 * HD), lambda i: (0, 0))
    out = pl.BlockSpec((width, HD), lambda i: (i, 0))
    return pl.pallas_call(
        weights_body,
        grid=(blocks,),
        in_specs=[block, block, whole, whole],
        out_specs=[out, out],
        out_shape=[jax.ShapeDtypeStruct((blocks * width, HD), F32)] * 2,
        compiler_params=params(),
        cost_estimate=pl.CostEstimate(flops=8 * rows * blocks * width * HD, bytes_accessed=17 * 2**20, transcendentals=0),
        name="weight_grads",
    )(near, far, gnear, gfar)


def swapped(value):
    return lax.ppermute(value, "c", [(0, 1), (1, 0)])


def local(memory, norm_gain, queries, key_weight, value_weight, context_grad):
    hidden = norm_gain.shape[0]
    rows_own, cols_own = memory.shape
    half, width = rows_own // 2, 2 * cols_own
    core = lax.axis_index("c")
    segment = lax.axis_index(("y", "xh"))
    pair = lax.axis_index(("xl", "z"))
    segs = lax.axis_size(("y", "xh"))
    blocks = lax.axis_size(("xl", "z"))
    key_own, value_own = key_weight[0], value_weight[0]
    halves = memory.reshape(2, half, cols_own)
    mine = lax.dynamic_index_in_dim(halves, core, 0, keepdims=False)
    other = swapped(lax.dynamic_index_in_dim(halves, 1 - core, 0, keepdims=False))
    key_sib, value_sib = swapped(key_own), swapped(value_own)
    block = jnp.where(
        core == 0, jnp.concatenate([mine, other], axis=1), jnp.concatenate([other, mine], axis=1)
    )
    copies = jnp.broadcast_to(block, (segs * blocks, half, width))
    everything = lax.all_to_all(copies, CHIPS, 0, 0, tiled=True).reshape(segs, blocks, half, width)
    own, sib, normed, scale = project(everything, norm_gain, key_own, value_own, key_sib, value_sib)
    far = swapped(sib)
    normed_far = swapped(normed)
    context, query_grad, gnear, gfar = attention(queries[0], context_grad[0], own, far)
    gsib = swapped(gfar)
    parts = back(gnear, gsib, key_own, value_own, key_sib, value_sib, segs, blocks)
    arrived = lax.all_to_all(parts.reshape(segs * blocks, half, width), CHIPS, 0, 0, tiled=True)
    key_grad, value_grad = weight_grads(normed, normed_far, gnear, gfar)
    summed = jnp.sum(arrived.astype(F32), axis=0)
    own_gain = lax.dynamic_slice_in_dim(norm_gain, pair * width, width)
    own_scale = lax.dynamic_slice_in_dim(scale, segment * half, half)
    upper = summed * own_gain
    centered = block.astype(F32) * own_scale
    inner = jnp.sum(upper * centered, axis=1)
    inner = lax.all_to_all(jnp.broadcast_to(inner, (blocks, half)), ("xl", "z"), 0, 0, tiled=True).sum(axis=0)
    result = own_scale * (upper - centered * (inner / hidden)[:, None])
    result = jnp.moveaxis(result.reshape(half, 2, cols_own), 1, 0)
    kept = lax.dynamic_index_in_dim(result, core, 0, keepdims=False)
    came = swapped(lax.dynamic_index_in_dim(result, 1 - core, 0, keepdims=False))
    result = jnp.where(core == 0, jnp.concatenate([kept, came]), jnp.concatenate([came, kept]))
    return context[None], query_grad[None], key_grad[None], value_grad[None], result


def solution(mesh):
    fine = Mesh(mesh.devices.reshape(4, 2, 2, 4, 2), AXES)
    seg, tp = ("y", "xh"), ("xl", "z", "c")
    heads = P(seg, None, tp)
    return jax.shard_map(
        local,
        mesh=fine,
        in_specs=(P(seg, tp), P(), heads, heads, heads, heads),
        out_specs=(heads, heads, heads, heads, P(seg, tp)),
        check_vma=False,
    )
```

```python
import functools

import jax
import jax.numpy as jnp
from jax import lax
from jax.experimental import pallas as pl
from jax.experimental.pallas import tpu as pltpu
from jax.sharding import Mesh
from jax.sharding import PartitionSpec as P

HD = 256
AXES = ("y", "xh", "xl", "z", "c")
PLANE = ("y", "xh", "xl")
RING = 4
EPS = 1e-06
F32 = jnp.float32
BF16 = jnp.bfloat16
MIB = 2**20


def nn(a, b):
    return lax.dot_general(a, b, (((1,), (0,)), ((), ())), preferred_element_type=F32)


def nt(a, b):
    return lax.dot_general(a, b, (((1,), (1,)), ((), ())), preferred_element_type=F32)


def tn(a, b):
    return lax.dot_general(a, b, (((0,), (0,)), ((), ())), preferred_element_type=F32)


def project_body(pieces, z_ref, gain_ref, *refs):
    xs = refs[: len(pieces)]
    w_own, w_sib, own_ref, sib_ref, scale_ref, normed_ref = refs[len(pieces) : len(pieces) + 6]
    held, rows_low, weights, x_sem, w_sem, out_sem = refs[len(pieces) + 6 :]
    blocks, segs, part, width = held.shape
    rows = segs * part
    z = z_ref[0]
    loads = [pltpu.make_async_copy(w, weights.at[i], w_sem.at[i]) for i, w in enumerate((w_own, w_sib))]
    copies = []
    for (distance, first, depth), x in zip(pieces, xs):
        for side in range(2):
            place = side * RING + lax.rem(z + distance, RING)
            source = x.at[:, side] if depth is None else x.at[:, side, depth]
            target = held.at[place, pl.ds(first, source.shape[0])]
            copies.append(pltpu.make_async_copy(source, target, x_sem.at[len(copies)]))
    for copy in copies:
        copy.start()
    for load in loads:
        load.start()
    for copy in copies:
        copy.wait()
    squares = jnp.zeros((rows, 128), F32)
    for p in range(blocks):
        wide = held[p].reshape(rows, width).astype(F32)
        wide = wide * wide
        for i in range(width // 128):
            squares += wide[:, i * 128 : (i + 1) * 128]
    scale = lax.rsqrt(jnp.sum(squares, axis=1, keepdims=True) / (blocks * width) + EPS)
    scale_ref[...] = scale
    for p in range(blocks):
        wide = held[p].reshape(rows, width).astype(F32)
        rows_low[:, p * width : (p + 1) * width] = (wide * scale * gain_ref[p]).astype(BF16)
    out = pltpu.make_async_copy(rows_low, normed_ref, out_sem)
    out.start()
    for load, out_ref, i in zip(loads, (own_ref, sib_ref), range(2)):
        load.wait()
        for j in range(out_ref.shape[1] // HD):
            out_ref[:, j * HD : (j + 1) * HD] = nn(rows_low[...], weights[i, :, j * HD : (j + 1) * HD]).astype(BF16)
    out.wait()


def project(pieces, xs, z, gain, w_own, w_sib, segs, name):
    part, width = xs[0].shape[-2:]
    blocks = gain.shape[0] // width
    rows = segs * part
    anywhere = pl.BlockSpec(memory_space=pl.ANY)
    vmem = pl.BlockSpec(memory_space=pltpu.VMEM)
    return pl.pallas_call(
        functools.partial(project_body, pieces),
        in_specs=[pl.BlockSpec(memory_space=pltpu.SMEM), vmem] + [anywhere] * (len(xs) + 2),
        out_specs=[vmem, vmem, vmem, anywhere],
        out_shape=[
            jax.ShapeDtypeStruct((rows, 2 * HD), BF16),
            jax.ShapeDtypeStruct((rows, 2 * HD), BF16),
            jax.ShapeDtypeStruct((rows, 1), F32),
            jax.ShapeDtypeStruct((rows, blocks * width), BF16),
        ],
        scratch_shapes=[
            pltpu.VMEM((blocks, segs, part, width), BF16),
            pltpu.VMEM((rows, blocks * width), BF16),
            pltpu.VMEM((2, blocks * width, 2 * HD), BF16),
            pltpu.SemaphoreType.DMA((2 * len(xs),)),
            pltpu.SemaphoreType.DMA((2,)),
            pltpu.SemaphoreType.DMA(()),
        ],
        compiler_params=pltpu.CompilerParams(vmem_limit_bytes=24 * MIB),
        cost_estimate=pl.CostEstimate(flops=2 * rows * blocks * width * 4 * HD, bytes_accessed=12 * MIB, transcendentals=0),
        name=name,
    )(z, gain.reshape(blocks, 1, width), *xs, w_own, w_sib)


def attend_body(q_ref, dc_ref, near_a, near_b, far_a, far_b, ctx_ref, qg_ref, gnear_ref, gfar_ref,
                keys, values, gkeys, gvalues):
    i = pl.program_id(0)
    part = near_a.shape[0]
    scale = HD ** (-0.5)

    @pl.when(i == 0)
    def _():
        for j, ref in enumerate((near_a, near_b, far_a, far_b)):
            keys[j * part : (j + 1) * part] = ref[:, :HD]
            values[j * part : (j + 1) * part] = ref[:, HD:]
        gkeys[...] = jnp.zeros_like(gkeys)
        gvalues[...] = jnp.zeros_like(gvalues)

    q, dc, k, v = q_ref[...], dc_ref[...], keys[...], values[...]
    scores = nt(q, k) * scale
    expo = jnp.exp(scores - jnp.max(scores, axis=-1, keepdims=True))
    attend = expo / jnp.sum(expo, axis=-1, keepdims=True)
    low = attend.astype(BF16)
    ctx_ref[...] = nn(low, v).astype(BF16)
    gattend = nt(dc, v)
    dots = jnp.sum(gattend * attend, axis=-1, keepdims=True)
    gscores = (attend * (gattend - dots) * scale).astype(BF16)
    qg_ref[...] = nn(gscores, k).astype(BF16)
    gkeys[...] += tn(gscores, q)
    gvalues[...] += tn(low, dc)

    @pl.when(i == pl.num_programs(0) - 1)
    def _():
        half = 2 * part
        gnear_ref[:, :HD] = gkeys[:half].astype(BF16)
        gnear_ref[:, HD:] = gvalues[:half].astype(BF16)
        gfar_ref[:, :HD] = gkeys[half:].astype(BF16)
        gfar_ref[:, HD:] = gvalues[half:].astype(BF16)


def attention(q, dc, near_a, near_b, far_a, far_b, tile=256):
    targets, half = q.shape[0], 2 * near_a.shape[0]
    tiled = pl.BlockSpec((tile, HD), lambda i: (i, 0))
    quarter = pl.BlockSpec((half // 2, 2 * HD), lambda i: (0, 0))
    whole = pl.BlockSpec((half, 2 * HD), lambda i: (0, 0))
    return pl.pallas_call(
        attend_body,
        grid=(targets // tile,),
        in_specs=[tiled, tiled] + [quarter] * 4,
        out_specs=[tiled, tiled, whole, whole],
        out_shape=[jax.ShapeDtypeStruct((targets, HD), BF16)] * 2
        + [jax.ShapeDtypeStruct((half, 2 * HD), BF16)] * 2,
        scratch_shapes=[pltpu.VMEM((2 * half, HD), BF16)] * 2 + [pltpu.VMEM((2 * half, HD), F32)] * 2,
        compiler_params=pltpu.CompilerParams(vmem_limit_bytes=24 * MIB),
        cost_estimate=pl.CostEstimate(flops=12 * targets * 2 * half * HD, bytes_accessed=8 * MIB, transcendentals=targets * 2 * half),
        name="attention",
    )(q, dc, near_a, near_b, far_a, far_b)


def back_body(order, lands, z_ref, own_ref, sib_ref, o0_ref, o1_ref, s0_ref, s1_ref, *outs):
    del z_ref
    step = pl.program_id(0)
    own, sib = own_ref[...], sib_ref[...]
    sides = []
    for wo, ws in ((o0_ref, s0_ref), (o1_ref, s1_ref)):
        sides.append((nn(own, wo[...]) + nn(sib, ws[...])).astype(BF16))
    parts, segs, part, width = 2, 8, own.shape[0] // 16, o0_ref.shape[1]
    for i, distance in enumerate(order):

        @pl.when(step == i)
        def _():
            for index, first in lands[distance]:
                out = outs[index]
                count = out.shape[0]
                for side in range(2):
                    value = sides[side].reshape(parts, segs, part, width)
                    for k in range(parts):
                        piece = value[k, first : first + count]
                        if len(out.shape) == 4:
                            out[:, side, k * part : (k + 1) * part] = piece
                        else:
                            out[:, side, 0, k * part : (k + 1) * part] = piece


def back(z, own, sib, wt_own, wt_sib, feature_half, order, lands, out_shapes, out_specs, name):
    rows, width = own.shape[0], HD

    def column(side):
        def index(i, z_ref):
            distance = jnp.int32(order[0])
            for j in range(1, len(order)):
                distance = jnp.where(i == j, order[j], distance)
            block = side * RING + lax.rem(z_ref[0] + distance, RING)
            return 0, 2 * block + feature_half
        return pl.BlockSpec((2 * HD, width), index)

    whole = pl.BlockSpec((rows, 2 * HD), lambda i, z_ref: (0, 0))
    return pl.pallas_call(
        functools.partial(back_body, order, lands),
        grid_spec=pltpu.PrefetchScalarGridSpec(
            num_scalar_prefetch=1,
            grid=(RING,),
            in_specs=[whole, whole, column(0), column(1), column(0), column(1)],
            out_specs=out_specs,
        ),
        out_shape=out_shapes,
        compiler_params=pltpu.CompilerParams(vmem_limit_bytes=24 * MIB),
        cost_estimate=pl.CostEstimate(flops=2 * rows * 8 * width * 4 * HD, bytes_accessed=7 * MIB, transcendentals=0),
        name=name,
    )(z, own, sib, wt_own, wt_own, wt_sib, wt_sib)


def weights_body(near_a, near_b, far_a, far_b, gnear_ref, gfar_ref, gk_ref, gv_ref):
    part = near_a.shape[0]
    total = tn(near_a[...], gnear_ref[:part]) + tn(near_b[...], gnear_ref[part:])
    total += tn(far_a[...], gfar_ref[:part]) + tn(far_b[...], gfar_ref[part:])
    gk_ref[...] = total[:, :HD]
    gv_ref[...] = total[:, HD:]


def weight_grads(near_a, near_b, far_a, far_b, gnear, gfar, width=512):
    rows, hidden = near_a.shape
    block = pl.BlockSpec((rows, width), lambda i: (0, i))
    whole = pl.BlockSpec((2 * rows, 2 * HD), lambda i: (0, 0))
    out = pl.BlockSpec((width, HD), lambda i: (i, 0))
    return pl.pallas_call(
        weights_body,
        grid=(hidden // width,),
        in_specs=[block] * 4 + [whole, whole],
        out_specs=[out, out],
        out_shape=[jax.ShapeDtypeStruct((hidden, HD), F32)] * 2,
        compiler_params=pltpu.CompilerParams(vmem_limit_bytes=24 * MIB),
        cost_estimate=pl.CostEstimate(flops=16 * rows * hidden * HD, bytes_accessed=17 * MIB, transcendentals=0),
        name="weight_grads",
    )(near_a, near_b, far_a, far_b, gnear, gfar)


def swapped(value):
    return lax.ppermute(value, "c", [(0, 1), (1, 0)])


def shifted(value, by):
    return lax.ppermute(value, "z", [(i, (i + by) % RING) for i in range(RING)])


def exchanged(value, axis, bit):
    size = lax.axis_size(axis)
    return lax.ppermute(value, axis, [(i, i ^ bit) for i in range(size)])


def over_plane(value):
    return lax.all_to_all(value, PLANE, 0, 0, tiled=True)


def local(memory, norm_gain, queries, key_weight, value_weight, context_grad):
    hidden = norm_gain.shape[0]
    rows_own, cols_own = memory.shape
    half, width = rows_own // 2, 2 * cols_own
    part = half // 2
    core, z = lax.axis_index("c"), lax.axis_index("z")
    segment = lax.axis_index(("y", "xh"))
    pair = lax.axis_index(("xl", "z"))
    segs, plane = lax.axis_size(("y", "xh")), lax.axis_size(PLANE)
    z_array = z.astype(jnp.int32).reshape(1)

    halves = memory.reshape(2, half, cols_own)
    mine = lax.dynamic_index_in_dim(halves, core, 0, keepdims=False)
    other = swapped(lax.dynamic_index_in_dim(halves, 1 - core, 0, keepdims=False))
    block = jnp.where(
        core == 0, jnp.concatenate([mine, other], axis=1), jnp.concatenate([other, mine], axis=1)
    )
    first_a = over_plane(jnp.broadcast_to(block[:part], (plane, part, width)))
    high = block[part:]
    near_z = jnp.stack([high, shifted(high, -1), shifted(high, 2), shifted(high, 1)])
    all_b = over_plane(jnp.broadcast_to(near_z, (plane, RING, part, width)))
    all_b = all_b.reshape(segs, 2, RING, part, width)
    low_0, high_0 = first_a[: plane // 2], first_a[plane // 2 :]
    low_3, high_1 = shifted(low_0, 1), shifted(high_0, -1)
    high_3, low_1 = shifted(high_0, 1), shifted(low_0, -1)
    low_2, high_2 = shifted(low_3, 1), shifted(high_1, -1)
    deep = lambda value: value.reshape(segs // 2, 2, part, width)

    w_own = jnp.concatenate([key_weight[0], value_weight[0]], axis=1)
    w_sib = swapped(w_own)
    wt_own, wt_sib = w_own.T, w_sib.T

    pieces_a = [(0, 0, None), (3, 0, None), (3, 4, None), (1, 0, None), (1, 4, None), (2, 0, None), (2, 4, None)]
    xs_a = [first_a.reshape(segs, 2, part, width)] + [deep(v) for v in (low_3, high_3, low_1, high_1, low_2, high_2)]
    own_a, sib_a, scale_a, normed_a = project(pieces_a, xs_a, z_array, norm_gain, w_own, w_sib, segs, "project_a")
    pieces_b = [(d, 0, d) for d in range(RING)]
    own_b, sib_b, scale_b, normed_b = project(pieces_b, [all_b] * RING, z_array, norm_gain, w_own, w_sib, segs, "project_b")
    far_a, far_b = swapped(sib_a), swapped(sib_b)
    context, query_grad, gnear, gfar = attention(queries[0], context_grad[0], own_a, own_b, far_a, far_b)
    gsib = swapped(gfar)

    half_shape = jax.ShapeDtypeStruct((segs // 2, 2, half, HD), BF16)
    half_spec = pl.BlockSpec((segs // 2, 2, half, HD), lambda i, z_ref: (0, 0, 0, 0))
    full_shape = jax.ShapeDtypeStruct((segs, 2, half, HD), BF16)
    full_spec = pl.BlockSpec((segs, 2, half, HD), lambda i, z_ref: (0, 0, 0, 0))
    parts_b, = back(
        z_array, gnear, gsib, wt_own, wt_sib, 1, (0, 1, 2, 3), {d: [(0, 0)] for d in range(RING)},
        [jax.ShapeDtypeStruct((segs, 2, RING, half, HD), BF16)],
        [pl.BlockSpec((segs, 2, 1, half, HD), lambda i, z_ref: (0, 0, i, 0, 0))],
        "back_b",
    )
    opp_low, opp_high, up_low, up_high, down_low, down_high, kept = back(
        z_array, gnear, gsib, wt_own, wt_sib, 0, (2, 1, 3, 0),
        {2: [(0, 0), (1, 4)], 1: [(2, 0), (3, 4)], 3: [(4, 0), (5, 4)], 0: [(6, 0)]},
        [half_shape] * 6 + [full_shape], [half_spec] * 6 + [full_spec],
        "back_a",
    )
    arrived_b = over_plane(parts_b.reshape(plane, RING, half, HD))
    from_low, from_high = shifted(opp_low, 1), shifted(opp_high, -1)
    got_high, got_low = shifted(up_high, 1), shifted(down_low, -1)
    wide = lambda value: value.astype(F32)
    last_low = shifted((wide(up_low) + wide(from_low)).astype(BF16), 1)
    last_high = shifted((wide(down_high) + wide(from_high)).astype(BF16), -1)
    summed_low = wide(kept[: segs // 2]) + wide(got_low) + wide(last_low)
    summed_high = wide(kept[segs // 2 :]) + wide(got_high) + wide(last_high)
    summed_a = jnp.concatenate([summed_low, summed_high]).astype(BF16).reshape(plane, half, HD)

    normed_far_a, normed_far_b = swapped(normed_a), swapped(normed_b)
    key_grad, value_grad = weight_grads(normed_a, normed_b, normed_far_a, normed_far_b, gnear, gfar)

    row_dot = lambda g, a, b: jnp.sum(wide(g) * jnp.concatenate([wide(a), wide(b)]), axis=1)
    inner = row_dot(gnear, own_a, own_b) + swapped(row_dot(gfar, far_a, far_b))
    for axis, bit in (("xl", 1), ("z", 1), ("z", 2), ("xh", 1), ("y", 1), ("y", 2)):
        inner = inner + exchanged(inner, axis, bit)
    inner = lax.dynamic_index_in_dim(inner.reshape(2, segs, part), segment, 1, keepdims=False).reshape(half)

    arrived_b, key_grad, value_grad, inner, summed_a = lax.optimization_barrier(
        (arrived_b, key_grad, value_grad, inner, summed_a)
    )
    arrived_a = over_plane(summed_a)
    near_b = jnp.sum(wide(arrived_b), axis=0).astype(BF16)
    total_b = wide(near_b[0]) + wide(shifted(near_b[1], 1)) + wide(shifted(near_b[2], 2)) + wide(shifted(near_b[3], -1))
    total_a = jnp.sum(wide(arrived_a), axis=0)

    scale = jnp.concatenate(
        [lax.dynamic_slice_in_dim(s, segment * part, part) for s in (scale_a, scale_b)]
    )
    gain = lax.dynamic_slice_in_dim(norm_gain, pair * width, width)
    mean = (inner / hidden)[:, None]

    def finish(total, lo):
        centered = wide(block[:, lo : lo + HD]) * scale
        return scale * (total * gain[lo : lo + HD] - centered * mean)

    left, right = finish(total_a, 0), finish(total_b, HD)
    kept_own = jnp.where(core == 0, left, right)
    came = swapped(jnp.where(core == 0, right, left))
    result = jnp.where(core == 0, jnp.concatenate([kept_own, came]), jnp.concatenate([came, kept_own]))
    return context[None], query_grad[None], key_grad[None], value_grad[None], result


def solution(mesh):
    fine = Mesh(mesh.devices.reshape(4, 2, 2, 4, 2), AXES)
    seg, tp = ("y", "xh"), ("xl", "z", "c")
    heads = P(seg, None, tp)
    return jax.shard_map(
        local,
        mesh=fine,
        in_specs=(P(seg, tp), P(), heads, heads, heads, heads),
        out_specs=(heads, heads, heads, heads, P(seg, tp)),
        check_vma=False,
    )
```

```python
import functools

import jax
import jax.numpy as jnp
from jax import lax
from jax.experimental import pallas as pl
from jax.experimental.pallas import tpu as pltpu
from jax.sharding import Mesh
from jax.sharding import PartitionSpec as P

HD = 256
AXES = ("y", "xh", "xl", "z", "c")
PLANE = ("y", "xh", "xl")
RING = 4
EXTRA = 16
EPS = 1e-06
F32 = jnp.float32
BF16 = jnp.bfloat16
MIB = 2**20
VMEM = pl.BlockSpec(memory_space=pltpu.VMEM)
SMEM = pl.BlockSpec(memory_space=pltpu.SMEM)
ANYWHERE = pl.BlockSpec(memory_space=pl.ANY)


def dot(a, b, contract):
    return lax.dot_general(a, b, ((contract[:1], contract[1:]), ((), ())), preferred_element_type=F32)


def nn(a, b):
    return dot(a, b, (1, 0))


def nt(a, b):
    return dot(a, b, (1, 1))


def tn(a, b):
    return dot(a, b, (0, 0))


def beside(*values):
    return jnp.concatenate(values, axis=1)


def above(*values):
    return jnp.concatenate(values, axis=0)


def limits(mib):
    return pltpu.CompilerParams(vmem_limit_bytes=mib * MIB)


def cost(flops, mib, transcendentals=0):
    return pl.CostEstimate(flops=flops, bytes_accessed=int(mib * MIB), transcendentals=transcendentals)


def project_body(pieces, z_ref, gain_ref, *refs):
    xs = refs[: len(pieces)]
    ko, vo, ks, vs, own_ref, sib_ref, scale_ref, normed_ref = refs[len(pieces) : len(pieces) + 8]
    held, rows_low, x_sem, out_sem = refs[len(pieces) + 8 :]
    blocks, segs, part, width = held.shape
    rows = segs * part
    z = z_ref[0]
    copies = []
    for (distance, first, depth), x in zip(pieces, xs):
        for side in range(2):
            place = side * RING + lax.rem(z + distance, RING)
            source = x.at[:, side] if depth is None else x.at[:, side, depth]
            target = held.at[place, pl.ds(first, source.shape[0])]
            copies.append(pltpu.make_async_copy(source, target, x_sem.at[len(copies)]))
    for copy in copies:
        copy.start()
    for copy in copies:
        copy.wait()
    squares = jnp.zeros((rows, 128), F32)
    for p in range(blocks):
        wide = held[p].reshape(rows, width).astype(F32)
        wide = wide * wide
        for i in range(width // 128):
            squares += wide[:, i * 128 : (i + 1) * 128]
    scale = lax.rsqrt(jnp.sum(squares, axis=1, keepdims=True) / (blocks * width) + EPS)
    scale_ref[...] = scale
    for p in range(blocks):
        wide = held[p].reshape(rows, width).astype(F32)
        rows_low[:, p * width : (p + 1) * width] = (wide * scale * gain_ref[p]).astype(BF16)
    out = pltpu.make_async_copy(rows_low, normed_ref, out_sem)
    out.start()
    for j, (w, out_ref) in enumerate(((ko, own_ref), (vo, own_ref), (ks, sib_ref), (vs, sib_ref))):
        at = (j % 2) * HD
        out_ref[:, at : at + HD] = nn(rows_low[...], w[...]).astype(BF16)
    out.wait()


def project(pieces, xs, z, gain, weights, segs, name):
    part, width = xs[0].shape[-2:]
    blocks = gain.shape[0] // width
    rows = segs * part
    return pl.pallas_call(
        functools.partial(project_body, pieces),
        in_specs=[SMEM, VMEM] + [ANYWHERE] * len(xs) + [VMEM] * 4,
        out_specs=[VMEM, VMEM, VMEM, ANYWHERE],
        out_shape=[
            jax.ShapeDtypeStruct((rows, 2 * HD), BF16),
            jax.ShapeDtypeStruct((rows, 2 * HD), BF16),
            jax.ShapeDtypeStruct((rows, 1), F32),
            jax.ShapeDtypeStruct((rows, blocks * width), BF16),
        ],
        scratch_shapes=[
            pltpu.VMEM((blocks, segs, part, width), BF16),
            pltpu.VMEM((rows, blocks * width), BF16),
            pltpu.SemaphoreType.DMA((2 * len(xs),)),
            pltpu.SemaphoreType.DMA(()),
        ],
        compiler_params=limits(20),
        cost_estimate=cost(2 * rows * blocks * width * 4 * HD, 5),
        name=name,
    )(z, gain.reshape(blocks, 1, width), *xs, *weights)


def attend_body(tile, q_ref, dc_ref, near_a, near_b, far_a, far_b, ctx_ref, qg_ref, gnear_ref, gfar_ref, gkeys, gvalues):
    kv = above(near_a[...], near_b[...], far_a[...], far_b[...])
    k, v = kv[:, :HD], kv[:, HD:]
    half = kv.shape[0] // 2
    scale = HD ** (-0.5)
    for i in range(q_ref.shape[0] // tile):
        here = slice(i * tile, (i + 1) * tile)
        q, dc = q_ref[here], dc_ref[here]
        scores = nt(q, k) * scale
        expo = jnp.exp(scores - jnp.max(scores, axis=-1, keepdims=True))
        attend = expo * (1.0 / jnp.sum(expo, axis=-1, keepdims=True))
        low = attend.astype(BF16)
        ctx_ref[here] = nn(low, v).astype(BF16)
        gattend = nt(dc, v)
        dots = jnp.sum(gattend * attend, axis=-1, keepdims=True)
        gscores = (attend * (gattend - dots) * scale).astype(BF16)
        qg_ref[here] = nn(gscores, k).astype(BF16)
        if i == 0:
            gkeys[...] = tn(gscores, q)
            gvalues[...] = tn(low, dc)
        else:
            gkeys[...] += tn(gscores, q)
            gvalues[...] += tn(low, dc)
    gnear_ref[:, :HD] = gkeys[:half].astype(BF16)
    gnear_ref[:, HD:] = gvalues[:half].astype(BF16)
    gfar_ref[:, :HD] = gkeys[half:].astype(BF16)
    gfar_ref[:, HD:] = gvalues[half:].astype(BF16)


def attention(q, dc, near_a, near_b, far_a, far_b, tile=256):
    targets, half = q.shape[0], 2 * near_a.shape[0]
    return pl.pallas_call(
        functools.partial(attend_body, tile),
        in_specs=[VMEM] * 6,
        out_specs=[VMEM] * 4,
        out_shape=[jax.ShapeDtypeStruct((targets, HD), BF16)] * 2
        + [jax.ShapeDtypeStruct((half, 2 * HD), BF16)] * 2,
        scratch_shapes=[pltpu.VMEM((2 * half, HD), F32)] * 2,
        compiler_params=limits(24),
        cost_estimate=cost(12 * targets * 2 * half * HD, 4, targets * 2 * half),
        name="attention",
    )(q, dc, near_a, near_b, far_a, far_b)


def feature_block(z, own, sib, weights, feature_half, distance, side):
    block = side * RING + lax.rem(z + distance, RING)
    at = pl.ds(pl.multiple_of(block * 2 * HD + feature_half * HD, HD), HD)
    return nt(beside(own, sib), beside(*[w[at] for w in weights])).astype(BF16)


def back_b_body(z_ref, own_ref, sib_ref, own_a, own_b, sib_a, sib_b, ko, vo, ks, vs, out_ref):
    own, sib = own_ref[...], sib_ref[...]
    segs = out_ref.shape[0]
    part = own.shape[0] // segs // 2
    wide = lambda value: value.astype(F32)
    products = beside(
        wide(own) * above(wide(own_a[...]), wide(own_b[...])),
        wide(sib) * above(wide(sib_a[...]), wide(sib_b[...])),
    )
    high = products.astype(BF16)
    low = (products - wide(high)).astype(BF16)
    ones = jnp.ones((EXTRA, high.shape[1]), BF16)
    dots = nt(ones, high) + nt(ones, low)
    out_ref[:, :, RING * 2 * part :] = jnp.broadcast_to(pieces_of(dots), (segs, 2, EXTRA, HD))
    for distance in range(RING):
        for side in range(2):
            value = feature_block(z_ref[0], own, sib, (ko, vo, ks, vs), 1, distance, side)
            value = value.reshape(2, segs, part, HD)
            for k in range(2):
                at = distance * 2 * part + k * part
                out_ref[:, side, at : at + part] = value[k]


def pieces_of(dots):
    high = dots.astype(BF16).astype(F32)
    low = dots - high
    row = lax.broadcasted_iota(jnp.int32, (EXTRA, HD), 0)
    zero = jnp.zeros((EXTRA, HD), F32)
    picked = jnp.where(row == 0, high[:, :HD], jnp.where(row == 1, high[:, HD:], zero))
    picked = jnp.where(row == 2, low[:, :HD], jnp.where(row == 3, low[:, HD:], picked))
    return picked.astype(BF16)


def back_b(z, own, sib, kvs, weights, segs):
    rows = own.shape[0]
    return pl.pallas_call(
        back_b_body,
        in_specs=[SMEM] + [VMEM] * 10,
        out_specs=VMEM,
        out_shape=jax.ShapeDtypeStruct((segs, 2, RING * rows // segs + EXTRA, HD), BF16),
        compiler_params=limits(20),
        cost_estimate=cost(2 * rows * 8 * HD * 4 * HD, 4),
        name="back_b",
    )(z, own, sib, *kvs, *weights)


def back_a_body(z_ref, own_ref, sib_ref, ko, vo, ks, vs, *outs):
    own, sib = own_ref[...], sib_ref[...]
    segs = outs[-1].shape[0]
    part = own.shape[0] // segs // 2
    lands = {2: ((0, 0), (1, segs // 2)), 1: ((2, 0), (3, segs // 2)), 3: ((4, 0), (5, segs // 2)), 0: ((6, 0),)}
    for distance in (2, 1, 3, 0):
        for side in range(2):
            value = feature_block(z_ref[0], own, sib, (ko, vo, ks, vs), 0, distance, side)
            value = value.reshape(2, segs, part, HD)
            for index, first in lands[distance]:
                for k in range(2):
                    count = outs[index].shape[0]
                    outs[index][:, side, k * part : (k + 1) * part] = value[k, first : first + count]


def back_a(z, own, sib, weights, segs):
    rows = own.shape[0]
    half = jax.ShapeDtypeStruct((segs // 2, 2, rows // segs, HD), BF16)
    full = jax.ShapeDtypeStruct((segs, 2, rows // segs, HD), BF16)
    return pl.pallas_call(
        back_a_body,
        in_specs=[SMEM] + [VMEM] * 6,
        out_specs=[VMEM] * 7,
        out_shape=[half] * 6 + [full],
        compiler_params=limits(20),
        cost_estimate=cost(2 * rows * 8 * HD * 4 * HD, 4),
        name="back_a",
    )(z, own, sib, *weights)


def weights_body(near_a, near_b, far_a, far_b, gnear_ref, gfar_ref, gk_ref, gv_ref):
    rows = above(near_a[...], near_b[...], far_a[...], far_b[...])
    total = tn(rows, above(gnear_ref[...], gfar_ref[...]))
    gk_ref[...] = total[:, :HD]
    gv_ref[...] = total[:, HD:]


def weight_grads(near_a, near_b, far_a, far_b, gnear, gfar, width=512):
    rows, hidden = near_a.shape
    block = pl.BlockSpec((rows, width), lambda i: (0, i))
    whole = pl.BlockSpec((2 * rows, 2 * HD), lambda i: (0, 0))
    out = pl.BlockSpec((width, HD), lambda i: (i, 0))
    return pl.pallas_call(
        weights_body,
        grid=(hidden // width,),
        in_specs=[block] * 4 + [whole, whole],
        out_specs=[out, out],
        out_shape=[jax.ShapeDtypeStruct((hidden, HD), F32)] * 2,
        compiler_params=limits(20),
        cost_estimate=cost(16 * rows * hidden * HD, 17),
        name="weight_grads",
    )(near_a, near_b, far_a, far_b, gnear, gfar)


def merge_b_body(arrived_ref, kept_ref, dots_ref, *send_refs):
    half = kept_ref.shape[0]
    total = arrived_ref[0].astype(F32)
    for i in range(1, arrived_ref.shape[0]):
        total += arrived_ref[i].astype(F32)
    kept_ref[...] = total[:half]
    extra = total[RING * half :]
    both = beside(extra[0:1] + extra[2:3], extra[1:2] + extra[3:4])
    dots_ref[...] = both
    pieces = pieces_of(jnp.broadcast_to(both, (EXTRA, 2 * HD)))
    for i, ref in enumerate(send_refs):
        ref[:half] = total[(i + 1) * half : (i + 2) * half].astype(BF16)
        ref[half:] = pieces


def merge_b(arrived, half):
    send = jax.ShapeDtypeStruct((half + EXTRA, HD), BF16)
    return pl.pallas_call(
        merge_b_body,
        in_specs=[VMEM],
        out_specs=[VMEM] * 5,
        out_shape=[jax.ShapeDtypeStruct((half, HD), F32), jax.ShapeDtypeStruct((1, 2 * HD), F32)] + [send] * 3,
        compiler_params=limits(16),
        cost_estimate=cost(0, 3),
        name="merge_b",
    )(arrived)


def finish_body(hidden, place_ref, gain_ref, block_ref, scale_a, scale_b, arrived_ref, kept_ref, dots_ref, r1, r2, r3,
                keep_ref, send_ref):
    core, segment, pair = place_ref[0], place_ref[1], place_ref[2]
    half = block_ref.shape[0]
    part = half // 2
    left = arrived_ref[0].astype(F32)
    for i in range(1, arrived_ref.shape[0]):
        left += arrived_ref[i].astype(F32)
    right, dots = kept_ref[...], dots_ref[...]
    for ref in (r1, r2, r3):
        right += ref[:half].astype(F32)
        extra = ref[half:].astype(F32)
        dots += beside(extra[0:1] + extra[2:3], extra[1:2] + extra[3:4])
    lane = lax.broadcasted_iota(jnp.int32, (part, HD), 1)
    row = lax.broadcasted_iota(jnp.int32, (part, HD), 0)
    mine = lane == row + segment * part
    pick = lambda values: jnp.sum(jnp.where(mine, values, 0.0), axis=1, keepdims=True)
    mean = above(pick(dots[:, :HD]), pick(dots[:, HD:])) / hidden
    rows = pl.ds(pl.multiple_of(segment * part, part), part)
    scale = above(scale_a[rows], scale_b[rows])
    gain = gain_ref[pair]
    for side, total in enumerate((left, right)):
        at = slice(side * HD, (side + 1) * HD)
        value = scale * (total * gain[:, at] - block_ref[:, at].astype(F32) * scale * mean)

        @pl.when(core == side)
        def _():
            keep_ref[...] = value

        @pl.when(core != side)
        def _():
            send_ref[...] = value


def finish(place, gain, block, scale_a, scale_b, arrived, kept, dots, received):
    half, width = block.shape
    hidden = gain.shape[0]
    return pl.pallas_call(
        functools.partial(finish_body, hidden),
        in_specs=[SMEM] + [VMEM] * 10,
        out_specs=[VMEM] * 2,
        out_shape=[jax.ShapeDtypeStruct((half, HD), F32)] * 2,
        compiler_params=limits(16),
        cost_estimate=cost(0, 1),
        name="finish",
    )(place, gain.reshape(hidden // width, 1, width), block, scale_a, scale_b, arrived, kept, dots, *received)


def swapped(value):
    return lax.ppermute(value, "c", [(0, 1), (1, 0)])


def shifted(value, by):
    return lax.ppermute(value, "z", [(i, (i + by) % RING) for i in range(RING)])


def over_plane(value):
    return lax.all_to_all(value, PLANE, 0, 0, tiled=True)


def after(values, *earlier):
    return lax.optimization_barrier((*values, *earlier))[: len(values)]


def local(memory, norm_gain, queries, key_weight, value_weight, context_grad):
    rows_own, cols_own = memory.shape
    half, width = rows_own // 2, 2 * cols_own
    part = half // 2
    core, z = lax.axis_index("c"), lax.axis_index("z")
    segment = lax.axis_index(("y", "xh"))
    pair = lax.axis_index(("xl", "z"))
    segs, plane = lax.axis_size(("y", "xh")), lax.axis_size(PLANE)
    z_array = z.astype(jnp.int32).reshape(1)
    place = jnp.stack([core, segment, pair]).astype(jnp.int32)
    wide = lambda value: value.astype(F32)

    halves = memory.reshape(2, half, cols_own)
    mine = lax.dynamic_index_in_dim(halves, core, 0, keepdims=False)
    other = swapped(lax.dynamic_index_in_dim(halves, 1 - core, 0, keepdims=False))
    block = jnp.where(core == 0, beside(mine, other), beside(other, mine))
    first_a = over_plane(jnp.broadcast_to(block[:part], (plane, part, width)))
    high = block[part:]
    near_z = jnp.stack([high, shifted(high, -1), shifted(high, 2), shifted(high, 1)])
    all_b = over_plane(jnp.broadcast_to(near_z, (plane, RING, part, width)))
    all_b = all_b.reshape(segs, 2, RING, part, width)
    low_0, high_0 = first_a[: plane // 2], first_a[plane // 2 :]
    low_3, high_1 = shifted(low_0, 1), shifted(high_0, -1)
    high_3, low_1 = shifted(high_0, 1), shifted(low_0, -1)
    low_2, high_2 = shifted(low_3, 1), shifted(high_1, -1)
    deep = lambda value: value.reshape(segs // 2, 2, part, width)

    key_own, value_own = after((key_weight[0], value_weight[0]), first_a)
    weights = (key_own, value_own, swapped(key_own), swapped(value_own))

    top = segs // 2
    pieces_a = [(0, 0, None), (3, 0, None), (3, top, None), (1, 0, None), (1, top, None), (2, 0, None), (2, top, None)]
    xs_a = [first_a.reshape(segs, 2, part, width)] + [deep(v) for v in (low_3, high_3, low_1, high_1, low_2, high_2)]
    own_a, sib_a, scale_a, normed_a = project(pieces_a, xs_a, z_array, norm_gain, weights, segs, "project_a")
    far_a = swapped(sib_a)
    all_b, = after((all_b,), own_a)
    pieces_b = [(d, 0, d) for d in range(RING)]
    own_b, sib_b, scale_b, normed_b = project(pieces_b, [all_b] * RING, z_array, norm_gain, weights, segs, "project_b")
    far_b = swapped(sib_b)
    context, query_grad, gnear, gfar = attention(queries[0], context_grad[0], own_a, own_b, far_a, far_b)
    gsib = swapped(gfar)

    parts_b = back_b(z_array, gnear, gsib, (own_a, own_b, sib_a, sib_b), weights, segs)
    arrived_b = over_plane(parts_b.reshape(plane, RING * half + EXTRA, HD))
    z_later, = after((z_array,), parts_b)
    opp_low, opp_high, up_low, up_high, down_low, down_high, kept = back_a(z_later, gnear, gsib, weights, segs)
    normed_far = [swapped(v) for v in after((normed_a, normed_b), gsib)]
    from_low, from_high = shifted(opp_low, 1), shifted(opp_high, -1)
    got_high, got_low = shifted(up_high, 1), shifted(down_low, -1)
    key_grad, value_grad = weight_grads(normed_a, normed_b, *normed_far, gnear, gfar)
    from_low, from_high = after((from_low, from_high), key_grad, value_grad)
    last_low = shifted((wide(up_low) + wide(from_low)).astype(BF16), 1)
    last_high = shifted((wide(down_high) + wide(from_high)).astype(BF16), -1)
    summed_low = wide(kept[: segs // 2]) + wide(got_low) + wide(last_low)
    summed_high = wide(kept[segs // 2 :]) + wide(got_high) + wide(last_high)
    summed_a = above(summed_low, summed_high).astype(BF16).reshape(plane, half, HD)

    arrived_b, summed_a = lax.optimization_barrier((arrived_b, summed_a))
    arrived_a = over_plane(summed_a)
    kept_b, dots, to_1, to_2, to_3 = merge_b(arrived_b, half)
    received = (shifted(to_1, 1), shifted(to_2, 2), shifted(to_3, -1))
    keep, send = finish(place, norm_gain, block, scale_a, scale_b, arrived_a, kept_b, dots, received)
    came = swapped(send)
    result = jnp.where(core == 0, above(keep, came), above(came, keep))
    return context[None], query_grad[None], key_grad[None], value_grad[None], result


def solution(mesh):
    fine = Mesh(mesh.devices.reshape(4, 2, 2, 4, 2), AXES)
    seg, tp = ("y", "xh"), ("xl", "z", "c")
    heads = P(seg, None, tp)
    return jax.shard_map(
        local,
        mesh=fine,
        in_specs=(P(seg, tp), P(), heads, heads, heads, heads),
        out_specs=(heads, heads, heads, heads, P(seg, tp)),
        check_vma=False,
    )
```

```python
import functools

import jax
import jax.numpy as jnp
from jax import lax
from jax.experimental import pallas as pl
from jax.experimental.pallas import tpu as pltpu
from jax.sharding import Mesh
from jax.sharding import PartitionSpec as P

HD = 256
AXES = ("y", "xh", "xl", "z", "c")
PLANE = ("y", "xh", "xl")
RING = 4
EXTRA = 16
EPS = 1e-06
F32 = jnp.float32
BF16 = jnp.bfloat16
MIB = 2**20
VMEM = pl.BlockSpec(memory_space=pltpu.VMEM)
SMEM = pl.BlockSpec(memory_space=pltpu.SMEM)
ANYWHERE = pl.BlockSpec(memory_space=pl.ANY)


def dot(a, b, contract):
    return lax.dot_general(a, b, ((contract[:1], contract[1:]), ((), ())), preferred_element_type=F32)


def nn(a, b):
    return dot(a, b, (1, 0))


def nt(a, b):
    return dot(a, b, (1, 1))


def tn(a, b):
    return dot(a, b, (0, 0))


def beside(*values):
    return jnp.concatenate(values, axis=1)


def above(*values):
    return jnp.concatenate(values, axis=0)


def limits(mib):
    return pltpu.CompilerParams(vmem_limit_bytes=mib * MIB)


def cost(flops, mib, transcendentals=0):
    return pl.CostEstimate(flops=flops, bytes_accessed=int(mib * MIB), transcendentals=transcendentals)


def project_body(pieces, z_ref, gain_ref, *refs):
    xs = refs[: len(pieces)]
    ws, (own_ref, sib_ref, scale_ref, normed_ref) = refs[len(pieces) : len(pieces) + 4], refs[len(pieces) + 4 : len(pieces) + 8]
    held, rows_low, weights, x_sem, w_sem, out_sem = refs[len(pieces) + 8 :]
    blocks, segs, part, width = held.shape
    rows = segs * part
    z = z_ref[0]
    copies = []
    for (distance, first, depth), x in zip(pieces, xs):
        for side in range(2):
            place = side * RING + lax.rem(z + distance, RING)
            source = x.at[:, side] if depth is None else x.at[:, side, depth]
            target = held.at[place, pl.ds(first, source.shape[0])]
            copies.append(pltpu.make_async_copy(source, target, x_sem.at[len(copies)]))
    loads = [pltpu.make_async_copy(w, weights.at[i], w_sem.at[i]) for i, w in enumerate(ws)]
    for copy in copies + loads:
        copy.start()
    for copy in copies:
        copy.wait()
    squares = jnp.zeros((rows, 128), F32)
    for p in range(blocks):
        wide = held[p].reshape(rows, width).astype(F32)
        wide = wide * wide
        for i in range(width // 128):
            squares += wide[:, i * 128 : (i + 1) * 128]
    scale = lax.rsqrt(jnp.sum(squares, axis=1, keepdims=True) / (blocks * width) + EPS)
    scale_ref[...] = scale
    for p in range(blocks):
        wide = held[p].reshape(rows, width).astype(F32)
        rows_low[:, p * width : (p + 1) * width] = (wide * scale * gain_ref[p]).astype(BF16)
    out = pltpu.make_async_copy(rows_low, normed_ref, out_sem)
    out.start()
    for i, load in enumerate(loads):
        load.wait()
        out_ref, at = (own_ref, sib_ref)[i // 2], (i % 2) * HD
        out_ref[:, at : at + HD] = nn(rows_low[...], weights[i]).astype(BF16)
    out.wait()


def project(pieces, xs, z, gain, weights, segs, name):
    part, width = xs[0].shape[-2:]
    blocks = gain.shape[0] // width
    rows = segs * part
    return pl.pallas_call(
        functools.partial(project_body, pieces),
        in_specs=[SMEM, VMEM] + [ANYWHERE] * (len(xs) + 4),
        out_specs=[VMEM, VMEM, VMEM, ANYWHERE],
        out_shape=[
            jax.ShapeDtypeStruct((rows, 2 * HD), BF16),
            jax.ShapeDtypeStruct((rows, 2 * HD), BF16),
            jax.ShapeDtypeStruct((rows, 1), F32),
            jax.ShapeDtypeStruct((rows, blocks * width), BF16),
        ],
        scratch_shapes=[
            pltpu.VMEM((blocks, segs, part, width), BF16),
            pltpu.VMEM((rows, blocks * width), BF16),
            pltpu.VMEM((4, blocks * width, HD), BF16),
            pltpu.SemaphoreType.DMA((2 * len(xs),)),
            pltpu.SemaphoreType.DMA((4,)),
            pltpu.SemaphoreType.DMA(()),
        ],
        compiler_params=limits(20),
        cost_estimate=cost(2 * rows * blocks * width * 4 * HD, 5),
        name=name,
    )(z, gain.reshape(blocks, 1, width), *xs, *weights)


def attend_body(tile, q_ref, dc_ref, near_a, near_b, far_a, far_b, ctx_ref, qg_ref, gnear_ref, gfar_ref, gkeys, gvalues):
    kv = above(near_a[...], near_b[...], far_a[...], far_b[...])
    k, v = kv[:, :HD], kv[:, HD:]
    half = kv.shape[0] // 2
    scale = HD ** (-0.5)
    for i in range(q_ref.shape[0] // tile):
        here = slice(i * tile, (i + 1) * tile)
        q, dc = q_ref[here], dc_ref[here]
        scores = nt(q, k) * scale
        expo = jnp.exp(scores - jnp.max(scores, axis=-1, keepdims=True))
        attend = expo * (1.0 / jnp.sum(expo, axis=-1, keepdims=True))
        low = attend.astype(BF16)
        ctx_ref[here] = nn(low, v).astype(BF16)
        gattend = nt(dc, v)
        dots = jnp.sum(gattend * attend, axis=-1, keepdims=True)
        gscores = (attend * (gattend - dots) * scale).astype(BF16)
        qg_ref[here] = nn(gscores, k).astype(BF16)
        if i == 0:
            gkeys[...] = tn(gscores, q)
            gvalues[...] = tn(low, dc)
        else:
            gkeys[...] += tn(gscores, q)
            gvalues[...] += tn(low, dc)
    gnear_ref[:, :HD] = gkeys[:half].astype(BF16)
    gnear_ref[:, HD:] = gvalues[:half].astype(BF16)
    gfar_ref[:, :HD] = gkeys[half:].astype(BF16)
    gfar_ref[:, HD:] = gvalues[half:].astype(BF16)


def attention(q, dc, near_a, near_b, far_a, far_b, tile=256):
    targets, half = q.shape[0], 2 * near_a.shape[0]
    return pl.pallas_call(
        functools.partial(attend_body, tile),
        in_specs=[VMEM] * 6,
        out_specs=[VMEM] * 4,
        out_shape=[jax.ShapeDtypeStruct((targets, HD), BF16)] * 2
        + [jax.ShapeDtypeStruct((half, 2 * HD), BF16)] * 2,
        scratch_shapes=[pltpu.VMEM((2 * half, HD), F32)] * 2,
        compiler_params=limits(24),
        cost_estimate=cost(12 * targets * 2 * half * HD, 4, targets * 2 * half),
        name="attention",
    )(q, dc, near_a, near_b, far_a, far_b)


def weight_loads(z, ws, held, sem, feature_half, order):
    loads = []
    for distance in order:
        for side in range(2):
            block = side * RING + lax.rem(z + distance, RING)
            at = pl.ds(pl.multiple_of(block * 2 * HD + feature_half * HD, HD), HD)
            i = len(loads)
            loads.append([
                pltpu.make_async_copy(w.at[at], held.at[i, :, pl.ds(j * HD, HD)], sem.at[i, j]) for j, w in enumerate(ws)
            ])
    for group in loads:
        for load in group:
            load.start()
    return loads


def feature_block(rows, loads, held, i):
    for load in loads[i]:
        load.wait()
    return nt(rows, held[i]).astype(BF16)


def back_b_body(z_ref, own_ref, sib_ref, own_a, own_b, sib_a, sib_b, ko, vo, ks, vs, out_ref, held, stage, w_sem, out_sem):
    loads = weight_loads(z_ref[0], (ko, vo, ks, vs), held, w_sem, 1, range(RING))
    own, sib = own_ref[...], sib_ref[...]
    segs = out_ref.shape[0]
    part = own.shape[0] // segs // 2
    wide = lambda value: value.astype(F32)
    products = beside(
        wide(own) * above(wide(own_a[...]), wide(own_b[...])),
        wide(sib) * above(wide(sib_a[...]), wide(sib_b[...])),
    )
    high = products.astype(BF16)
    low = (products - wide(high)).astype(BF16)
    ones = jnp.ones((EXTRA, high.shape[1]), BF16)
    dots = nt(ones, high) + nt(ones, low)
    tail = RING * 2 * part
    stage[:, :, tail:] = jnp.broadcast_to(pieces_of(dots), (segs, 2, EXTRA, HD))
    rows = beside(own, sib)
    outs = []
    for distance in range(RING):
        at = distance * 2 * part
        for side in range(2):
            value = feature_block(rows, loads, held, distance * 2 + side).reshape(2, segs, part, HD)
            for k in range(2):
                stage[:, side, at + k * part : at + (k + 1) * part] = value[k]
        size = 2 * part if distance < RING - 1 else 2 * part + EXTRA
        outs.append(pltpu.make_async_copy(stage.at[:, :, pl.ds(at, size)], out_ref.at[:, :, pl.ds(at, size)], out_sem.at[distance]))
        outs[-1].start()
    for out in outs:
        out.wait()


def pieces_of(dots):
    high = dots.astype(BF16).astype(F32)
    low = dots - high
    row = lax.broadcasted_iota(jnp.int32, (EXTRA, HD), 0)
    zero = jnp.zeros((EXTRA, HD), F32)
    picked = jnp.where(row == 0, high[:, :HD], jnp.where(row == 1, high[:, HD:], zero))
    picked = jnp.where(row == 2, low[:, :HD], jnp.where(row == 3, low[:, HD:], picked))
    return picked.astype(BF16)


def back_b(z, own, sib, kvs, weights, segs):
    rows = own.shape[0]
    return pl.pallas_call(
        back_b_body,
        in_specs=[SMEM] + [VMEM] * 6 + [ANYWHERE] * 4,
        out_specs=ANYWHERE,
        out_shape=pltpu.HBM((segs, 2, RING * rows // segs + EXTRA, HD), BF16),
        scratch_shapes=[
            pltpu.VMEM((2 * RING, HD, 4 * HD), BF16),
            pltpu.VMEM((segs, 2, RING * rows // segs + EXTRA, HD), BF16),
            pltpu.SemaphoreType.DMA((2 * RING, 4)),
            pltpu.SemaphoreType.DMA((RING,)),
        ],
        compiler_params=limits(20),
        cost_estimate=cost(2 * rows * 8 * HD * 4 * HD, 4),
        name="back_b",
    )(z, own, sib, *kvs, *weights)


def back_a_body(z_ref, own_ref, sib_ref, ko, vo, ks, vs, *refs):
    outs, (held, w_sem) = refs[:7], refs[7:]
    order = (2, 1, 3, 0)
    loads = weight_loads(z_ref[0], (ko, vo, ks, vs), held, w_sem, 0, order)
    rows = beside(own_ref[...], sib_ref[...])
    segs = outs[-1].shape[0]
    part = rows.shape[0] // segs // 2
    lands = {2: ((0, 0), (1, segs // 2)), 1: ((2, 0), (3, segs // 2)), 3: ((4, 0), (5, segs // 2)), 0: ((6, 0),)}
    for i, distance in enumerate(order):
        for side in range(2):
            value = feature_block(rows, loads, held, 2 * i + side).reshape(2, segs, part, HD)
            for index, first in lands[distance]:
                for k in range(2):
                    count = outs[index].shape[0]
                    outs[index][:, side, k * part : (k + 1) * part] = value[k, first : first + count]


def back_a(z, own, sib, weights, segs):
    rows = own.shape[0]
    half = jax.ShapeDtypeStruct((segs // 2, 2, rows // segs, HD), BF16)
    full = jax.ShapeDtypeStruct((segs, 2, rows // segs, HD), BF16)
    return pl.pallas_call(
        back_a_body,
        in_specs=[SMEM] + [VMEM] * 2 + [ANYWHERE] * 4,
        out_specs=[VMEM] * 7,
        out_shape=[half] * 6 + [full],
        scratch_shapes=[pltpu.VMEM((2 * RING, HD, 4 * HD), BF16), pltpu.SemaphoreType.DMA((2 * RING, 4))],
        compiler_params=limits(20),
        cost_estimate=cost(2 * rows * 8 * HD * 4 * HD, 4),
        name="back_a",
    )(z, own, sib, *weights)


def weights_body(near_a, near_b, far_a, far_b, gnear_ref, gfar_ref, gk_ref, gv_ref):
    rows = above(near_a[...], near_b[...], far_a[...], far_b[...])
    total = tn(rows, above(gnear_ref[...], gfar_ref[...]))
    gk_ref[...] = total[:, :HD]
    gv_ref[...] = total[:, HD:]


def weight_grads(near_a, near_b, far_a, far_b, gnear, gfar, width=512):
    rows, hidden = near_a.shape
    block = pl.BlockSpec((rows, width), lambda i: (0, i))
    whole = pl.BlockSpec((2 * rows, 2 * HD), lambda i: (0, 0))
    out = pl.BlockSpec((width, HD), lambda i: (i, 0))
    return pl.pallas_call(
        weights_body,
        grid=(hidden // width,),
        in_specs=[block] * 4 + [whole, whole],
        out_specs=[out, out],
        out_shape=[jax.ShapeDtypeStruct((hidden, HD), F32)] * 2,
        compiler_params=limits(20),
        cost_estimate=cost(16 * rows * hidden * HD, 17),
        name="weight_grads",
    )(near_a, near_b, far_a, far_b, gnear, gfar)


def merge_b_body(arrived_ref, kept_ref, dots_ref, *send_refs):
    half = kept_ref.shape[0]
    total = arrived_ref[0].astype(F32)
    for i in range(1, arrived_ref.shape[0]):
        total += arrived_ref[i].astype(F32)
    kept_ref[...] = total[:half]
    extra = total[RING * half :]
    both = beside(extra[0:1] + extra[2:3], extra[1:2] + extra[3:4])
    dots_ref[...] = both
    pieces = pieces_of(jnp.broadcast_to(both, (EXTRA, 2 * HD)))
    for i, ref in enumerate(send_refs):
        ref[:half] = total[(i + 1) * half : (i + 2) * half].astype(BF16)
        ref[half:] = pieces


def merge_b(arrived, half):
    send = jax.ShapeDtypeStruct((half + EXTRA, HD), BF16)
    return pl.pallas_call(
        merge_b_body,
        in_specs=[VMEM],
        out_specs=[VMEM] * 5,
        out_shape=[jax.ShapeDtypeStruct((half, HD), F32), jax.ShapeDtypeStruct((1, 2 * HD), F32)] + [send] * 3,
        compiler_params=limits(16),
        cost_estimate=cost(0, 3),
        name="merge_b",
    )(arrived)


def finish_body(hidden, place_ref, gain_ref, block_ref, scale_a, scale_b, arrived_ref, kept_ref, dots_ref, r1, r2, r3,
                keep_ref, send_ref):
    core, segment, pair = place_ref[0], place_ref[1], place_ref[2]
    half = block_ref.shape[0]
    part = half // 2
    left = arrived_ref[0].astype(F32)
    for i in range(1, arrived_ref.shape[0]):
        left += arrived_ref[i].astype(F32)
    right, dots = kept_ref[...], dots_ref[...]
    for ref in (r1, r2, r3):
        right += ref[:half].astype(F32)
        extra = ref[half:].astype(F32)
        dots += beside(extra[0:1] + extra[2:3], extra[1:2] + extra[3:4])
    lane = lax.broadcasted_iota(jnp.int32, (part, HD), 1)
    row = lax.broadcasted_iota(jnp.int32, (part, HD), 0)
    mine = lane == row + segment * part
    pick = lambda values: jnp.sum(jnp.where(mine, values, 0.0), axis=1, keepdims=True)
    mean = above(pick(dots[:, :HD]), pick(dots[:, HD:])) / hidden
    rows = pl.ds(pl.multiple_of(segment * part, part), part)
    scale = above(scale_a[rows], scale_b[rows])
    gain = gain_ref[pair]
    for side, total in enumerate((left, right)):
        at = slice(side * HD, (side + 1) * HD)
        value = scale * (total * gain[:, at] - block_ref[:, at].astype(F32) * scale * mean)

        @pl.when(core == side)
        def _():
            keep_ref[...] = value

        @pl.when(core != side)
        def _():
            send_ref[...] = value


def finish(place, gain, block, scale_a, scale_b, arrived, kept, dots, received):
    half, width = block.shape
    hidden = gain.shape[0]
    return pl.pallas_call(
        functools.partial(finish_body, hidden),
        in_specs=[SMEM] + [VMEM] * 10,
        out_specs=[VMEM] * 2,
        out_shape=[jax.ShapeDtypeStruct((half, HD), F32)] * 2,
        compiler_params=limits(16),
        cost_estimate=cost(0, 1),
        name="finish",
    )(place, gain.reshape(hidden // width, 1, width), block, scale_a, scale_b, arrived, kept, dots, *received)


def in_hbm(value):
    return pltpu.with_memory_space_constraint(value, pltpu.HBM)


def swapped(value):
    return lax.ppermute(value, "c", [(0, 1), (1, 0)])


def shifted(value, by):
    return lax.ppermute(value, "z", [(i, (i + by) % RING) for i in range(RING)])


def over_plane(value):
    return lax.all_to_all(value, PLANE, 0, 0, tiled=True)


def after(values, *earlier):
    return lax.optimization_barrier((*values, *earlier))[: len(values)]


def local(memory, norm_gain, queries, key_weight, value_weight, context_grad):
    rows_own, cols_own = memory.shape
    half, width = rows_own // 2, 2 * cols_own
    part = half // 2
    core, z = lax.axis_index("c"), lax.axis_index("z")
    segment = lax.axis_index(("y", "xh"))
    pair = lax.axis_index(("xl", "z"))
    segs, plane = lax.axis_size(("y", "xh")), lax.axis_size(PLANE)
    z_array = z.astype(jnp.int32).reshape(1)
    place = jnp.stack([core, segment, pair]).astype(jnp.int32)
    wide = lambda value: value.astype(F32)

    halves = memory.reshape(2, half, cols_own)
    mine = lax.dynamic_index_in_dim(halves, core, 0, keepdims=False)
    other = swapped(lax.dynamic_index_in_dim(halves, 1 - core, 0, keepdims=False))
    block = jnp.where(core == 0, beside(mine, other), beside(other, mine))
    first_a = over_plane(jnp.broadcast_to(block[:part], (plane, part, width)))
    high = block[part:]
    near_z = jnp.stack([high, shifted(high, -1), shifted(high, 2), shifted(high, 1)])
    all_b = over_plane(jnp.broadcast_to(near_z, (plane, RING, part, width)))
    all_b = all_b.reshape(segs, 2, RING, part, width)
    low_0, high_0 = first_a[: plane // 2], first_a[plane // 2 :]
    low_3, high_1 = shifted(low_0, 1), shifted(high_0, -1)
    high_3, low_1 = shifted(high_0, 1), shifted(low_0, -1)
    low_2, high_2 = shifted(low_3, 1), shifted(high_1, -1)
    deep = lambda value: value.reshape(segs // 2, 2, part, width)

    key_own, value_own = after((key_weight[0], value_weight[0]), near_z)
    weights = [in_hbm(w) for w in (key_own, value_own, swapped(key_own), swapped(value_own))]

    top = segs // 2
    pieces_a = [(0, 0, None), (3, 0, None), (3, top, None), (1, 0, None), (1, top, None), (2, 0, None), (2, top, None)]
    xs_a = [first_a.reshape(segs, 2, part, width)] + [deep(v) for v in (low_3, high_3, low_1, high_1, low_2, high_2)]
    xs_a = [in_hbm(x) for x in xs_a]
    own_a, sib_a, scale_a, normed_a = project(pieces_a, xs_a, z_array, norm_gain, weights, segs, "project_a")
    far_a = swapped(sib_a)
    all_b, = after((all_b,), own_a)
    pieces_b = [(d, 0, d) for d in range(RING)]
    own_b, sib_b, scale_b, normed_b = project(pieces_b, [all_b] * RING, z_array, norm_gain, weights, segs, "project_b")
    far_b = swapped(sib_b)
    context, query_grad, gnear, gfar = attention(queries[0], context_grad[0], own_a, own_b, far_a, far_b)
    gsib = swapped(gfar)

    parts_b = back_b(z_array, gnear, gsib, (own_a, own_b, sib_a, sib_b), weights, segs)
    arrived_b = over_plane(parts_b.reshape(plane, RING * half + EXTRA, HD))
    z_later, = after((z_array,), parts_b)
    opp_low, opp_high, up_low, up_high, down_low, down_high, kept = back_a(z_later, gnear, gsib, weights, segs)
    normed_far = [swapped(v) for v in after((normed_a, normed_b), gsib)]
    from_low, from_high = shifted(opp_low, 1), shifted(opp_high, -1)
    got_high, got_low = shifted(up_high, 1), shifted(down_low, -1)
    key_grad, value_grad = weight_grads(normed_a, normed_b, *normed_far, gnear, gfar)
    from_low, from_high = after((from_low, from_high), key_grad, value_grad)
    last_low = shifted((wide(up_low) + wide(from_low)).astype(BF16), 1)
    last_high = shifted((wide(down_high) + wide(from_high)).astype(BF16), -1)
    summed_low = wide(kept[: segs // 2]) + wide(got_low) + wide(last_low)
    summed_high = wide(kept[segs // 2 :]) + wide(got_high) + wide(last_high)
    summed_a = above(summed_low, summed_high).astype(BF16).reshape(plane, half, HD)

    arrived_b, summed_a = lax.optimization_barrier((arrived_b, summed_a))
    arrived_a = over_plane(summed_a)
    kept_b, dots, to_1, to_2, to_3 = merge_b(arrived_b, half)
    received = (shifted(to_1, 1), shifted(to_2, 2), shifted(to_3, -1))
    keep, send = finish(place, norm_gain, block, scale_a, scale_b, arrived_a, kept_b, dots, received)
    came = swapped(send)
    result = jnp.where(core == 0, above(keep, came), above(came, keep))
    return context[None], query_grad[None], key_grad[None], value_grad[None], result


def solution(mesh):
    fine = Mesh(mesh.devices.reshape(4, 2, 2, 4, 2), AXES)
    seg, tp = ("y", "xh"), ("xl", "z", "c")
    heads = P(seg, None, tp)
    return jax.shard_map(
        local,
        mesh=fine,
        in_specs=(P(seg, tp), P(), heads, heads, heads, heads),
        out_specs=(heads, heads, heads, heads, P(seg, tp)),
        check_vma=False,
    )
```

```python
import functools

import jax
import jax.numpy as jnp
from jax import lax
from jax.experimental import pallas as pl
from jax.experimental.pallas import tpu as pltpu
from jax.sharding import Mesh
from jax.sharding import PartitionSpec as P

HD = 256
AXES = ("y", "xh", "xl", "z", "c")
PLANE = ("y", "xh", "xl")
RING = 4
EXTRA = 16
EPS = 1e-06
F32 = jnp.float32
BF16 = jnp.bfloat16
MIB = 2**20
VMEM = pl.BlockSpec(memory_space=pltpu.VMEM)
SMEM = pl.BlockSpec(memory_space=pltpu.SMEM)
ANYWHERE = pl.BlockSpec(memory_space=pl.ANY)


def dot(a, b, contract):
    return lax.dot_general(a, b, ((contract[:1], contract[1:]), ((), ())), preferred_element_type=F32)


def nn(a, b):
    return dot(a, b, (1, 0))


def nt(a, b):
    return dot(a, b, (1, 1))


def tn(a, b):
    return dot(a, b, (0, 0))


def beside(*values):
    return jnp.concatenate(values, axis=1)


def above(*values):
    return jnp.concatenate(values, axis=0)


def limits(mib):
    return pltpu.CompilerParams(vmem_limit_bytes=mib * MIB)


def cost(flops, mib, transcendentals=0):
    return pl.CostEstimate(flops=flops, bytes_accessed=int(mib * MIB), transcendentals=transcendentals)


def stage_body(*refs):
    sources, out_ref, sem = refs[:-2], refs[-2], refs[-1]
    copies = [
        pltpu.make_async_copy(source, out_ref.at[:, pl.ds(i * HD, HD)], sem.at[i]) for i, source in enumerate(sources)
    ]
    for copy in copies:
        copy.start()
    for copy in copies:
        copy.wait()


def staged(weights):
    count, hidden = len(weights), weights[0].shape[0]
    out = pl.pallas_call(
        stage_body,
        in_specs=[ANYWHERE] * count,
        out_specs=ANYWHERE,
        out_shape=pltpu.HBM((hidden, count * HD), BF16),
        scratch_shapes=[pltpu.SemaphoreType.DMA((count,))],
        compiler_params=limits(4),
        cost_estimate=cost(0, 8),
        name="stage",
    )(*[in_hbm(w) for w in weights])
    return in_hbm(out)


def project_body(pieces, z_ref, gain_ref, *refs):
    xs = refs[: len(pieces)]
    w_ref, own_ref, sib_ref, scale_ref, normed_ref, held, rows_low, weights, x_sem, w_sem, out_sem = refs[len(pieces) :]
    blocks, segs, part, width = held.shape
    rows = segs * part
    z = z_ref[0]
    copies = []
    for (distance, first, depth), x in zip(pieces, xs):
        for side in range(2):
            place = side * RING + lax.rem(z + distance, RING)
            source = x.at[:, side] if depth is None else x.at[:, side, depth]
            target = held.at[place, pl.ds(first, source.shape[0])]
            copies.append(pltpu.make_async_copy(source, target, x_sem.at[len(copies)]))
    load = pltpu.make_async_copy(w_ref, weights, w_sem)
    for copy in copies + [load]:
        copy.start()
    for copy in copies:
        copy.wait()
    squares = jnp.zeros((rows, 128), F32)
    for p in range(blocks):
        wide = held[p].reshape(rows, width).astype(F32)
        wide = wide * wide
        for i in range(width // 128):
            squares += wide[:, i * 128 : (i + 1) * 128]
    scale = lax.rsqrt(jnp.sum(squares, axis=1, keepdims=True) / (blocks * width) + EPS)
    scale_ref[...] = scale
    for p in range(blocks):
        wide = held[p].reshape(rows, width).astype(F32)
        rows_low[:, p * width : (p + 1) * width] = (wide * scale * gain_ref[p]).astype(BF16)
    out = pltpu.make_async_copy(rows_low, normed_ref, out_sem)
    out.start()
    load.wait()
    for i, out_ref in enumerate((own_ref, sib_ref)):
        at = 2 * HD * i
        out_ref[...] = nn(rows_low[...], weights[:, at : at + 2 * HD]).astype(BF16)
    out.wait()


def project(pieces, xs, z, gain, weights, segs, name):
    part, width = xs[0].shape[-2:]
    blocks = gain.shape[0] // width
    rows = segs * part
    return pl.pallas_call(
        functools.partial(project_body, pieces),
        in_specs=[SMEM, VMEM] + [ANYWHERE] * (len(xs) + 1),
        out_specs=[VMEM, VMEM, VMEM, ANYWHERE],
        out_shape=[
            jax.ShapeDtypeStruct((rows, 2 * HD), BF16),
            jax.ShapeDtypeStruct((rows, 2 * HD), BF16),
            jax.ShapeDtypeStruct((rows, 1), F32),
            jax.ShapeDtypeStruct((rows, blocks * width), BF16),
        ],
        scratch_shapes=[
            pltpu.VMEM((blocks, segs, part, width), BF16),
            pltpu.VMEM((rows, blocks * width), BF16),
            pltpu.VMEM((blocks * width, 4 * HD), BF16),
            pltpu.SemaphoreType.DMA((2 * len(xs),)),
            pltpu.SemaphoreType.DMA(()),
            pltpu.SemaphoreType.DMA(()),
        ],
        compiler_params=limits(24),
        cost_estimate=cost(2 * rows * blocks * width * 4 * HD, 12),
        name=name,
    )(z, gain.reshape(blocks, 1, width), *xs, weights)


def pieces_of(dots):
    high = dots.astype(BF16).astype(F32)
    shape = (EXTRA, dots.shape[1])
    row = lax.broadcasted_iota(jnp.int32, shape, 0)
    low = jnp.broadcast_to(dots - high, shape)
    return jnp.where(row == 0, jnp.broadcast_to(high, shape), jnp.where(row == 1, low, 0.0)).astype(BF16)


def in_two_rows(pieces):
    return above(pieces[:, :HD], pieces[:, HD:])


def dots_of(rows):
    return beside(rows[0:1] + rows[1:2], rows[EXTRA : EXTRA + 1] + rows[EXTRA + 1 : EXTRA + 2])


def attend_body(tile, q_ref, dc_ref, near_a, near_b, far_a, far_b, ctx_ref, qg_ref, gnear_ref, gfar_ref, near_dots, gkeys, gvalues):
    kv = above(near_a[...], near_b[...], far_a[...], far_b[...])
    k, v = kv[:, :HD], kv[:, HD:]
    half = kv.shape[0] // 2
    scale = HD ** (-0.5)
    row_products = jnp.zeros((8, kv.shape[0]), F32)
    for i in range(q_ref.shape[0] // tile):
        here = slice(i * tile, (i + 1) * tile)
        q, dc = q_ref[here], dc_ref[here]
        scores = nt(q, k) * scale
        expo = jnp.exp(scores - jnp.max(scores, axis=-1, keepdims=True))
        attend = expo * (1.0 / jnp.sum(expo, axis=-1, keepdims=True))
        low = attend.astype(BF16)
        ctx_ref[here] = nn(low, v).astype(BF16)
        gattend = nt(dc, v)
        dots = jnp.sum(gattend * attend, axis=-1, keepdims=True)
        gscores = attend * (gattend - dots)
        both = gscores * scores + attend * gattend
        row_products += jnp.sum(both.reshape(tile // 8, 8, kv.shape[0]), axis=0)
        gscores = (gscores * scale).astype(BF16)
        qg_ref[here] = nn(gscores, k).astype(BF16)
        if i == 0:
            gkeys[...] = tn(gscores, q)
            gvalues[...] = tn(low, dc)
        else:
            gkeys[...] += tn(gscores, q)
            gvalues[...] += tn(low, dc)
    gnear_ref[:, :HD] = gkeys[:half].astype(BF16)
    gnear_ref[:, HD:] = gvalues[:half].astype(BF16)
    gfar_ref[:half, :HD] = gkeys[half:].astype(BF16)
    gfar_ref[:half, HD:] = gvalues[half:].astype(BF16)
    row_products = jnp.sum(row_products, axis=0, keepdims=True)
    near_dots[...] = row_products[:, :half]
    gfar_ref[half:] = pieces_of(row_products[:, half:])


def attention(q, dc, near_a, near_b, far_a, far_b, tile=256):
    targets, half = q.shape[0], 2 * near_a.shape[0]
    return pl.pallas_call(
        functools.partial(attend_body, tile),
        in_specs=[VMEM] * 6,
        out_specs=[VMEM] * 5,
        out_shape=[jax.ShapeDtypeStruct((targets, HD), BF16)] * 2
        + [
            jax.ShapeDtypeStruct((half, 2 * HD), BF16),
            jax.ShapeDtypeStruct((half + EXTRA, 2 * HD), BF16),
            jax.ShapeDtypeStruct((1, half), F32),
        ],
        scratch_shapes=[pltpu.VMEM((2 * half, HD), F32)] * 2,
        compiler_params=limits(20),
        cost_estimate=cost(12 * targets * 2 * half * HD, 4, targets * 2 * half),
        name="attention",
    )(q, dc, near_a, near_b, far_a, far_b)


def weight_loads(z, w_ref, held, sem, feature_half, order):
    loads = []
    for distance in order:
        for side in range(2):
            block = side * RING + lax.rem(z + distance, RING)
            at = pl.ds(pl.multiple_of(block * 2 * HD + feature_half * HD, HD), HD)
            i = len(loads)
            loads.append(pltpu.make_async_copy(w_ref.at[at], held.at[i], sem.at[i]))
    for load in loads:
        load.start()
    return loads


def feature_block(rows, loads, held, i):
    loads[i].wait()
    return nt(rows, held[i]).astype(BF16)


def back_b_body(z_ref, own_ref, sib_ref, dots_ref, w_ref, out_ref, stage, held, w_sem, out_sem):
    loads = weight_loads(z_ref[0], w_ref, held, w_sem, 1, range(RING))
    half = own_ref.shape[0]
    segs = out_ref.shape[0]
    part = half // segs // 2
    rows = beside(own_ref[...], sib_ref[:half])
    outs = []
    for distance in range(RING):
        at = distance * 2 * part
        for side in range(2):
            value = feature_block(rows, loads, held, distance * 2 + side).reshape(2, segs, part, HD)
            for k in range(2):
                stage[:, side, at + k * part : at + (k + 1) * part] = value[k]
        size = 2 * part
        if distance == RING - 1:
            extra = sib_ref[half:].astype(F32)
            pieces = in_two_rows(pieces_of(dots_ref[...] + extra[0:1] + extra[1:2]))
            stage[:, :, at + size :] = jnp.broadcast_to(pieces, (segs, 2, 2 * EXTRA, HD))
            size += 2 * EXTRA
        outs.append(pltpu.make_async_copy(stage.at[:, :, pl.ds(at, size)], out_ref.at[:, :, pl.ds(at, size)], out_sem.at[distance]))
        outs[-1].start()
    for out in outs:
        out.wait()


def back_b(z, own, sib, dots, weights, segs):
    rows = own.shape[0]
    shape = (segs, 2, RING * rows // segs + 2 * EXTRA, HD)
    return pl.pallas_call(
        back_b_body,
        in_specs=[SMEM] + [VMEM] * 3 + [ANYWHERE],
        out_specs=ANYWHERE,
        out_shape=pltpu.HBM(shape, BF16),
        scratch_shapes=[
            pltpu.VMEM(shape, BF16),
            pltpu.VMEM((2 * RING, HD, 4 * HD), BF16),
            pltpu.SemaphoreType.DMA((2 * RING,)),
            pltpu.SemaphoreType.DMA((RING,)),
        ],
        compiler_params=limits(16),
        cost_estimate=cost(2 * rows * 8 * HD * 4 * HD, 4),
        name="back_b",
    )(z, own, sib, dots, weights)


def back_a_body(z_ref, own_ref, sib_ref, w_ref, *refs):
    outs, (held, w_sem) = refs[:7], refs[7:]
    order = (2, 1, 3, 0)
    loads = weight_loads(z_ref[0], w_ref, held, w_sem, 0, order)
    rows = beside(own_ref[...], sib_ref[: own_ref.shape[0]])
    segs = outs[-1].shape[0]
    part = rows.shape[0] // segs // 2
    lands = {2: ((0, 0), (1, segs // 2)), 1: ((2, 0), (3, segs // 2)), 3: ((4, 0), (5, segs // 2)), 0: ((6, 0),)}
    for i, distance in enumerate(order):
        for side in range(2):
            value = feature_block(rows, loads, held, 2 * i + side).reshape(2, segs, part, HD)
            for index, first in lands[distance]:
                for k in range(2):
                    count = outs[index].shape[0]
                    outs[index][:, side, k * part : (k + 1) * part] = value[k, first : first + count]


def back_a(z, own, sib, weights, segs):
    rows = own.shape[0]
    half = jax.ShapeDtypeStruct((segs // 2, 2, rows // segs, HD), BF16)
    full = jax.ShapeDtypeStruct((segs, 2, rows // segs, HD), BF16)
    return pl.pallas_call(
        back_a_body,
        in_specs=[SMEM] + [VMEM] * 2 + [ANYWHERE],
        out_specs=[VMEM] * 7,
        out_shape=[half] * 6 + [full],
        scratch_shapes=[pltpu.VMEM((2 * RING, HD, 4 * HD), BF16), pltpu.SemaphoreType.DMA((2 * RING,))],
        compiler_params=limits(16),
        cost_estimate=cost(2 * rows * 8 * HD * 4 * HD, 4),
        name="back_a",
    )(z, own, sib, weights)


def weights_body(near_a, near_b, far_a, far_b, gnear_ref, gfar_ref, gk_ref, gv_ref):
    rows = above(near_a[...], near_b[...], far_a[...], far_b[...])
    total = tn(rows, above(gnear_ref[...], gfar_ref[: gnear_ref.shape[0]]))
    gk_ref[...] = total[:, :HD]
    gv_ref[...] = total[:, HD:]


def weight_grads(near_a, near_b, far_a, far_b, gnear, gfar, width=512):
    rows, hidden = near_a.shape
    block = pl.BlockSpec((rows, width), lambda i: (0, i))
    near = pl.BlockSpec(gnear.shape, lambda i: (0, 0))
    far = pl.BlockSpec(gfar.shape, lambda i: (0, 0))
    out = pl.BlockSpec((width, HD), lambda i: (i, 0))
    return pl.pallas_call(
        weights_body,
        grid=(hidden // width,),
        in_specs=[block] * 4 + [near, far],
        out_specs=[out, out],
        out_shape=[jax.ShapeDtypeStruct((hidden, HD), F32)] * 2,
        compiler_params=limits(16),
        cost_estimate=cost(16 * rows * hidden * HD, 17),
        name="weight_grads",
    )(near_a, near_b, far_a, far_b, gnear, gfar)


def merge_b_body(arrived_ref, kept_ref, dots_ref, *send_refs):
    half = kept_ref.shape[0]
    total = arrived_ref[0].astype(F32)
    for i in range(1, arrived_ref.shape[0]):
        total += arrived_ref[i].astype(F32)
    kept_ref[...] = total[:half]
    both = dots_of(total[RING * half :])
    dots_ref[...] = both
    pieces = in_two_rows(pieces_of(both))
    for i, ref in enumerate(send_refs):
        ref[:half] = total[(i + 1) * half : (i + 2) * half].astype(BF16)
        ref[half:] = pieces


def merge_b(arrived, half):
    send = jax.ShapeDtypeStruct((half + 2 * EXTRA, HD), BF16)
    return pl.pallas_call(
        merge_b_body,
        in_specs=[VMEM],
        out_specs=[VMEM] * 5,
        out_shape=[jax.ShapeDtypeStruct((half, HD), F32), jax.ShapeDtypeStruct((1, 2 * HD), F32)] + [send] * 3,
        compiler_params=limits(16),
        cost_estimate=cost(0, 3),
        name="merge_b",
    )(arrived)


def finish_body(hidden, place_ref, gain_ref, block_ref, scale_a, scale_b, arrived_ref, kept_ref, dots_ref, r1, r2, r3,
                keep_ref, send_ref):
    core, segment, pair = place_ref[0], place_ref[1], place_ref[2]
    half = block_ref.shape[0]
    part = half // 2
    left = arrived_ref[0].astype(F32)
    for i in range(1, arrived_ref.shape[0]):
        left += arrived_ref[i].astype(F32)
    right, dots = kept_ref[...], dots_ref[...]
    for ref in (r1, r2, r3):
        right += ref[:half].astype(F32)
        dots += dots_of(ref[half:].astype(F32))
    lane = lax.broadcasted_iota(jnp.int32, (part, HD), 1)
    row = lax.broadcasted_iota(jnp.int32, (part, HD), 0)
    mine = lane == row + segment * part
    pick = lambda values: jnp.sum(jnp.where(mine, values, 0.0), axis=1, keepdims=True)
    mean = above(pick(dots[:, :HD]), pick(dots[:, HD:])) / hidden
    rows = pl.ds(pl.multiple_of(segment * part, part), part)
    scale = above(scale_a[rows], scale_b[rows])
    gain = gain_ref[pair]
    for side, total in enumerate((left, right)):
        at = slice(side * HD, (side + 1) * HD)
        value = scale * (total * gain[:, at] - block_ref[:, at].astype(F32) * scale * mean)

        @pl.when(core == side)
        def _():
            keep_ref[...] = value

        @pl.when(core != side)
        def _():
            send_ref[...] = value


def finish(place, gain, block, scale_a, scale_b, arrived, kept, dots, received):
    half, width = block.shape
    hidden = gain.shape[0]
    return pl.pallas_call(
        functools.partial(finish_body, hidden),
        in_specs=[SMEM] + [VMEM] * 10,
        out_specs=[VMEM] * 2,
        out_shape=[jax.ShapeDtypeStruct((half, HD), F32)] * 2,
        compiler_params=limits(16),
        cost_estimate=cost(0, 1),
        name="finish",
    )(place, gain.reshape(hidden // width, 1, width), block, scale_a, scale_b, arrived, kept, dots, *received)


def in_hbm(value):
    return pltpu.with_memory_space_constraint(value, pltpu.HBM)


def swapped(value):
    return lax.ppermute(value, "c", [(0, 1), (1, 0)])


def shifted(value, by):
    return lax.ppermute(value, "z", [(i, (i + by) % RING) for i in range(RING)])


def over_plane(value):
    return lax.all_to_all(value, PLANE, 0, 0, tiled=True)


def after(values, *earlier):
    return lax.optimization_barrier((*values, *earlier))[: len(values)]


def local(memory, norm_gain, queries, key_weight, value_weight, context_grad):
    rows_own, cols_own = memory.shape
    half, width = rows_own // 2, 2 * cols_own
    part = half // 2
    core, z = lax.axis_index("c"), lax.axis_index("z")
    segment = lax.axis_index(("y", "xh"))
    pair = lax.axis_index(("xl", "z"))
    segs, plane = lax.axis_size(("y", "xh")), lax.axis_size(PLANE)
    z_array = z.astype(jnp.int32).reshape(1)
    place = jnp.stack([core, segment, pair]).astype(jnp.int32)
    wide = lambda value: value.astype(F32)

    halves = memory.reshape(2, half, cols_own)
    mine = lax.dynamic_index_in_dim(halves, core, 0, keepdims=False)
    other = swapped(lax.dynamic_index_in_dim(halves, 1 - core, 0, keepdims=False))
    block = jnp.where(core == 0, beside(mine, other), beside(other, mine))
    first_a = over_plane(jnp.broadcast_to(block[:part], (plane, part, width)))
    high = block[part:]
    near_z = jnp.stack([high, shifted(high, -1), shifted(high, 2), shifted(high, 1)])
    all_b = over_plane(jnp.broadcast_to(near_z, (plane, RING, part, width)))
    all_b = all_b.reshape(segs, 2, RING, part, width)
    low_0, high_0 = first_a[: plane // 2], first_a[plane // 2 :]
    low_3, high_1 = shifted(low_0, 1), shifted(high_0, -1)
    high_3, low_1 = shifted(high_0, 1), shifted(low_0, -1)
    low_2, high_2 = shifted(low_3, 1), shifted(high_1, -1)
    deep = lambda value: value.reshape(segs // 2, 2, part, width)

    key_own, value_own = after((key_weight[0], value_weight[0]), near_z, first_a)
    weights = staged((key_own, value_own, swapped(key_own), swapped(value_own)))

    top = segs // 2
    pieces_a = [(0, 0, None), (3, 0, None), (3, top, None), (1, 0, None), (1, top, None), (2, 0, None), (2, top, None)]
    xs_a = [first_a.reshape(segs, 2, part, width)] + [deep(v) for v in (low_3, high_3, low_1, high_1, low_2, high_2)]
    xs_a = [in_hbm(x) for x in xs_a]
    own_a, sib_a, scale_a, normed_a = project(pieces_a, xs_a, z_array, norm_gain, weights, segs, "project_a")
    far_a = swapped(sib_a)
    all_b, = after((all_b,), own_a)
    pieces_b = [(d, 0, d) for d in range(RING)]
    own_b, sib_b, scale_b, normed_b = project(pieces_b, [all_b] * RING, z_array, norm_gain, weights, segs, "project_b")
    far_b = swapped(sib_b)
    context, query_grad, gnear, gfar, near_dots = attention(queries[0], context_grad[0], own_a, own_b, far_a, far_b)
    gsib = swapped(gfar)

    parts_b = back_b(z_array, gnear, gsib, near_dots, weights, segs)
    arrived_b = over_plane(parts_b.reshape(plane, RING * half + 2 * EXTRA, HD))
    z_later, = after((z_array,), parts_b)
    opp_low, opp_high, up_low, up_high, down_low, down_high, kept = back_a(z_later, gnear, gsib, weights, segs)
    normed_far = [swapped(v) for v in after((normed_a, normed_b), gsib)]
    from_low, from_high = shifted(opp_low, 1), shifted(opp_high, -1)
    got_high, got_low = shifted(up_high, 1), shifted(down_low, -1)
    key_grad, value_grad = weight_grads(normed_a, normed_b, *normed_far, gnear, gfar)
    from_low, from_high = after((from_low, from_high), key_grad, value_grad)
    last_low = shifted((wide(up_low) + wide(from_low)).astype(BF16), 1)
    last_high = shifted((wide(down_high) + wide(from_high)).astype(BF16), -1)
    summed_low = wide(kept[: segs // 2]) + wide(got_low) + wide(last_low)
    summed_high = wide(kept[segs // 2 :]) + wide(got_high) + wide(last_high)
    summed_a = above(summed_low, summed_high).astype(BF16).reshape(plane, half, HD)

    arrived_b, summed_a = lax.optimization_barrier((arrived_b, summed_a))
    arrived_a = over_plane(summed_a)
    kept_b, dots, to_1, to_2, to_3 = merge_b(arrived_b, half)
    received = (shifted(to_1, 1), shifted(to_2, 2), shifted(to_3, -1))
    keep, send = finish(place, norm_gain, block, scale_a, scale_b, arrived_a, kept_b, dots, received)
    came = swapped(send)
    result = jnp.where(core == 0, above(keep, came), above(came, keep))
    return context[None], query_grad[None], key_grad[None], value_grad[None], result


def solution(mesh):
    fine = Mesh(mesh.devices.reshape(4, 2, 2, 4, 2), AXES)
    seg, tp = ("y", "xh"), ("xl", "z", "c")
    heads = P(seg, None, tp)
    return jax.shard_map(
        local,
        mesh=fine,
        in_specs=(P(seg, tp), P(), heads, heads, heads, heads),
        out_specs=(heads, heads, heads, heads, P(seg, tp)),
        check_vma=False,
    )
```

```python
import functools

import jax
import jax.numpy as jnp
from jax import lax
from jax.experimental import pallas as pl
from jax.experimental.pallas import tpu as pltpu
from jax.sharding import Mesh
from jax.sharding import PartitionSpec as P

HD = 256
AXES = ("y", "xh", "xl", "z", "c")
PLANE = ("y", "xh", "xl")
RING = 4
EXTRA = 16
EPS = 1e-06
F32 = jnp.float32
BF16 = jnp.bfloat16
MIB = 2**20
VMEM = pl.BlockSpec(memory_space=pltpu.VMEM)
SMEM = pl.BlockSpec(memory_space=pltpu.SMEM)
ANYWHERE = pl.BlockSpec(memory_space=pl.ANY)


def dot(a, b, contract):
    return lax.dot_general(a, b, ((contract[:1], contract[1:]), ((), ())), preferred_element_type=F32)


def nn(a, b):
    return dot(a, b, (1, 0))


def nt(a, b):
    return dot(a, b, (1, 1))


def tn(a, b):
    return dot(a, b, (0, 0))


def beside(*values):
    return jnp.concatenate(values, axis=1)


def above(*values):
    return jnp.concatenate(values, axis=0)


def limits(mib):
    return pltpu.CompilerParams(vmem_limit_bytes=mib * MIB)


def cost(flops, mib, transcendentals=0):
    return pl.CostEstimate(flops=flops, bytes_accessed=int(mib * MIB), transcendentals=transcendentals)


def stage_body(*refs):
    sources, (first_ref, second_ref) = refs[:-2], refs[-2:]
    for i, source in enumerate(sources):
        first_ref[0, :, i * HD : (i + 1) * HD] = source[:HD]
        second_ref[0, :, i * HD : (i + 1) * HD] = source[HD:]


def staged(weights):
    count, blocks = len(weights), weights[0].shape[0] // (2 * HD)
    block = pl.BlockSpec((1, HD, count * HD), lambda i: (i, 0, 0))
    out = pltpu.HBM((blocks, HD, count * HD), BF16)
    return pl.pallas_call(
        stage_body,
        grid=(blocks,),
        in_specs=[pl.BlockSpec((2 * HD, HD), lambda i: (i, 0))] * count,
        out_specs=[block] * 2,
        out_shape=[out] * 2,
        compiler_params=limits(8),
        cost_estimate=cost(0, 16),
        name="stage",
    )(*[in_hbm(w) for w in weights])


def project_body(pieces, z_ref, gain_ref, *refs):
    xs = refs[: len(pieces)]
    w_refs, refs = refs[len(pieces) : len(pieces) + 2], refs[len(pieces) + 2 :]
    own_ref, sib_ref, scale_ref, normed_ref, held, rows_low, weights, x_sem, w_sem, out_sem = refs
    blocks, segs, part, width = held.shape
    rows = segs * part
    z = z_ref[0]
    copies = []
    for (distance, first, depth), x in zip(pieces, xs):
        for side in range(2):
            place = side * RING + lax.rem(z + distance, RING)
            source = x.at[:, side] if depth is None else x.at[:, side, depth]
            target = held.at[place, pl.ds(first, source.shape[0])]
            copies.append(pltpu.make_async_copy(source, target, x_sem.at[len(copies)]))
    loads = [
        pltpu.make_async_copy(w.at[p], weights.at[pl.ds((2 * p + i) * HD, HD)], w_sem.at[2 * p + i])
        for p in range(blocks)
        for i, w in enumerate(w_refs)
    ]
    for copy in copies + loads:
        copy.start()
    for copy in copies:
        copy.wait()
    squares = jnp.zeros((rows, 128), F32)
    for p in range(blocks):
        wide = held[p].reshape(rows, width).astype(F32)
        wide = wide * wide
        for i in range(width // 128):
            squares += wide[:, i * 128 : (i + 1) * 128]
    scale = lax.rsqrt(jnp.sum(squares, axis=1, keepdims=True) / (blocks * width) + EPS)
    scale_ref[...] = scale
    for p in range(blocks):
        wide = held[p].reshape(rows, width).astype(F32)
        rows_low[:, p * width : (p + 1) * width] = (wide * scale * gain_ref[p]).astype(BF16)
    out = pltpu.make_async_copy(rows_low, normed_ref, out_sem)
    out.start()
    for load in loads:
        load.wait()
    for i, out_ref in enumerate((own_ref, sib_ref)):
        at = 2 * HD * i
        out_ref[...] = nn(rows_low[...], weights[:, at : at + 2 * HD]).astype(BF16)
    out.wait()


def project(pieces, xs, z, gain, weights, segs, name):
    part, width = xs[0].shape[-2:]
    blocks = gain.shape[0] // width
    rows = segs * part
    return pl.pallas_call(
        functools.partial(project_body, pieces),
        in_specs=[SMEM, VMEM] + [ANYWHERE] * (len(xs) + 2),
        out_specs=[VMEM, VMEM, VMEM, ANYWHERE],
        out_shape=[
            jax.ShapeDtypeStruct((rows, 2 * HD), BF16),
            jax.ShapeDtypeStruct((rows, 2 * HD), BF16),
            jax.ShapeDtypeStruct((rows, 1), F32),
            jax.ShapeDtypeStruct((rows, blocks * width), BF16),
        ],
        scratch_shapes=[
            pltpu.VMEM((blocks, segs, part, width), BF16),
            pltpu.VMEM((rows, blocks * width), BF16),
            pltpu.VMEM((blocks * width, 4 * HD), BF16),
            pltpu.SemaphoreType.DMA((2 * len(xs),)),
            pltpu.SemaphoreType.DMA((2 * blocks,)),
            pltpu.SemaphoreType.DMA(()),
        ],
        compiler_params=limits(24),
        cost_estimate=cost(2 * rows * blocks * width * 4 * HD, 12),
        name=name,
    )(z, gain.reshape(blocks, 1, width), *xs, *[in_hbm(w) for w in weights])


def pieces_of(dots):
    high = dots.astype(BF16).astype(F32)
    shape = (EXTRA, dots.shape[1])
    row = lax.broadcasted_iota(jnp.int32, shape, 0)
    low = jnp.broadcast_to(dots - high, shape)
    return jnp.where(row == 0, jnp.broadcast_to(high, shape), jnp.where(row == 1, low, 0.0)).astype(BF16)


def in_two_rows(pieces):
    return above(pieces[:, :HD], pieces[:, HD:])


def dots_of(rows):
    return beside(rows[0:1] + rows[1:2], rows[EXTRA : EXTRA + 1] + rows[EXTRA + 1 : EXTRA + 2])


def attend_body(tile, q_ref, dc_ref, near_a, near_b, far_a, far_b, ctx_ref, qg_ref, gnear_ref, gfar_ref, near_dots, gkeys, gvalues):
    kv = above(near_a[...], near_b[...], far_a[...], far_b[...])
    k, v = kv[:, :HD], kv[:, HD:]
    half = kv.shape[0] // 2
    scale = HD ** (-0.5)
    row_products = jnp.zeros((8, kv.shape[0]), F32)
    for i in range(q_ref.shape[0] // tile):
        here = slice(i * tile, (i + 1) * tile)
        q, dc = q_ref[here], dc_ref[here]
        scores = nt(q, k) * scale
        expo = jnp.exp(scores - jnp.max(scores, axis=-1, keepdims=True))
        attend = expo * (1.0 / jnp.sum(expo, axis=-1, keepdims=True))
        low = attend.astype(BF16)
        ctx_ref[here] = nn(low, v).astype(BF16)
        gattend = nt(dc, v)
        dots = jnp.sum(gattend * attend, axis=-1, keepdims=True)
        gscores = attend * (gattend - dots)
        both = gscores * scores + attend * gattend
        row_products += jnp.sum(both.reshape(tile // 8, 8, kv.shape[0]), axis=0)
        gscores = (gscores * scale).astype(BF16)
        qg_ref[here] = nn(gscores, k).astype(BF16)
        if i == 0:
            gkeys[...] = tn(gscores, q)
            gvalues[...] = tn(low, dc)
        else:
            gkeys[...] += tn(gscores, q)
            gvalues[...] += tn(low, dc)
    gnear_ref[:, :HD] = gkeys[:half].astype(BF16)
    gnear_ref[:, HD:] = gvalues[:half].astype(BF16)
    gfar_ref[:half, :HD] = gkeys[half:].astype(BF16)
    gfar_ref[:half, HD:] = gvalues[half:].astype(BF16)
    row_products = jnp.sum(row_products, axis=0, keepdims=True)
    near_dots[...] = row_products[:, :half]
    gfar_ref[half:] = pieces_of(row_products[:, half:])


def attention(q, dc, near_a, near_b, far_a, far_b, tile=256):
    targets, half = q.shape[0], 2 * near_a.shape[0]
    return pl.pallas_call(
        functools.partial(attend_body, tile),
        in_specs=[VMEM] * 6,
        out_specs=[VMEM] * 5,
        out_shape=[jax.ShapeDtypeStruct((targets, HD), BF16)] * 2
        + [
            jax.ShapeDtypeStruct((half, 2 * HD), BF16),
            jax.ShapeDtypeStruct((half + EXTRA, 2 * HD), BF16),
            jax.ShapeDtypeStruct((1, half), F32),
        ],
        scratch_shapes=[pltpu.VMEM((2 * half, HD), F32)] * 2,
        compiler_params=limits(20),
        cost_estimate=cost(12 * targets * 2 * half * HD, 4, targets * 2 * half),
        name="attention",
    )(q, dc, near_a, near_b, far_a, far_b)


def feature_block(z, rows, w_ref, distance, side):
    return nt(rows, w_ref[side * RING + lax.rem(z + distance, RING)]).astype(BF16)


def back_b_body(z_ref, own_ref, sib_ref, dots_ref, w_ref, out_ref, stage, out_sem):
    half = own_ref.shape[0]
    segs = out_ref.shape[0]
    part = half // segs // 2
    rows = beside(own_ref[...], sib_ref[:half])
    outs = []
    for distance in range(RING):
        at = distance * 2 * part
        for side in range(2):
            value = feature_block(z_ref[0], rows, w_ref, distance, side).reshape(2, segs, part, HD)
            for k in range(2):
                stage[:, side, at + k * part : at + (k + 1) * part] = value[k]
        size = 2 * part
        if distance == RING - 1:
            extra = sib_ref[half:].astype(F32)
            pieces = in_two_rows(pieces_of(dots_ref[...] + extra[0:1] + extra[1:2]))
            stage[:, :, at + size :] = jnp.broadcast_to(pieces, (segs, 2, 2 * EXTRA, HD))
            size += 2 * EXTRA
        outs.append(pltpu.make_async_copy(stage.at[:, :, pl.ds(at, size)], out_ref.at[:, :, pl.ds(at, size)], out_sem.at[distance]))
        outs[-1].start()
    for out in outs:
        out.wait()


def back_b(z, own, sib, dots, weights, segs):
    rows = own.shape[0]
    shape = (segs, 2, RING * rows // segs + 2 * EXTRA, HD)
    return pl.pallas_call(
        back_b_body,
        in_specs=[SMEM] + [VMEM] * 4,
        out_specs=ANYWHERE,
        out_shape=pltpu.HBM(shape, BF16),
        scratch_shapes=[
            pltpu.VMEM(shape, BF16),
            pltpu.SemaphoreType.DMA((RING,)),
        ],
        compiler_params=limits(16),
        cost_estimate=cost(2 * rows * 8 * HD * 4 * HD, 4),
        name="back_b",
    )(z, own, sib, dots, in_vmem(weights))


def back_a_body(z_ref, own_ref, sib_ref, w_ref, *outs):
    rows = beside(own_ref[...], sib_ref[: own_ref.shape[0]])
    segs = outs[-1].shape[0]
    part = rows.shape[0] // segs // 2
    lands = {2: ((0, 0), (1, segs // 2)), 1: ((2, 0), (3, segs // 2)), 3: ((4, 0), (5, segs // 2)), 0: ((6, 0),)}
    for distance in (2, 1, 3, 0):
        for side in range(2):
            value = feature_block(z_ref[0], rows, w_ref, distance, side).reshape(2, segs, part, HD)
            for index, first in lands[distance]:
                for k in range(2):
                    count = outs[index].shape[0]
                    outs[index][:, side, k * part : (k + 1) * part] = value[k, first : first + count]


def back_a(z, own, sib, weights, segs):
    rows = own.shape[0]
    half = jax.ShapeDtypeStruct((segs // 2, 2, rows // segs, HD), BF16)
    full = jax.ShapeDtypeStruct((segs, 2, rows // segs, HD), BF16)
    return pl.pallas_call(
        back_a_body,
        in_specs=[SMEM] + [VMEM] * 3,
        out_specs=[VMEM] * 7,
        out_shape=[half] * 6 + [full],
        compiler_params=limits(16),
        cost_estimate=cost(2 * rows * 8 * HD * 4 * HD, 4),
        name="back_a",
    )(z, own, sib, in_vmem(weights))


def weights_body(near_a, near_b, far_a, far_b, gnear_ref, gfar_ref, gk_ref, gv_ref):
    rows = above(near_a[...], near_b[...], far_a[...], far_b[...])
    total = tn(rows, above(gnear_ref[...], gfar_ref[: gnear_ref.shape[0]]))
    gk_ref[...] = total[:, :HD]
    gv_ref[...] = total[:, HD:]


def weight_grads(near_a, near_b, far_a, far_b, gnear, gfar, width=512):
    rows, hidden = near_a.shape
    block = pl.BlockSpec((rows, width), lambda i: (0, i))
    near = pl.BlockSpec(gnear.shape, lambda i: (0, 0))
    far = pl.BlockSpec(gfar.shape, lambda i: (0, 0))
    out = pl.BlockSpec((width, HD), lambda i: (i, 0))
    return pl.pallas_call(
        weights_body,
        grid=(hidden // width,),
        in_specs=[block] * 4 + [near, far],
        out_specs=[out, out],
        out_shape=[jax.ShapeDtypeStruct((hidden, HD), F32)] * 2,
        compiler_params=limits(16),
        cost_estimate=cost(16 * rows * hidden * HD, 17),
        name="weight_grads",
    )(near_a, near_b, far_a, far_b, gnear, gfar)


def merge_b_body(arrived_ref, kept_ref, dots_ref, *send_refs):
    half = kept_ref.shape[0]
    total = arrived_ref[0].astype(F32)
    for i in range(1, arrived_ref.shape[0]):
        total += arrived_ref[i].astype(F32)
    kept_ref[...] = total[:half]
    both = dots_of(total[RING * half :])
    dots_ref[...] = both
    pieces = in_two_rows(pieces_of(both))
    for i, ref in enumerate(send_refs):
        ref[:half] = total[(i + 1) * half : (i + 2) * half].astype(BF16)
        ref[half:] = pieces


def merge_b(arrived, half):
    send = jax.ShapeDtypeStruct((half + 2 * EXTRA, HD), BF16)
    return pl.pallas_call(
        merge_b_body,
        in_specs=[VMEM],
        out_specs=[VMEM] * 5,
        out_shape=[jax.ShapeDtypeStruct((half, HD), F32), jax.ShapeDtypeStruct((1, 2 * HD), F32)] + [send] * 3,
        compiler_params=limits(16),
        cost_estimate=cost(0, 3),
        name="merge_b",
    )(arrived)


def finish_body(hidden, place_ref, gain_ref, block_ref, scale_a, scale_b, arrived_ref, kept_ref, dots_ref, r1, r2, r3,
                keep_ref, send_ref):
    core, segment, pair = place_ref[0], place_ref[1], place_ref[2]
    half = block_ref.shape[0]
    part = half // 2
    left = arrived_ref[0].astype(F32)
    for i in range(1, arrived_ref.shape[0]):
        left += arrived_ref[i].astype(F32)
    right, dots = kept_ref[...], dots_ref[...]
    for ref in (r1, r2, r3):
        right += ref[:half].astype(F32)
        dots += dots_of(ref[half:].astype(F32))
    lane = lax.broadcasted_iota(jnp.int32, (part, HD), 1)
    row = lax.broadcasted_iota(jnp.int32, (part, HD), 0)
    mine = lane == row + segment * part
    pick = lambda values: jnp.sum(jnp.where(mine, values, 0.0), axis=1, keepdims=True)
    mean = above(pick(dots[:, :HD]), pick(dots[:, HD:])) / hidden
    rows = pl.ds(pl.multiple_of(segment * part, part), part)
    scale = above(scale_a[rows], scale_b[rows])
    gain = gain_ref[pair]
    for side, total in enumerate((left, right)):
        at = slice(side * HD, (side + 1) * HD)
        value = scale * (total * gain[:, at] - block_ref[:, at].astype(F32) * scale * mean)

        @pl.when(core == side)
        def _():
            keep_ref[...] = value

        @pl.when(core != side)
        def _():
            send_ref[...] = value


def finish(place, gain, block, scale_a, scale_b, arrived, kept, dots, received):
    half, width = block.shape
    hidden = gain.shape[0]
    return pl.pallas_call(
        functools.partial(finish_body, hidden),
        in_specs=[SMEM] + [VMEM] * 10,
        out_specs=[VMEM] * 2,
        out_shape=[jax.ShapeDtypeStruct((half, HD), F32)] * 2,
        compiler_params=limits(16),
        cost_estimate=cost(0, 1),
        name="finish",
    )(place, gain.reshape(hidden // width, 1, width), block, scale_a, scale_b, arrived, kept, dots, *received)


def in_vmem(value):
    return pltpu.with_memory_space_constraint(value, pltpu.VMEM)


def in_hbm(value):
    return pltpu.with_memory_space_constraint(value, pltpu.HBM)


def swapped(value):
    return lax.ppermute(value, "c", [(0, 1), (1, 0)])


def shifted(value, by):
    return lax.ppermute(value, "z", [(i, (i + by) % RING) for i in range(RING)])


def over_plane(value):
    return lax.all_to_all(value, PLANE, 0, 0, tiled=True)


def after(values, *earlier):
    return lax.optimization_barrier((*values, *earlier))[: len(values)]


def local(memory, norm_gain, queries, key_weight, value_weight, context_grad):
    rows_own, cols_own = memory.shape
    half, width = rows_own // 2, 2 * cols_own
    part = half // 2
    core, z = lax.axis_index("c"), lax.axis_index("z")
    segment = lax.axis_index(("y", "xh"))
    pair = lax.axis_index(("xl", "z"))
    segs, plane = lax.axis_size(("y", "xh")), lax.axis_size(PLANE)
    z_array = z.astype(jnp.int32).reshape(1)
    place = jnp.stack([core, segment, pair]).astype(jnp.int32)
    wide = lambda value: value.astype(F32)

    halves = memory.reshape(2, half, cols_own)
    mine = lax.dynamic_index_in_dim(halves, core, 0, keepdims=False)
    other = swapped(lax.dynamic_index_in_dim(halves, 1 - core, 0, keepdims=False))
    block = jnp.where(core == 0, beside(mine, other), beside(other, mine))
    first_a = over_plane(jnp.broadcast_to(block[:part], (plane, part, width)))
    high = block[part:]
    near_z = jnp.stack([high, shifted(high, -1), shifted(high, 2), shifted(high, 1)])
    all_b = over_plane(jnp.broadcast_to(near_z, (plane, RING, part, width)))
    all_b = all_b.reshape(segs, 2, RING, part, width)
    low_0, high_0 = first_a[: plane // 2], first_a[plane // 2 :]
    low_3, high_1 = shifted(low_0, 1), shifted(high_0, -1)
    high_3, low_1 = shifted(high_0, 1), shifted(low_0, -1)
    low_2, high_2 = shifted(low_3, 1), shifted(high_1, -1)
    deep = lambda value: value.reshape(segs // 2, 2, part, width)

    key_own, value_own = after((key_weight[0], value_weight[0]), near_z, first_a)
    weights = staged((key_own, value_own, swapped(key_own), swapped(value_own)))

    top = segs // 2
    pieces_a = [(0, 0, None), (3, 0, None), (3, top, None), (1, 0, None), (1, top, None), (2, 0, None), (2, top, None)]
    xs_a = [first_a.reshape(segs, 2, part, width)] + [deep(v) for v in (low_3, high_3, low_1, high_1, low_2, high_2)]
    xs_a = [in_hbm(x) for x in xs_a]
    own_a, sib_a, scale_a, normed_a = project(pieces_a, xs_a, z_array, norm_gain, weights, segs, "project_a")
    far_a = swapped(sib_a)
    all_b, = after((all_b,), own_a)
    pieces_b = [(d, 0, d) for d in range(RING)]
    own_b, sib_b, scale_b, normed_b = project(pieces_b, [all_b] * RING, z_array, norm_gain, weights, segs, "project_b")
    far_b = swapped(sib_b)
    context, query_grad, gnear, gfar, near_dots = attention(queries[0], context_grad[0], own_a, own_b, far_a, far_b)
    gsib = swapped(gfar)

    parts_b = back_b(z_array, gnear, gsib, near_dots, weights[1], segs)
    arrived_b = over_plane(parts_b.reshape(plane, RING * half + 2 * EXTRA, HD))
    z_later, = after((z_array,), parts_b)
    opp_low, opp_high, up_low, up_high, down_low, down_high, kept = back_a(z_later, gnear, gsib, weights[0], segs)
    normed_far = [swapped(v) for v in after((normed_a, normed_b), parts_b)]
    from_low, from_high = shifted(opp_low, 1), shifted(opp_high, -1)
    got_high, got_low = shifted(up_high, 1), shifted(down_low, -1)
    key_grad, value_grad = weight_grads(normed_a, normed_b, *normed_far, gnear, gfar)
    from_low, from_high = after((from_low, from_high), key_grad, value_grad)
    last_low = shifted((wide(up_low) + wide(from_low)).astype(BF16), 1)
    last_high = shifted((wide(down_high) + wide(from_high)).astype(BF16), -1)
    summed_low = wide(kept[: segs // 2]) + wide(got_low) + wide(last_low)
    summed_high = wide(kept[segs // 2 :]) + wide(got_high) + wide(last_high)
    summed_a = above(summed_low, summed_high).astype(BF16).reshape(plane, half, HD)

    arrived_b, summed_a = lax.optimization_barrier((arrived_b, summed_a))
    arrived_a = over_plane(summed_a)
    kept_b, dots, to_1, to_2, to_3 = merge_b(arrived_b, half)
    received = (shifted(to_1, 1), shifted(to_2, 2), shifted(to_3, -1))
    keep, send = finish(place, norm_gain, block, scale_a, scale_b, arrived_a, kept_b, dots, received)
    came = swapped(send)
    result = jnp.where(core == 0, above(keep, came), above(came, keep))
    return context[None], query_grad[None], key_grad[None], value_grad[None], result


def solution(mesh):
    fine = Mesh(mesh.devices.reshape(4, 2, 2, 4, 2), AXES)
    seg, tp = ("y", "xh"), ("xl", "z", "c")
    heads = P(seg, None, tp)
    return jax.shard_map(
        local,
        mesh=fine,
        in_specs=(P(seg, tp), P(), heads, heads, heads, heads),
        out_specs=(heads, heads, heads, heads, P(seg, tp)),
        check_vma=False,
    )
```

```python
import functools

import jax
import jax.numpy as jnp
from jax import lax
from jax.experimental import pallas as pl
from jax.experimental.pallas import tpu as pltpu
from jax.sharding import Mesh
from jax.sharding import PartitionSpec as P

HD = 256
AXES = ("y", "xh", "xl", "z", "c")
PLANE = ("y", "xh", "xl")
RING = 4
EXTRA = 16
EPS = 1e-06
F32 = jnp.float32
BF16 = jnp.bfloat16
MIB = 2**20
VMEM = pl.BlockSpec(memory_space=pltpu.VMEM)
SMEM = pl.BlockSpec(memory_space=pltpu.SMEM)
ANYWHERE = pl.BlockSpec(memory_space=pl.ANY)


def dot(a, b, contract):
    return lax.dot_general(a, b, ((contract[:1], contract[1:]), ((), ())), preferred_element_type=F32)


def nn(a, b):
    return dot(a, b, (1, 0))


def nt(a, b):
    return dot(a, b, (1, 1))


def tn(a, b):
    return dot(a, b, (0, 0))


def beside(*values):
    return jnp.concatenate(values, axis=1)


def above(*values):
    return jnp.concatenate(values, axis=0)


def limits(mib):
    return pltpu.CompilerParams(vmem_limit_bytes=mib * MIB)


def cost(flops, mib, transcendentals=0):
    return pl.CostEstimate(flops=flops, bytes_accessed=int(mib * MIB), transcendentals=transcendentals)


def stage_body(*refs):
    sources, (first_ref, second_ref) = refs[:-2], refs[-2:]
    for i, source in enumerate(sources):
        first_ref[0, :, i * HD : (i + 1) * HD] = source[:HD]
        second_ref[0, :, i * HD : (i + 1) * HD] = source[HD:]


def staged(weights):
    count, blocks = len(weights), weights[0].shape[0] // (2 * HD)
    block = pl.BlockSpec((1, HD, count * HD), lambda i: (i, 0, 0))
    out = pltpu.HBM((blocks, HD, count * HD), BF16)
    return pl.pallas_call(
        stage_body,
        grid=(blocks,),
        in_specs=[pl.BlockSpec((2 * HD, HD), lambda i: (i, 0))] * count,
        out_specs=[block] * 2,
        out_shape=[out] * 2,
        compiler_params=limits(8),
        cost_estimate=cost(0, 16),
        name="stage",
    )(*[in_hbm(w) for w in weights])


def project_body(pieces, z_ref, gain_ref, *refs):
    xs = refs[: len(pieces)]
    w_refs, refs = refs[len(pieces) : len(pieces) + 2], refs[len(pieces) + 2 :]
    own_ref, sib_ref, scale_ref, normed_ref, held, rows_low, weights, x_sem, w_sem, out_sem = refs
    blocks, segs, part, width = held.shape
    rows = segs * part
    z = z_ref[0]
    copies = []
    for (distance, first, depth), x in zip(pieces, xs):
        for side in range(2):
            place = side * RING + lax.rem(z + distance, RING)
            source = x.at[:, side] if depth is None else x.at[:, side, depth]
            target = held.at[place, pl.ds(first, source.shape[0])]
            copies.append(pltpu.make_async_copy(source, target, x_sem.at[len(copies)]))
    loads = [pltpu.make_async_copy(w, weights.at[i], w_sem.at[i]) for i, w in enumerate(w_refs)]
    for copy in copies + loads:
        copy.start()
    for copy in copies:
        copy.wait()
    squares = jnp.zeros((rows, 128), F32)
    for p in range(blocks):
        wide = held[p].reshape(rows, width).astype(F32)
        wide = wide * wide
        for i in range(width // 128):
            squares += wide[:, i * 128 : (i + 1) * 128]
    scale = lax.rsqrt(jnp.sum(squares, axis=1, keepdims=True) / (blocks * width) + EPS)
    scale_ref[...] = scale
    for p in range(blocks):
        wide = held[p].reshape(rows, width).astype(F32)
        rows_low[:, p * width : (p + 1) * width] = (wide * scale * gain_ref[p]).astype(BF16)
    out = pltpu.make_async_copy(rows_low, normed_ref, out_sem)
    out.start()
    total = 0.0
    for i, load in enumerate(loads):
        load.wait()
        columns = beside(*[rows_low[:, (2 * p + i) * HD : (2 * p + i + 1) * HD] for p in range(blocks)])
        total += nn(columns, weights[i].reshape(blocks * HD, 4 * HD))
    own_ref[...] = total[:, : 2 * HD].astype(BF16)
    sib_ref[...] = total[:, 2 * HD :].astype(BF16)
    out.wait()


def project(pieces, xs, z, gain, weights, segs, name):
    part, width = xs[0].shape[-2:]
    blocks = gain.shape[0] // width
    rows = segs * part
    return pl.pallas_call(
        functools.partial(project_body, pieces),
        in_specs=[SMEM, VMEM] + [ANYWHERE] * (len(xs) + 2),
        out_specs=[VMEM, VMEM, VMEM, ANYWHERE],
        out_shape=[
            jax.ShapeDtypeStruct((rows, 2 * HD), BF16),
            jax.ShapeDtypeStruct((rows, 2 * HD), BF16),
            jax.ShapeDtypeStruct((rows, 1), F32),
            jax.ShapeDtypeStruct((rows, blocks * width), BF16),
        ],
        scratch_shapes=[
            pltpu.VMEM((blocks, segs, part, width), BF16),
            pltpu.VMEM((rows, blocks * width), BF16),
            pltpu.VMEM((2, blocks, HD, 4 * HD), BF16),
            pltpu.SemaphoreType.DMA((2 * len(xs),)),
            pltpu.SemaphoreType.DMA((2,)),
            pltpu.SemaphoreType.DMA(()),
        ],
        compiler_params=limits(24),
        cost_estimate=cost(2 * rows * blocks * width * 4 * HD, 12),
        name=name,
    )(z, gain.reshape(blocks, 1, width), *xs, *[in_hbm(w) for w in weights])


def pieces_of(dots):
    high = dots.astype(BF16).astype(F32)
    shape = (EXTRA, dots.shape[1])
    row = lax.broadcasted_iota(jnp.int32, shape, 0)
    low = jnp.broadcast_to(dots - high, shape)
    return jnp.where(row == 0, jnp.broadcast_to(high, shape), jnp.where(row == 1, low, 0.0)).astype(BF16)


def in_four_rows(dots):
    left, right = pieces_of(dots[:, :HD]).astype(F32), pieces_of(dots[:, HD:]).astype(F32)
    row = lax.broadcasted_iota(jnp.int32, left.shape, 0)
    later = jnp.where(row == 2, right[0:1], jnp.where(row == 3, right[1:2], 0.0))
    return jnp.where(row < 2, left, later).astype(BF16)


def dots_of(rows):
    return beside(rows[0:1] + rows[1:2], rows[2:3] + rows[3:4])


def attend_body(tile, q_ref, dc_ref, near_a, near_b, far_a, far_b, ctx_ref, qg_ref, gnear_ref, gfar_ref, near_dots, gkeys, gvalues):
    kv = above(near_a[...], near_b[...], far_a[...], far_b[...])
    k, v = kv[:, :HD], kv[:, HD:]
    half = kv.shape[0] // 2
    scale = HD ** (-0.5)
    row_products = jnp.zeros((8, kv.shape[0]), F32)
    for i in range(q_ref.shape[0] // tile):
        here = slice(i * tile, (i + 1) * tile)
        q, dc = q_ref[here], dc_ref[here]
        scores = nt(q, k) * scale
        expo = jnp.exp(scores - jnp.max(scores, axis=-1, keepdims=True))
        attend = expo * (1.0 / jnp.sum(expo, axis=-1, keepdims=True))
        low = attend.astype(BF16)
        ctx_ref[here] = nn(low, v).astype(BF16)
        gattend = nt(dc, v)
        dots = jnp.sum(gattend * attend, axis=-1, keepdims=True)
        gscores = attend * (gattend - dots)
        both = gscores * scores + attend * gattend
        row_products += jnp.sum(both.reshape(tile // 8, 8, kv.shape[0]), axis=0)
        gscores = (gscores * scale).astype(BF16)
        qg_ref[here] = nn(gscores, k).astype(BF16)
        if i == 0:
            gkeys[...] = tn(gscores, q)
            gvalues[...] = tn(low, dc)
        else:
            gkeys[...] += tn(gscores, q)
            gvalues[...] += tn(low, dc)
    gnear_ref[:, :HD] = gkeys[:half].astype(BF16)
    gnear_ref[:, HD:] = gvalues[:half].astype(BF16)
    gfar_ref[:half, :HD] = gkeys[half:].astype(BF16)
    gfar_ref[:half, HD:] = gvalues[half:].astype(BF16)
    row_products = jnp.sum(row_products, axis=0, keepdims=True)
    near_dots[...] = row_products[:, :half]
    gfar_ref[half:] = pieces_of(row_products[:, half:])


def attention(q, dc, near_a, near_b, far_a, far_b, tile=256):
    targets, half = q.shape[0], 2 * near_a.shape[0]
    return pl.pallas_call(
        functools.partial(attend_body, tile),
        in_specs=[VMEM] * 6,
        out_specs=[VMEM] * 5,
        out_shape=[jax.ShapeDtypeStruct((targets, HD), BF16)] * 2
        + [
            jax.ShapeDtypeStruct((half, 2 * HD), BF16),
            jax.ShapeDtypeStruct((half + EXTRA, 2 * HD), BF16),
            jax.ShapeDtypeStruct((1, half), F32),
        ],
        scratch_shapes=[pltpu.VMEM((2 * half, HD), F32)] * 2,
        compiler_params=limits(20),
        cost_estimate=cost(12 * targets * 2 * half * HD, 4, targets * 2 * half),
        name="attention",
    )(q, dc, near_a, near_b, far_a, far_b)


def feature_block(z, rows, w_ref, distance, side):
    return nt(rows, w_ref[side * RING + lax.rem(z + distance, RING)]).astype(BF16)


def back_b_body(z_ref, own_ref, sib_ref, dots_ref, w_ref, out_ref, stage, out_sem):
    half = own_ref.shape[0]
    segs = out_ref.shape[0]
    part = half // segs // 2
    rows = beside(own_ref[...], sib_ref[:half])
    outs = []
    for distance in range(RING):
        at = distance * 2 * part
        for side in range(2):
            value = feature_block(z_ref[0], rows, w_ref, distance, side).reshape(2, segs, part, HD)
            for k in range(2):
                stage[:, side, at + k * part : at + (k + 1) * part] = value[k]
        size = 2 * part
        if distance == RING - 1:
            extra = sib_ref[half:].astype(F32)
            pieces = in_four_rows(dots_ref[...] + extra[0:1] + extra[1:2])
            stage[:, :, at + size :] = jnp.broadcast_to(pieces, (segs, 2, EXTRA, HD))
            size += EXTRA
        outs.append(pltpu.make_async_copy(stage.at[:, :, pl.ds(at, size)], out_ref.at[:, :, pl.ds(at, size)], out_sem.at[distance]))
        outs[-1].start()
    for out in outs:
        out.wait()


def back_b(z, own, sib, dots, weights, segs):
    rows = own.shape[0]
    shape = (segs, 2, RING * rows // segs + EXTRA, HD)
    return pl.pallas_call(
        back_b_body,
        in_specs=[SMEM] + [VMEM] * 4,
        out_specs=ANYWHERE,
        out_shape=pltpu.HBM(shape, BF16),
        scratch_shapes=[
            pltpu.VMEM(shape, BF16),
            pltpu.SemaphoreType.DMA((RING,)),
        ],
        compiler_params=limits(16),
        cost_estimate=cost(2 * rows * 8 * HD * 4 * HD, 4),
        name="back_b",
    )(z, own, sib, dots, in_vmem(weights))


def back_a_body(z_ref, own_ref, sib_ref, w_ref, *outs):
    rows = beside(own_ref[...], sib_ref[: own_ref.shape[0]])
    segs = outs[-1].shape[0]
    part = rows.shape[0] // segs // 2
    lands = {2: ((0, 0), (1, segs // 2)), 1: ((2, 0), (3, segs // 2)), 3: ((4, 0), (5, segs // 2)), 0: ((6, 0),)}
    for distance in (2, 1, 3, 0):
        for side in range(2):
            value = feature_block(z_ref[0], rows, w_ref, distance, side).reshape(2, segs, part, HD)
            for index, first in lands[distance]:
                for k in range(2):
                    count = outs[index].shape[0]
                    outs[index][:, side, k * part : (k + 1) * part] = value[k, first : first + count]


def back_a(z, own, sib, weights, segs):
    rows = own.shape[0]
    half = jax.ShapeDtypeStruct((segs // 2, 2, rows // segs, HD), BF16)
    full = jax.ShapeDtypeStruct((segs, 2, rows // segs, HD), BF16)
    return pl.pallas_call(
        back_a_body,
        in_specs=[SMEM] + [VMEM] * 3,
        out_specs=[VMEM] * 7,
        out_shape=[half] * 6 + [full],
        compiler_params=limits(16),
        cost_estimate=cost(2 * rows * 8 * HD * 4 * HD, 4),
        name="back_a",
    )(z, own, sib, in_vmem(weights))


def weights_body(near_a, near_b, far_a, far_b, gnear_ref, gfar_ref, gk_ref, gv_ref):
    rows = above(near_a[...], near_b[...], far_a[...], far_b[...])
    total = tn(rows, above(gnear_ref[...], gfar_ref[: gnear_ref.shape[0]]))
    gk_ref[...] = total[:, :HD]
    gv_ref[...] = total[:, HD:]


def weight_grads(near_a, near_b, far_a, far_b, gnear, gfar, width=512):
    rows, hidden = near_a.shape
    block = pl.BlockSpec((rows, width), lambda i: (0, i))
    near = pl.BlockSpec(gnear.shape, lambda i: (0, 0))
    far = pl.BlockSpec(gfar.shape, lambda i: (0, 0))
    out = pl.BlockSpec((width, HD), lambda i: (i, 0))
    return pl.pallas_call(
        weights_body,
        grid=(hidden // width,),
        in_specs=[block] * 4 + [near, far],
        out_specs=[out, out],
        out_shape=[jax.ShapeDtypeStruct((hidden, HD), F32)] * 2,
        compiler_params=limits(16),
        cost_estimate=cost(16 * rows * hidden * HD, 17),
        name="weight_grads",
    )(near_a, near_b, far_a, far_b, gnear, gfar)


def merge_b_body(arrived_ref, kept_ref, dots_ref, *send_refs):
    half = kept_ref.shape[0]
    total = arrived_ref[0].astype(F32)
    for i in range(1, arrived_ref.shape[0]):
        total += arrived_ref[i].astype(F32)
    kept_ref[...] = total[:half]
    both = dots_of(total[RING * half :])
    dots_ref[...] = both
    pieces = in_four_rows(both)
    for i, ref in enumerate(send_refs):
        ref[:half] = total[(i + 1) * half : (i + 2) * half].astype(BF16)
        ref[half:] = pieces


def merge_b(arrived, half):
    send = jax.ShapeDtypeStruct((half + EXTRA, HD), BF16)
    return pl.pallas_call(
        merge_b_body,
        in_specs=[VMEM],
        out_specs=[VMEM] * 5,
        out_shape=[jax.ShapeDtypeStruct((half, HD), F32), jax.ShapeDtypeStruct((1, 2 * HD), F32)] + [send] * 3,
        compiler_params=limits(16),
        cost_estimate=cost(0, 3),
        name="merge_b",
    )(arrived)


def finish_body(hidden, place_ref, gain_ref, block_ref, scale_a, scale_b, arrived_ref, kept_ref, dots_ref, r1, r2, r3,
                keep_ref, send_ref):
    core, segment, pair = place_ref[0], place_ref[1], place_ref[2]
    half = block_ref.shape[0]
    part = half // 2
    left = arrived_ref[0].astype(F32)
    for i in range(1, arrived_ref.shape[0]):
        left += arrived_ref[i].astype(F32)
    right, dots = kept_ref[...], dots_ref[...]
    for ref in (r1, r2, r3):
        right += ref[:half].astype(F32)
        dots += dots_of(ref[half:].astype(F32))
    lane = lax.broadcasted_iota(jnp.int32, (part, HD), 1)
    row = lax.broadcasted_iota(jnp.int32, (part, HD), 0)
    mine = lane == row + segment * part
    pick = lambda values: jnp.sum(jnp.where(mine, values, 0.0), axis=1, keepdims=True)
    mean = above(pick(dots[:, :HD]), pick(dots[:, HD:])) / hidden
    rows = pl.ds(pl.multiple_of(segment * part, part), part)
    scale = above(scale_a[rows], scale_b[rows])
    gain = gain_ref[pair]
    for side, total in enumerate((left, right)):
        at = slice(side * HD, (side + 1) * HD)
        value = scale * (total * gain[:, at] - block_ref[:, at].astype(F32) * scale * mean)

        @pl.when(core == side)
        def _():
            keep_ref[...] = value

        @pl.when(core != side)
        def _():
            send_ref[...] = value


def finish(place, gain, block, scale_a, scale_b, arrived, kept, dots, received):
    half, width = block.shape
    hidden = gain.shape[0]
    return pl.pallas_call(
        functools.partial(finish_body, hidden),
        in_specs=[SMEM] + [VMEM] * 10,
        out_specs=[VMEM] * 2,
        out_shape=[jax.ShapeDtypeStruct((half, HD), F32)] * 2,
        compiler_params=limits(16),
        cost_estimate=cost(0, 1),
        name="finish",
    )(place, gain.reshape(hidden // width, 1, width), block, scale_a, scale_b, arrived, kept, dots, *received)


def in_vmem(value):
    return pltpu.with_memory_space_constraint(value, pltpu.VMEM)


def in_hbm(value):
    return pltpu.with_memory_space_constraint(value, pltpu.HBM)


def swapped(value):
    return lax.ppermute(value, "c", [(0, 1), (1, 0)])


def shifted(value, by):
    return lax.ppermute(value, "z", [(i, (i + by) % RING) for i in range(RING)])


def over_plane(value):
    return lax.all_to_all(value, PLANE, 0, 0, tiled=True)


def after(values, *earlier):
    return lax.optimization_barrier((*values, *earlier))[: len(values)]


def local(memory, norm_gain, queries, key_weight, value_weight, context_grad):
    rows_own, cols_own = memory.shape
    half, width = rows_own // 2, 2 * cols_own
    part = half // 2
    core, z = lax.axis_index("c"), lax.axis_index("z")
    segment = lax.axis_index(("y", "xh"))
    pair = lax.axis_index(("xl", "z"))
    segs, plane = lax.axis_size(("y", "xh")), lax.axis_size(PLANE)
    z_array = z.astype(jnp.int32).reshape(1)
    place = jnp.stack([core, segment, pair]).astype(jnp.int32)
    wide = lambda value: value.astype(F32)

    halves = memory.reshape(2, half, cols_own)
    mine = lax.dynamic_index_in_dim(halves, core, 0, keepdims=False)
    other = swapped(lax.dynamic_index_in_dim(halves, 1 - core, 0, keepdims=False))
    block = jnp.where(core == 0, beside(mine, other), beside(other, mine))
    first_a = over_plane(jnp.broadcast_to(block[:part], (plane, part, width)))
    high = block[part:]
    near_z = jnp.stack([high, shifted(high, -1), shifted(high, 2), shifted(high, 1)])
    all_b = over_plane(jnp.broadcast_to(near_z, (plane, RING, part, width)))
    all_b = all_b.reshape(segs, 2, RING, part, width)
    low_0, high_0 = first_a[: plane // 2], first_a[plane // 2 :]
    low_3, high_1 = shifted(low_0, 1), shifted(high_0, -1)
    high_3, low_1 = shifted(high_0, 1), shifted(low_0, -1)
    low_2, high_2 = shifted(low_3, 1), shifted(high_1, -1)
    deep = lambda value: value.reshape(segs // 2, 2, part, width)

    key_own, value_own = after((key_weight[0], value_weight[0]), near_z, first_a)
    weights = staged((key_own, value_own, swapped(key_own), swapped(value_own)))

    top = segs // 2
    pieces_a = [(0, 0, None), (3, 0, None), (3, top, None), (1, 0, None), (1, top, None), (2, 0, None), (2, top, None)]
    xs_a = [first_a.reshape(segs, 2, part, width)] + [deep(v) for v in (low_3, high_3, low_1, high_1, low_2, high_2)]
    xs_a = [in_hbm(x) for x in xs_a]
    own_a, sib_a, scale_a, normed_a = project(pieces_a, xs_a, z_array, norm_gain, weights, segs, "project_a")
    far_a = swapped(sib_a)
    all_b, = after((all_b,), own_a)
    pieces_b = [(d, 0, d) for d in range(RING)]
    own_b, sib_b, scale_b, normed_b = project(pieces_b, [all_b] * RING, z_array, norm_gain, weights, segs, "project_b")
    far_b = swapped(sib_b)
    context, query_grad, gnear, gfar, near_dots = attention(queries[0], context_grad[0], own_a, own_b, far_a, far_b)
    gsib = swapped(gfar)

    parts_b = back_b(z_array, gnear, gsib, near_dots, weights[1], segs)
    arrived_b = over_plane(parts_b.reshape(plane, RING * half + EXTRA, HD))
    z_later, = after((z_array,), parts_b)
    opp_low, opp_high, up_low, up_high, down_low, down_high, kept = back_a(z_later, gnear, gsib, weights[0], segs)
    normed_far = [swapped(v) for v in after((normed_a, normed_b), parts_b)]
    from_low, from_high = shifted(opp_low, 1), shifted(opp_high, -1)
    got_high, got_low = shifted(up_high, 1), shifted(down_low, -1)
    key_grad, value_grad = weight_grads(normed_a, normed_b, *normed_far, gnear, gfar)
    from_low, from_high = after((from_low, from_high), key_grad, value_grad)
    last_low = shifted((wide(up_low) + wide(from_low)).astype(BF16), 1)
    last_high = shifted((wide(down_high) + wide(from_high)).astype(BF16), -1)
    summed_low = wide(kept[: segs // 2]) + wide(got_low) + wide(last_low)
    summed_high = wide(kept[segs // 2 :]) + wide(got_high) + wide(last_high)
    summed_a = above(summed_low, summed_high).astype(BF16).reshape(plane, half, HD)

    arrived_b, summed_a = lax.optimization_barrier((arrived_b, summed_a))
    arrived_a = over_plane(summed_a)
    kept_b, dots, to_1, to_2, to_3 = merge_b(arrived_b, half)
    received = (shifted(to_1, 1), shifted(to_2, 2), shifted(to_3, -1))
    keep, send = finish(place, norm_gain, block, scale_a, scale_b, arrived_a, kept_b, dots, received)
    came = swapped(send)
    result = jnp.where(core == 0, above(keep, came), above(came, keep))
    return context[None], query_grad[None], key_grad[None], value_grad[None], result


def solution(mesh):
    fine = Mesh(mesh.devices.reshape(4, 2, 2, 4, 2), AXES)
    seg, tp = ("y", "xh"), ("xl", "z", "c")
    heads = P(seg, None, tp)
    return jax.shard_map(
        local,
        mesh=fine,
        in_specs=(P(seg, tp), P(), heads, heads, heads, heads),
        out_specs=(heads, heads, heads, heads, P(seg, tp)),
        check_vma=False,
    )
```

```python
import functools

import jax
import jax.numpy as jnp
from jax import lax
from jax.experimental import pallas as pl
from jax.experimental.pallas import tpu as pltpu
from jax.sharding import Mesh
from jax.sharding import PartitionSpec as P

HD = 256
AXES = ("y", "xh", "xl", "z", "c")
PLANE = ("y", "xh", "xl")
RING = 4
EXTRA = 16
EPS = 1e-06
F32 = jnp.float32
BF16 = jnp.bfloat16
MIB = 2**20
VMEM = pl.BlockSpec(memory_space=pltpu.VMEM)
SMEM = pl.BlockSpec(memory_space=pltpu.SMEM)
ANYWHERE = pl.BlockSpec(memory_space=pl.ANY)


def dot(a, b, contract):
    return lax.dot_general(a, b, ((contract[:1], contract[1:]), ((), ())), preferred_element_type=F32)


def nn(a, b):
    return dot(a, b, (1, 0))


def nt(a, b):
    return dot(a, b, (1, 1))


def tn(a, b):
    return dot(a, b, (0, 0))


def beside(*values):
    return jnp.concatenate(values, axis=1)


def above(*values):
    return jnp.concatenate(values, axis=0)


def limits(mib):
    return pltpu.CompilerParams(vmem_limit_bytes=mib * MIB)


def cost(flops, mib, transcendentals=0):
    return pl.CostEstimate(flops=flops, bytes_accessed=int(mib * MIB), transcendentals=transcendentals)


def stage_body(*refs):
    sources, (first_ref, second_ref) = refs[:-2], refs[-2:]
    for i, source in enumerate(sources):
        first_ref[0, :, i * HD : (i + 1) * HD] = source[:HD]
        second_ref[0, :, i * HD : (i + 1) * HD] = source[HD:]


def staged(weights):
    count, blocks = len(weights), weights[0].shape[0] // (2 * HD)
    block = pl.BlockSpec((1, HD, count * HD), lambda i: (i, 0, 0))
    out = pltpu.HBM((blocks, HD, count * HD), BF16)
    return pl.pallas_call(
        stage_body,
        grid=(blocks,),
        in_specs=[pl.BlockSpec((2 * HD, HD), lambda i: (i, 0))] * count,
        out_specs=[block] * 2,
        out_shape=[out] * 2,
        compiler_params=limits(8),
        cost_estimate=cost(0, 16),
        name="stage",
    )(*[in_hbm(w) for w in weights])


def project_body(pieces, z_ref, gain_ref, *refs):
    xs = refs[: len(pieces)]
    w_refs, refs = refs[len(pieces) : len(pieces) + 2], refs[len(pieces) + 2 :]
    own_ref, sib_ref, scale_ref, normed_ref, held, rows_low, weights, x_sem, w_sem, out_sem = refs
    blocks, segs, part, width = held.shape
    rows = segs * part
    z = z_ref[0]
    copies = []
    for (distance, first, depth), x in zip(pieces, xs):
        for side in range(2):
            place = side * RING + lax.rem(z + distance, RING)
            source = x.at[:, side] if depth is None else x.at[:, side, depth]
            target = held.at[place, pl.ds(first, source.shape[0])]
            copies.append(pltpu.make_async_copy(source, target, x_sem.at[len(copies)]))
    loads = [pltpu.make_async_copy(w, weights.at[i], w_sem.at[i]) for i, w in enumerate(w_refs)]
    for copy in copies + loads:
        copy.start()
    for copy in copies:
        copy.wait()
    squares = jnp.zeros((rows, 128), F32)
    for p in range(blocks):
        wide = held[p].reshape(rows, width).astype(F32)
        wide = wide * wide
        for i in range(width // 128):
            squares += wide[:, i * 128 : (i + 1) * 128]
    scale = lax.rsqrt(jnp.sum(squares, axis=1, keepdims=True) / (blocks * width) + EPS)
    scale_ref[...] = scale
    for p in range(blocks):
        wide = held[p].reshape(rows, width).astype(F32)
        rows_low[:, p * width : (p + 1) * width] = (wide * scale * gain_ref[p]).astype(BF16)
    out = pltpu.make_async_copy(rows_low, normed_ref, out_sem)
    out.start()
    total = 0.0
    for i, load in enumerate(loads):
        load.wait()
        columns = beside(*[rows_low[:, (2 * p + i) * HD : (2 * p + i + 1) * HD] for p in range(blocks)])
        total += nn(columns, weights[i].reshape(blocks * HD, 4 * HD))
    own_ref[...] = total[:, : 2 * HD].astype(BF16)
    sib_ref[...] = total[:, 2 * HD :].astype(BF16)
    out.wait()


def project(pieces, xs, z, gain, weights, segs, name):
    part, width = xs[0].shape[-2:]
    blocks = gain.shape[0] // width
    rows = segs * part
    return pl.pallas_call(
        functools.partial(project_body, pieces),
        in_specs=[SMEM, VMEM] + [ANYWHERE] * (len(xs) + 2),
        out_specs=[VMEM, VMEM, VMEM, ANYWHERE],
        out_shape=[
            jax.ShapeDtypeStruct((rows, 2 * HD), BF16),
            jax.ShapeDtypeStruct((rows, 2 * HD), BF16),
            jax.ShapeDtypeStruct((rows, 1), F32),
            jax.ShapeDtypeStruct((rows, blocks * width), BF16),
        ],
        scratch_shapes=[
            pltpu.VMEM((blocks, segs, part, width), BF16),
            pltpu.VMEM((rows, blocks * width), BF16),
            pltpu.VMEM((2, blocks, HD, 4 * HD), BF16),
            pltpu.SemaphoreType.DMA((2 * len(xs),)),
            pltpu.SemaphoreType.DMA((2,)),
            pltpu.SemaphoreType.DMA(()),
        ],
        compiler_params=limits(24),
        cost_estimate=cost(2 * rows * blocks * width * 4 * HD, 12),
        name=name,
    )(z, gain.reshape(blocks, 1, width), *xs, *[in_hbm(w) for w in weights])


def pieces_of(dots):
    high = dots.astype(BF16).astype(F32)
    shape = (EXTRA, dots.shape[1])
    row = lax.broadcasted_iota(jnp.int32, shape, 0)
    low = jnp.broadcast_to(dots - high, shape)
    return jnp.where(row == 0, jnp.broadcast_to(high, shape), jnp.where(row == 1, low, 0.0)).astype(BF16)


def in_four_rows(dots):
    left, right = pieces_of(dots[:, :HD]).astype(F32), pieces_of(dots[:, HD:]).astype(F32)
    row = lax.broadcasted_iota(jnp.int32, left.shape, 0)
    later = jnp.where(row == 2, right[0:1], jnp.where(row == 3, right[1:2], 0.0))
    return jnp.where(row < 2, left, later).astype(BF16)


def dots_of(rows):
    return beside(rows[0:1] + rows[1:2], rows[2:3] + rows[3:4])


def attend_body(tile, q_ref, dc_ref, near_a, near_b, far_a, far_b, ctx_ref, qg_ref, gnear_ref, gfar_ref, near_dots, gkeys, gvalues):
    kv = above(near_a[...], near_b[...], far_a[...], far_b[...])
    k, v = kv[:, :HD], kv[:, HD:]
    half = kv.shape[0] // 2
    scale = HD ** (-0.5)
    row_products = jnp.zeros((8, kv.shape[0]), F32)
    for i in range(q_ref.shape[0] // tile):
        here = slice(i * tile, (i + 1) * tile)
        q, dc = q_ref[here], dc_ref[here]
        scores = nt(q, k) * scale
        expo = jnp.exp(scores - jnp.max(scores, axis=-1, keepdims=True))
        attend = expo * (1.0 / jnp.sum(expo, axis=-1, keepdims=True))
        low = attend.astype(BF16)
        ctx_ref[here] = nn(low, v).astype(BF16)
        gattend = nt(dc, v)
        dots = jnp.sum(gattend * attend, axis=-1, keepdims=True)
        gscores = attend * (gattend - dots)
        both = gscores * scores + attend * gattend
        row_products += jnp.sum(both.reshape(tile // 8, 8, kv.shape[0]), axis=0)
        gscores = (gscores * scale).astype(BF16)
        qg_ref[here] = nn(gscores, k).astype(BF16)
        if i == 0:
            gkeys[...] = tn(gscores, q)
            gvalues[...] = tn(low, dc)
        else:
            gkeys[...] += tn(gscores, q)
            gvalues[...] += tn(low, dc)
    gnear_ref[:, :HD] = gkeys[:half].astype(BF16)
    gnear_ref[:, HD:] = gvalues[:half].astype(BF16)
    gfar_ref[:half, :HD] = gkeys[half:].astype(BF16)
    gfar_ref[:half, HD:] = gvalues[half:].astype(BF16)
    row_products = jnp.sum(row_products, axis=0, keepdims=True)
    near_dots[...] = row_products[:, :half]
    gfar_ref[half:] = pieces_of(row_products[:, half:])


def attention(q, dc, near_a, near_b, far_a, far_b, tile=256):
    targets, half = q.shape[0], 2 * near_a.shape[0]
    return pl.pallas_call(
        functools.partial(attend_body, tile),
        in_specs=[VMEM] * 6,
        out_specs=[VMEM] * 5,
        out_shape=[jax.ShapeDtypeStruct((targets, HD), BF16)] * 2
        + [
            jax.ShapeDtypeStruct((half, 2 * HD), BF16),
            jax.ShapeDtypeStruct((half + EXTRA, 2 * HD), BF16),
            jax.ShapeDtypeStruct((1, half), F32),
        ],
        scratch_shapes=[pltpu.VMEM((2 * half, HD), F32)] * 2,
        compiler_params=limits(20),
        cost_estimate=cost(12 * targets * 2 * half * HD, 4, targets * 2 * half),
        name="attention",
    )(q, dc, near_a, near_b, far_a, far_b)


def feature_block(z, rows, w_ref, distance, side):
    return nt(rows, w_ref[side * RING + lax.rem(z + distance, RING)]).astype(BF16)


def back_b_body(z_ref, own_ref, sib_ref, dots_ref, w_ref, out_ref, stage, out_sem):
    half = own_ref.shape[0]
    segs = out_ref.shape[0]
    part = half // segs // 2
    rows = beside(own_ref[...], sib_ref[:half])
    outs = []
    for distance in range(RING):
        at = distance * 2 * part
        for side in range(2):
            value = feature_block(z_ref[0], rows, w_ref, distance, side).reshape(2, segs, part, HD)
            for k in range(2):
                stage[:, side, at + k * part : at + (k + 1) * part] = value[k]
        size = 2 * part
        if distance == RING - 1:
            extra = sib_ref[half:].astype(F32)
            pieces = in_four_rows(dots_ref[...] + extra[0:1] + extra[1:2])
            stage[:, :, at + size :] = jnp.broadcast_to(pieces, (segs, 2, EXTRA, HD))
            size += EXTRA
        outs.append(pltpu.make_async_copy(stage.at[:, :, pl.ds(at, size)], out_ref.at[:, :, pl.ds(at, size)], out_sem.at[distance]))
        outs[-1].start()
    for out in outs:
        out.wait()


def back_b(z, own, sib, dots, weights, segs):
    rows = own.shape[0]
    shape = (segs, 2, RING * rows // segs + EXTRA, HD)
    return pl.pallas_call(
        back_b_body,
        in_specs=[SMEM] + [VMEM] * 4,
        out_specs=ANYWHERE,
        out_shape=pltpu.HBM(shape, BF16),
        scratch_shapes=[
            pltpu.VMEM(shape, BF16),
            pltpu.SemaphoreType.DMA((RING,)),
        ],
        compiler_params=limits(16),
        cost_estimate=cost(2 * rows * 8 * HD * 4 * HD, 4),
        name="back_b",
    )(z, own, sib, dots, in_vmem(weights))


def back_a_body(z_ref, own_ref, sib_ref, w_ref, *outs):
    rows = beside(own_ref[...], sib_ref[: own_ref.shape[0]])
    segs = outs[-1].shape[0]
    part = rows.shape[0] // segs // 2
    lands = {2: ((0, 0), (1, segs // 2)), 1: ((2, 0), (3, segs // 2)), 3: ((4, 0), (5, segs // 2)), 0: ((6, 0),)}
    for distance in (2, 1, 3, 0):
        for side in range(2):
            value = feature_block(z_ref[0], rows, w_ref, distance, side).reshape(2, segs, part, HD)
            for index, first in lands[distance]:
                for k in range(2):
                    count = outs[index].shape[0]
                    outs[index][:, side, k * part : (k + 1) * part] = value[k, first : first + count]


def back_a(z, own, sib, weights, segs):
    rows = own.shape[0]
    half = jax.ShapeDtypeStruct((segs // 2, 2, rows // segs, HD), BF16)
    full = jax.ShapeDtypeStruct((segs, 2, rows // segs, HD), BF16)
    return pl.pallas_call(
        back_a_body,
        in_specs=[SMEM] + [VMEM] * 3,
        out_specs=[VMEM] * 7,
        out_shape=[half] * 6 + [full],
        compiler_params=limits(16),
        cost_estimate=cost(2 * rows * 8 * HD * 4 * HD, 4),
        name="back_a",
    )(z, own, sib, in_vmem(weights))


def weights_body(near_a, near_b, far_a, far_b, gnear_ref, gfar_ref, out_ref):
    rows = above(near_a[...], near_b[...], far_a[...], far_b[...])
    out_ref[...] = tn(rows, above(gnear_ref[...], gfar_ref[...]))


def weight_grad(normed, gnear, gfar, which, width=1024):
    rows, hidden = normed[0].shape
    block = pl.BlockSpec((rows, width), lambda i: (0, i))
    columns = pl.BlockSpec((2 * rows, HD), lambda i: (0, which))
    return pl.pallas_call(
        weights_body,
        grid=(hidden // width,),
        in_specs=[block] * 4 + [columns, columns],
        out_specs=pl.BlockSpec((width, HD), lambda i: (i, 0)),
        out_shape=jax.ShapeDtypeStruct((hidden, HD), F32),
        compiler_params=limits(24),
        cost_estimate=cost(8 * rows * hidden * HD, 13),
        name=("key_grad", "value_grad")[which],
    )(*normed, gnear, gfar)


def merge_b_body(arrived_ref, kept_ref, dots_ref, *send_refs):
    half = kept_ref.shape[0]
    total = arrived_ref[0].astype(F32)
    for i in range(1, arrived_ref.shape[0]):
        total += arrived_ref[i].astype(F32)
    kept_ref[...] = total[:half]
    both = dots_of(total[RING * half :])
    dots_ref[...] = both
    pieces = in_four_rows(both)
    for i, ref in enumerate(send_refs):
        ref[:half] = total[(i + 1) * half : (i + 2) * half].astype(BF16)
        ref[half:] = pieces


def merge_b(arrived, half):
    send = jax.ShapeDtypeStruct((half + EXTRA, HD), BF16)
    return pl.pallas_call(
        merge_b_body,
        in_specs=[VMEM],
        out_specs=[VMEM] * 5,
        out_shape=[jax.ShapeDtypeStruct((half, HD), F32), jax.ShapeDtypeStruct((1, 2 * HD), F32)] + [send] * 3,
        compiler_params=limits(16),
        cost_estimate=cost(0, 3),
        name="merge_b",
    )(arrived)


def finish_body(hidden, place_ref, gain_ref, block_ref, scale_a, scale_b, arrived_ref, kept_ref, dots_ref, r1, r2, r3,
                keep_ref, send_ref):
    core, segment, pair = place_ref[0], place_ref[1], place_ref[2]
    half = block_ref.shape[0]
    part = half // 2
    left = arrived_ref[0].astype(F32)
    for i in range(1, arrived_ref.shape[0]):
        left += arrived_ref[i].astype(F32)
    right, dots = kept_ref[...], dots_ref[...]
    for ref in (r1, r2, r3):
        right += ref[:half].astype(F32)
        dots += dots_of(ref[half:].astype(F32))
    lane = lax.broadcasted_iota(jnp.int32, (part, HD), 1)
    row = lax.broadcasted_iota(jnp.int32, (part, HD), 0)
    mine = lane == row + segment * part
    pick = lambda values: jnp.sum(jnp.where(mine, values, 0.0), axis=1, keepdims=True)
    mean = above(pick(dots[:, :HD]), pick(dots[:, HD:])) / hidden
    rows = pl.ds(pl.multiple_of(segment * part, part), part)
    scale = above(scale_a[rows], scale_b[rows])
    gain = gain_ref[pair]
    for side, total in enumerate((left, right)):
        at = slice(side * HD, (side + 1) * HD)
        value = scale * (total * gain[:, at] - block_ref[:, at].astype(F32) * scale * mean)

        @pl.when(core == side)
        def _():
            keep_ref[...] = value

        @pl.when(core != side)
        def _():
            send_ref[...] = value


def finish(place, gain, block, scale_a, scale_b, arrived, kept, dots, received):
    half, width = block.shape
    hidden = gain.shape[0]
    return pl.pallas_call(
        functools.partial(finish_body, hidden),
        in_specs=[SMEM] + [VMEM] * 10,
        out_specs=[VMEM] * 2,
        out_shape=[jax.ShapeDtypeStruct((half, HD), F32)] * 2,
        compiler_params=limits(16),
        cost_estimate=cost(0, 1),
        name="finish",
    )(place, gain.reshape(hidden // width, 1, width), block, scale_a, scale_b, arrived, kept, dots, *received)


def in_vmem(value):
    return pltpu.with_memory_space_constraint(value, pltpu.VMEM)


def in_hbm(value):
    return pltpu.with_memory_space_constraint(value, pltpu.HBM)


def swapped(value):
    return lax.ppermute(value, "c", [(0, 1), (1, 0)])


def shifted(value, by):
    return lax.ppermute(value, "z", [(i, (i + by) % RING) for i in range(RING)])


def over_plane(value):
    return lax.all_to_all(value, PLANE, 0, 0, tiled=True)


def after(values, *earlier):
    return lax.optimization_barrier((*values, *earlier))[: len(values)]


def local(memory, norm_gain, queries, key_weight, value_weight, context_grad):
    rows_own, cols_own = memory.shape
    half, width = rows_own // 2, 2 * cols_own
    part = half // 2
    core, z = lax.axis_index("c"), lax.axis_index("z")
    segment = lax.axis_index(("y", "xh"))
    pair = lax.axis_index(("xl", "z"))
    segs, plane = lax.axis_size(("y", "xh")), lax.axis_size(PLANE)
    z_array = z.astype(jnp.int32).reshape(1)
    place = jnp.stack([core, segment, pair]).astype(jnp.int32)
    wide = lambda value: value.astype(F32)

    halves = memory.reshape(2, half, cols_own)
    mine = lax.dynamic_index_in_dim(halves, core, 0, keepdims=False)
    other = swapped(lax.dynamic_index_in_dim(halves, 1 - core, 0, keepdims=False))
    block = jnp.where(core == 0, beside(mine, other), beside(other, mine))
    first_a = over_plane(jnp.broadcast_to(block[:part], (plane, part, width)))
    high = block[part:]
    near_z = jnp.stack([high, shifted(high, -1), shifted(high, 2), shifted(high, 1)])
    all_b = over_plane(jnp.broadcast_to(near_z, (plane, RING, part, width)))
    all_b = all_b.reshape(segs, 2, RING, part, width)
    low_0, high_0 = first_a[: plane // 2], first_a[plane // 2 :]
    low_3, high_1 = shifted(low_0, 1), shifted(high_0, -1)
    high_3, low_1 = shifted(high_0, 1), shifted(low_0, -1)
    low_2, high_2 = shifted(low_3, 1), shifted(high_1, -1)
    deep = lambda value: value.reshape(segs // 2, 2, part, width)

    key_own, value_own = after((key_weight[0], value_weight[0]), block)
    weights = staged((key_own, value_own, swapped(key_own), swapped(value_own)))

    top = segs // 2
    pieces_a = [(0, 0, None), (3, 0, None), (3, top, None), (1, 0, None), (1, top, None), (2, 0, None), (2, top, None)]
    xs_a = [first_a.reshape(segs, 2, part, width)] + [deep(v) for v in (low_3, high_3, low_1, high_1, low_2, high_2)]
    xs_a = [in_hbm(x) for x in xs_a]
    own_a, sib_a, scale_a, normed_a = project(pieces_a, xs_a, z_array, norm_gain, weights, segs, "project_a")
    far_a = swapped(sib_a)
    all_b, = after((all_b,), own_a)
    normed_far_a = swapped(after((normed_a,), all_b, far_a)[0])
    pieces_b = [(d, 0, d) for d in range(RING)]
    own_b, sib_b, scale_b, normed_b = project(pieces_b, [all_b] * RING, z_array, norm_gain, weights, segs, "project_b")
    far_b = swapped(sib_b)
    normed_far_b = swapped(after((normed_b,), far_b)[0])
    context, query_grad, gnear, gfar, near_dots = attention(queries[0], context_grad[0], own_a, own_b, far_a, far_b)
    gsib = swapped(gfar)

    parts_b = back_b(z_array, gnear, gsib, near_dots, weights[1], segs)
    arrived_b = over_plane(parts_b.reshape(plane, RING * half + EXTRA, HD))
    z_later, = after((z_array,), parts_b)
    opp_low, opp_high, up_low, up_high, down_low, down_high, kept = back_a(z_later, gnear, gsib, weights[0], segs)
    from_low, from_high = shifted(opp_low, 1), shifted(opp_high, -1)
    got_high, got_low = shifted(up_high, 1), shifted(down_low, -1)
    all_normed = (normed_a, normed_b, normed_far_a, normed_far_b)
    key_grad = weight_grad(all_normed, gnear, gfar, 0)
    from_low, from_high = after((from_low, from_high), key_grad)
    last_low = shifted((wide(up_low) + wide(from_low)).astype(BF16), 1)
    last_high = shifted((wide(down_high) + wide(from_high)).astype(BF16), -1)
    value_grad = weight_grad(all_normed, gnear, gfar, 1)
    got_low, got_high = after((got_low, got_high), value_grad)
    summed_low = wide(kept[: segs // 2]) + wide(got_low) + wide(last_low)
    summed_high = wide(kept[segs // 2 :]) + wide(got_high) + wide(last_high)
    summed_a = above(summed_low, summed_high).astype(BF16).reshape(plane, half, HD)

    arrived_b, summed_a = lax.optimization_barrier((arrived_b, summed_a))
    arrived_a = over_plane(summed_a)
    kept_b, dots, to_1, to_2, to_3 = merge_b(arrived_b, half)
    received = (shifted(to_1, 1), shifted(to_2, 2), shifted(to_3, -1))
    keep, send = finish(place, norm_gain, block, scale_a, scale_b, arrived_a, kept_b, dots, received)
    came = swapped(send)
    result = jnp.where(core == 0, above(keep, came), above(came, keep))
    return context[None], query_grad[None], key_grad[None], value_grad[None], result


def solution(mesh):
    fine = Mesh(mesh.devices.reshape(4, 2, 2, 4, 2), AXES)
    seg, tp = ("y", "xh"), ("xl", "z", "c")
    heads = P(seg, None, tp)
    return jax.shard_map(
        local,
        mesh=fine,
        in_specs=(P(seg, tp), P(), heads, heads, heads, heads),
        out_specs=(heads, heads, heads, heads, P(seg, tp)),
        check_vma=False,
    )
```

```python
import functools

import jax
import jax.numpy as jnp
from jax import lax
from jax.experimental import pallas as pl
from jax.experimental.pallas import tpu as pltpu
from jax.sharding import Mesh
from jax.sharding import PartitionSpec as P

HD = 256
AXES = ("y", "xh", "xl", "z", "c")
PLANE = ("y", "xh", "xl")
RING = 4
EXTRA = 16
EPS = 1e-06
F32 = jnp.float32
BF16 = jnp.bfloat16
MIB = 2**20
VMEM = pl.BlockSpec(memory_space=pltpu.VMEM)
SMEM = pl.BlockSpec(memory_space=pltpu.SMEM)
ANYWHERE = pl.BlockSpec(memory_space=pl.ANY)


def dot(a, b, contract):
    return lax.dot_general(a, b, ((contract[:1], contract[1:]), ((), ())), preferred_element_type=F32)


def nn(a, b):
    return dot(a, b, (1, 0))


def nt(a, b):
    return dot(a, b, (1, 1))


def tn(a, b):
    return dot(a, b, (0, 0))


def beside(*values):
    return jnp.concatenate(values, axis=1)


def above(*values):
    return jnp.concatenate(values, axis=0)


def limits(mib):
    return pltpu.CompilerParams(vmem_limit_bytes=mib * MIB)


def cost(flops, mib, transcendentals=0):
    return pl.CostEstimate(flops=flops, bytes_accessed=int(mib * MIB), transcendentals=transcendentals)


def project_body(pieces, z_ref, gain_ref, *refs):
    xs = refs[: len(pieces)]
    w_refs, refs = refs[len(pieces) : len(pieces) + 4], refs[len(pieces) + 4 :]
    own_ref, sib_ref, scale_ref, normed_ref, held, rows_low, weights, x_sem, w_sem, out_sem = refs
    blocks, segs, part, width = held.shape
    rows = segs * part
    z = z_ref[0]
    copies = []
    for (distance, first, depth), x in zip(pieces, xs):
        for side in range(2):
            place = side * RING + lax.rem(z + distance, RING)
            source = x.at[:, side] if depth is None else x.at[:, side, depth]
            target = held.at[place, pl.ds(first, source.shape[0])]
            copies.append(pltpu.make_async_copy(source, target, x_sem.at[len(copies)]))
    loads = [pltpu.make_async_copy(w, weights.at[i], w_sem.at[i]) for i, w in enumerate(w_refs)]
    for copy in copies + loads:
        copy.start()
    for copy in copies:
        copy.wait()
    squares = jnp.zeros((rows, 128), F32)
    for p in range(blocks):
        wide = held[p].reshape(rows, width).astype(F32)
        wide = wide * wide
        for i in range(width // 128):
            squares += wide[:, i * 128 : (i + 1) * 128]
    scale = lax.rsqrt(jnp.sum(squares, axis=1, keepdims=True) / (blocks * width) + EPS)
    scale_ref[...] = scale
    for p in range(blocks):
        wide = held[p].reshape(rows, width).astype(F32)
        rows_low[:, p * width : (p + 1) * width] = (wide * scale * gain_ref[p]).astype(BF16)
    out = pltpu.make_async_copy(rows_low, normed_ref, out_sem)
    out.start()
    for i, load in enumerate(loads):
        load.wait()
        out_ref, at = (own_ref, sib_ref)[i // 2], (i % 2) * HD
        out_ref[:, at : at + HD] = nn(rows_low[...], weights[i]).astype(BF16)
    out.wait()


def project(pieces, xs, z, gain, weights, segs, name):
    part, width = xs[0].shape[-2:]
    blocks = gain.shape[0] // width
    rows = segs * part
    return pl.pallas_call(
        functools.partial(project_body, pieces),
        in_specs=[SMEM, VMEM] + [ANYWHERE] * (len(xs) + 4),
        out_specs=[VMEM, VMEM, VMEM, ANYWHERE],
        out_shape=[
            jax.ShapeDtypeStruct((rows, 2 * HD), BF16),
            jax.ShapeDtypeStruct((rows, 2 * HD), BF16),
            jax.ShapeDtypeStruct((rows, 1), F32),
            jax.ShapeDtypeStruct((rows, blocks * width), BF16),
        ],
        scratch_shapes=[
            pltpu.VMEM((blocks, segs, part, width), BF16),
            pltpu.VMEM((rows, blocks * width), BF16),
            pltpu.VMEM((4, blocks * width, HD), BF16),
            pltpu.SemaphoreType.DMA((2 * len(xs),)),
            pltpu.SemaphoreType.DMA((4,)),
            pltpu.SemaphoreType.DMA(()),
        ],
        compiler_params=limits(24),
        cost_estimate=cost(2 * rows * blocks * width * 4 * HD, 12),
        name=name,
    )(z, gain.reshape(blocks, 1, width), *xs, *[in_hbm(w) for w in weights])


def pieces_of(dots):
    high = dots.astype(BF16).astype(F32)
    shape = (EXTRA, dots.shape[1])
    row = lax.broadcasted_iota(jnp.int32, shape, 0)
    low = jnp.broadcast_to(dots - high, shape)
    return jnp.where(row == 0, jnp.broadcast_to(high, shape), jnp.where(row == 1, low, 0.0)).astype(BF16)


def in_four_rows(dots):
    left, right = pieces_of(dots[:, :HD]).astype(F32), pieces_of(dots[:, HD:]).astype(F32)
    row = lax.broadcasted_iota(jnp.int32, left.shape, 0)
    later = jnp.where(row == 2, right[0:1], jnp.where(row == 3, right[1:2], 0.0))
    return jnp.where(row < 2, left, later).astype(BF16)


def dots_of(rows):
    return beside(rows[0:1] + rows[1:2], rows[2:3] + rows[3:4])


def attend_body(tile, q_ref, dc_ref, near_a, near_b, far_a, far_b, ctx_ref, qg_ref, gnear_ref, gfar_ref, near_dots, gkeys, gvalues):
    kv = above(near_a[...], near_b[...], far_a[...], far_b[...])
    k, v = kv[:, :HD], kv[:, HD:]
    half = kv.shape[0] // 2
    scale = HD ** (-0.5)
    row_products = jnp.zeros((8, kv.shape[0]), F32)
    for i in range(q_ref.shape[0] // tile):
        here = slice(i * tile, (i + 1) * tile)
        q, dc = q_ref[here], dc_ref[here]
        scores = nt(q, k) * scale
        expo = jnp.exp(scores - jnp.max(scores, axis=-1, keepdims=True))
        attend = expo * (1.0 / jnp.sum(expo, axis=-1, keepdims=True))
        low = attend.astype(BF16)
        ctx_ref[here] = nn(low, v).astype(BF16)
        gattend = nt(dc, v)
        dots = jnp.sum(gattend * attend, axis=-1, keepdims=True)
        gscores = attend * (gattend - dots)
        both = gscores * scores + attend * gattend
        row_products += jnp.sum(both.reshape(tile // 8, 8, kv.shape[0]), axis=0)
        gscores = (gscores * scale).astype(BF16)
        qg_ref[here] = nn(gscores, k).astype(BF16)
        if i == 0:
            gkeys[...] = tn(gscores, q)
            gvalues[...] = tn(low, dc)
        else:
            gkeys[...] += tn(gscores, q)
            gvalues[...] += tn(low, dc)
    gnear_ref[:, :HD] = gkeys[:half].astype(BF16)
    gnear_ref[:, HD:] = gvalues[:half].astype(BF16)
    gfar_ref[:half, :HD] = gkeys[half:].astype(BF16)
    gfar_ref[:half, HD:] = gvalues[half:].astype(BF16)
    row_products = jnp.sum(row_products, axis=0, keepdims=True)
    near_dots[...] = row_products[:, :half]
    gfar_ref[half:] = pieces_of(row_products[:, half:])


def attention(q, dc, near_a, near_b, far_a, far_b, tile=256):
    targets, half = q.shape[0], 2 * near_a.shape[0]
    return pl.pallas_call(
        functools.partial(attend_body, tile),
        in_specs=[VMEM] * 6,
        out_specs=[VMEM] * 5,
        out_shape=[jax.ShapeDtypeStruct((targets, HD), BF16)] * 2
        + [
            jax.ShapeDtypeStruct((half, 2 * HD), BF16),
            jax.ShapeDtypeStruct((half + EXTRA, 2 * HD), BF16),
            jax.ShapeDtypeStruct((1, half), F32),
        ],
        scratch_shapes=[pltpu.VMEM((2 * half, HD), F32)] * 2,
        compiler_params=limits(20),
        cost_estimate=cost(12 * targets * 2 * half * HD, 4, targets * 2 * half),
        name="attention",
    )(q, dc, near_a, near_b, far_a, far_b)


def feature_block(z, rows, weights, feature_half, distance, side):
    block = side * RING + lax.rem(z + distance, RING)
    at = pl.ds(pl.multiple_of((2 * block + feature_half) * HD, HD), HD)
    return nt(rows, beside(*[w[at, :] for w in weights])).astype(BF16)


def back_b_body(z_ref, own_ref, sib_ref, dots_ref, ko, vo, ks, vs, out_ref, stage, out_sem):
    z, core = z_ref[0], z_ref[1]
    half = own_ref.shape[0]
    segs = out_ref.shape[0]
    part = half // segs // 2
    rows = beside(own_ref[...], sib_ref[:half])
    outs = []
    for distance in range(RING):
        at = distance * 2 * part
        for side in range(2):
            value = feature_block(z, rows, (ko, vo, ks, vs), 1 - core, distance, side).reshape(2, segs, part, HD)
            for k in range(2):
                stage[:, side, at + k * part : at + (k + 1) * part] = value[k]
        size = 2 * part
        if distance == RING - 1:
            extra = sib_ref[half:].astype(F32)
            pieces = in_four_rows(dots_ref[...] + extra[0:1] + extra[1:2])
            stage[:, :, at + size :] = jnp.broadcast_to(pieces, (segs, 2, EXTRA, HD))
            size += EXTRA
        outs.append(pltpu.make_async_copy(stage.at[:, :, pl.ds(at, size)], out_ref.at[:, :, pl.ds(at, size)], out_sem.at[distance]))
        outs[-1].start()
    for out in outs:
        out.wait()


def back_b(z, own, sib, dots, weights, segs):
    rows = own.shape[0]
    shape = (segs, 2, RING * rows // segs + EXTRA, HD)
    return pl.pallas_call(
        back_b_body,
        in_specs=[SMEM] + [VMEM] * 7,
        out_specs=ANYWHERE,
        out_shape=pltpu.HBM(shape, BF16),
        scratch_shapes=[
            pltpu.VMEM(shape, BF16),
            pltpu.SemaphoreType.DMA((RING,)),
        ],
        compiler_params=limits(16),
        cost_estimate=cost(2 * rows * 8 * HD * 4 * HD, 4),
        name="back_b",
    )(z, own, sib, dots, *[in_vmem(w) for w in weights])


def back_a_body(z_ref, own_ref, sib_ref, ko, vo, ks, vs, *outs):
    z, core = z_ref[0], z_ref[1]
    rows = beside(own_ref[...], sib_ref[: own_ref.shape[0]])
    segs = outs[-1].shape[0]
    part = rows.shape[0] // segs // 2
    lands = {2: ((0, 0), (1, segs // 2)), 1: ((2, 0), (3, segs // 2)), 3: ((4, 0), (5, segs // 2)), 0: ((6, 0),)}
    for distance in (2, 1, 3, 0):
        for side in range(2):
            value = feature_block(z, rows, (ko, vo, ks, vs), core, distance, side).reshape(2, segs, part, HD)
            for index, first in lands[distance]:
                for k in range(2):
                    count = outs[index].shape[0]
                    outs[index][:, side, k * part : (k + 1) * part] = value[k, first : first + count]


def back_a(z, own, sib, weights, segs):
    rows = own.shape[0]
    half = jax.ShapeDtypeStruct((segs // 2, 2, rows // segs, HD), BF16)
    full = jax.ShapeDtypeStruct((segs, 2, rows // segs, HD), BF16)
    return pl.pallas_call(
        back_a_body,
        in_specs=[SMEM] + [VMEM] * 6,
        out_specs=[VMEM] * 7,
        out_shape=[half] * 6 + [full],
        compiler_params=limits(16),
        cost_estimate=cost(2 * rows * 8 * HD * 4 * HD, 4),
        name="back_a",
    )(z, own, sib, *[in_vmem(w) for w in weights])


def weights_body(near_a, near_b, far_a, far_b, gnear_ref, gfar_ref, out_ref):
    rows = above(near_a[...], near_b[...], far_a[...], far_b[...])
    out_ref[...] = tn(rows, above(gnear_ref[...], gfar_ref[...]))


def weight_grad(normed, gnear, gfar, which, width=1024):
    rows, hidden = normed[0].shape
    block = pl.BlockSpec((rows, width), lambda i: (0, i))
    columns = pl.BlockSpec((2 * rows, HD), lambda i: (0, which))
    return pl.pallas_call(
        weights_body,
        grid=(hidden // width,),
        in_specs=[block] * 4 + [columns, columns],
        out_specs=pl.BlockSpec((width, HD), lambda i: (i, 0)),
        out_shape=jax.ShapeDtypeStruct((hidden, HD), F32),
        compiler_params=limits(24),
        cost_estimate=cost(8 * rows * hidden * HD, 13),
        name=("key_grad", "value_grad")[which],
    )(*normed, gnear, gfar)


def merge_b_body(arrived_ref, kept_ref, dots_ref, *send_refs):
    half = kept_ref.shape[0]
    total = arrived_ref[0].astype(F32)
    for i in range(1, arrived_ref.shape[0]):
        total += arrived_ref[i].astype(F32)
    kept_ref[...] = total[:half]
    both = dots_of(total[RING * half :])
    dots_ref[...] = both
    pieces = in_four_rows(both)
    for i, ref in enumerate(send_refs):
        ref[:half] = total[(i + 1) * half : (i + 2) * half].astype(BF16)
        ref[half:] = pieces


def merge_b(arrived, half):
    send = jax.ShapeDtypeStruct((half + EXTRA, HD), BF16)
    return pl.pallas_call(
        merge_b_body,
        in_specs=[VMEM],
        out_specs=[VMEM] * 5,
        out_shape=[jax.ShapeDtypeStruct((half, HD), F32), jax.ShapeDtypeStruct((1, 2 * HD), F32)] + [send] * 3,
        compiler_params=limits(16),
        cost_estimate=cost(0, 3),
        name="merge_b",
    )(arrived)


def finish_b_body(hidden, place_ref, gain_ref, block_ref, scale_a, scale_b, kept_ref, dots_ref, r1, r2, r3,
                  out_ref, scale_ref, mean_ref):
    core, segment, pair = place_ref[0], place_ref[1], place_ref[2]
    half = block_ref.shape[0]
    part = half // 2
    total, dots = kept_ref[...], dots_ref[...]
    for ref in (r1, r2, r3):
        total += ref[:half].astype(F32)
        dots += dots_of(ref[half:].astype(F32))
    lane = lax.broadcasted_iota(jnp.int32, (part, HD), 1)
    row = lax.broadcasted_iota(jnp.int32, (part, HD), 0)
    mine = lane == row + segment * part
    pick = lambda values: jnp.sum(jnp.where(mine, values, 0.0), axis=1, keepdims=True)
    mean = above(pick(dots[:, :HD]), pick(dots[:, HD:])) / hidden
    rows = pl.ds(pl.multiple_of(segment * part, part), part)
    scale = above(scale_a[rows], scale_b[rows])
    out_ref[...] = finished(core == 1, total, gain_ref[pair], block_ref[...], scale, mean)
    scale_ref[...] = scale
    mean_ref[...] = mean


def finished(first, total, gain, block, scale, mean):
    gain = jnp.where(first, gain[:, :HD], gain[:, HD:])
    centered = jnp.where(first, block[:, :HD].astype(F32), block[:, HD:].astype(F32)) * scale
    return scale * (total * gain - centered * mean)


def finish_b(place, gain, block, scale_a, scale_b, kept, dots, received):
    half, width = block.shape
    hidden = gain.shape[0]
    column = jax.ShapeDtypeStruct((half, 1), F32)
    return pl.pallas_call(
        functools.partial(finish_b_body, hidden),
        in_specs=[SMEM] + [VMEM] * 9,
        out_specs=[VMEM] * 3,
        out_shape=[jax.ShapeDtypeStruct((half, HD), F32), column, column],
        compiler_params=limits(16),
        cost_estimate=cost(0, 1),
        name="finish_b",
    )(place, gain.reshape(hidden // width, 1, width), block, scale_a, scale_b, kept, dots, *received)


def finish_a_body(place_ref, gain_ref, block_ref, scale_ref, mean_ref, came_ref, arrived_ref, out_ref):
    core, pair = place_ref[0], place_ref[2]
    half = block_ref.shape[0]
    total = arrived_ref[0].astype(F32)
    for i in range(1, arrived_ref.shape[0]):
        total += arrived_ref[i].astype(F32)
    kept = finished(core == 0, total, gain_ref[pair], block_ref[...], scale_ref[...], mean_ref[...])
    out_ref[pl.ds(pl.multiple_of(core * half, half), half)] = kept
    out_ref[pl.ds(pl.multiple_of((1 - core) * half, half), half)] = came_ref[...]


def finish_a(place, gain, block, scale, mean, came, arrived):
    half, width = block.shape
    hidden = gain.shape[0]
    return pl.pallas_call(
        finish_a_body,
        in_specs=[SMEM] + [VMEM] * 6,
        out_specs=VMEM,
        out_shape=jax.ShapeDtypeStruct((2 * half, HD), F32),
        compiler_params=limits(16),
        cost_estimate=cost(0, 1),
        name="finish_a",
    )(place, gain.reshape(hidden // width, 1, width), block, scale, mean, came, arrived)


def in_vmem(value):
    return pltpu.with_memory_space_constraint(value, pltpu.VMEM)


def in_hbm(value):
    return pltpu.with_memory_space_constraint(value, pltpu.HBM)


def swapped(value):
    return lax.ppermute(value, "c", [(0, 1), (1, 0)])


def shifted(value, by):
    return lax.ppermute(value, "z", [(i, (i + by) % RING) for i in range(RING)])


def over_plane(value):
    return lax.all_to_all(value, PLANE, 0, 0, tiled=True)


def after(values, *earlier):
    return lax.optimization_barrier((*values, *earlier))[: len(values)]


def local(memory, norm_gain, queries, key_weight, value_weight, context_grad):
    rows_own, cols_own = memory.shape
    half, width = rows_own // 2, 2 * cols_own
    part = half // 2
    core, z = lax.axis_index("c"), lax.axis_index("z")
    segment = lax.axis_index(("y", "xh"))
    pair = lax.axis_index(("xl", "z"))
    segs, plane = lax.axis_size(("y", "xh")), lax.axis_size(PLANE)
    z_array = jnp.stack([z, core]).astype(jnp.int32)
    place = jnp.stack([core, segment, pair]).astype(jnp.int32)
    wide = lambda value: value.astype(F32)

    halves = memory.reshape(2, half, cols_own)
    mine = lax.dynamic_index_in_dim(halves, core, 0, keepdims=False)
    other = swapped(lax.dynamic_index_in_dim(halves, 1 - core, 0, keepdims=False))
    block = jnp.where(core == 0, beside(mine, other), beside(other, mine))
    first_a = over_plane(jnp.broadcast_to(block[:part], (plane, part, width)))
    high = block[part:]
    near_z = jnp.stack([high, shifted(high, -1), shifted(high, 2), shifted(high, 1)])
    all_b = over_plane(jnp.broadcast_to(near_z, (plane, RING, part, width)))
    all_b = all_b.reshape(segs, 2, RING, part, width)
    low_0, high_0 = first_a[: plane // 2], first_a[plane // 2 :]
    low_3, high_1 = shifted(low_0, 1), shifted(high_0, -1)
    high_3, low_1 = shifted(high_0, 1), shifted(low_0, -1)
    low_2, high_2 = shifted(low_3, 1), shifted(high_1, -1)
    deep = lambda value: value.reshape(segs // 2, 2, part, width)

    key_own, value_own = after((key_weight[0], value_weight[0]), block)
    weights = (key_own, value_own, swapped(key_own), swapped(value_own))

    top = segs // 2
    pieces_a = [(0, 0, None), (3, 0, None), (3, top, None), (1, 0, None), (1, top, None), (2, 0, None), (2, top, None)]
    xs_a = [first_a.reshape(segs, 2, part, width)] + [deep(v) for v in (low_3, high_3, low_1, high_1, low_2, high_2)]
    xs_a = [in_hbm(x) for x in xs_a]
    own_a, sib_a, scale_a, normed_a = project(pieces_a, xs_a, z_array, norm_gain, weights, segs, "project_a")
    far_a = swapped(sib_a)
    all_b, = after((all_b,), own_a)
    normed_far_a = swapped(after((normed_a,), all_b, far_a)[0])
    pieces_b = [(d, 0, d) for d in range(RING)]
    own_b, sib_b, scale_b, normed_b = project(pieces_b, [all_b] * RING, z_array, norm_gain, weights, segs, "project_b")
    far_b = swapped(sib_b)
    normed_far_b = swapped(after((normed_b,), far_b)[0])
    context, query_grad, gnear, gfar, near_dots = attention(queries[0], context_grad[0], own_a, own_b, far_a, far_b)
    gsib = swapped(gfar)

    parts_b = back_b(z_array, gnear, gsib, near_dots, weights, segs)
    arrived_b = over_plane(parts_b.reshape(plane, RING * half + EXTRA, HD))
    z_later, = after((z_array,), parts_b)
    opp_low, opp_high, up_low, up_high, down_low, down_high, kept = back_a(z_later, gnear, gsib, weights, segs)
    from_low, from_high = shifted(opp_low, 1), shifted(opp_high, -1)
    got_high, got_low = shifted(up_high, 1), shifted(down_low, -1)
    all_normed = (normed_a, normed_b, normed_far_a, normed_far_b)
    key_grad = weight_grad(all_normed, gnear, gfar, 0)
    from_low, from_high = after((from_low, from_high), key_grad)
    last_low = shifted((wide(up_low) + wide(from_low)).astype(BF16), 1)
    last_high = shifted((wide(down_high) + wide(from_high)).astype(BF16), -1)
    value_grad = weight_grad(all_normed, gnear, gfar, 1)
    got_low, got_high = after((got_low, got_high), value_grad)
    summed_low = wide(kept[: segs // 2]) + wide(got_low) + wide(last_low)
    summed_high = wide(kept[segs // 2 :]) + wide(got_high) + wide(last_high)
    summed_a = above(summed_low, summed_high).astype(BF16).reshape(plane, half, HD)

    arrived_b, summed_a = lax.optimization_barrier((arrived_b, summed_a))
    arrived_a = over_plane(summed_a)
    kept_b, dots, to_1, to_2, to_3 = merge_b(arrived_b, half)
    received = (shifted(to_1, 1), shifted(to_2, 2), shifted(to_3, -1))
    value_b, own_scale, mean = finish_b(place, norm_gain, block, scale_a, scale_b, kept_b, dots, received)
    result = finish_a(place, norm_gain, block, own_scale, mean, swapped(value_b), arrived_a)
    return context[None], query_grad[None], key_grad[None], value_grad[None], result


def solution(mesh):
    fine = Mesh(mesh.devices.reshape(4, 2, 2, 4, 2), AXES)
    seg, tp = ("y", "xh"), ("xl", "z", "c")
    heads = P(seg, None, tp)
    return jax.shard_map(
        local,
        mesh=fine,
        in_specs=(P(seg, tp), P(), heads, heads, heads, heads),
        out_specs=(heads, heads, heads, heads, P(seg, tp)),
        check_vma=False,
    )
```

```python
import functools

import jax
import jax.numpy as jnp
from jax import lax
from jax.experimental import pallas as pl
from jax.experimental.pallas import tpu as pltpu
from jax.sharding import Mesh
from jax.sharding import PartitionSpec as P

HD = 256
AXES = ("y", "xh", "xl", "z", "c")
PLANE = ("y", "xh", "xl")
RING = 4
EXTRA = 16
EPS = 1e-06
F32 = jnp.float32
BF16 = jnp.bfloat16
MIB = 2**20
VMEM = pl.BlockSpec(memory_space=pltpu.VMEM)
SMEM = pl.BlockSpec(memory_space=pltpu.SMEM)
ANYWHERE = pl.BlockSpec(memory_space=pl.ANY)


def dot(a, b, contract):
    return lax.dot_general(a, b, ((contract[:1], contract[1:]), ((), ())), preferred_element_type=F32)


def nn(a, b):
    return dot(a, b, (1, 0))


def nt(a, b):
    return dot(a, b, (1, 1))


def tn(a, b):
    return dot(a, b, (0, 0))


def beside(*values):
    return jnp.concatenate(values, axis=1)


def above(*values):
    return jnp.concatenate(values, axis=0)


def limits(mib):
    return pltpu.CompilerParams(vmem_limit_bytes=mib * MIB)


def cost(flops, mib, transcendentals=0):
    return pl.CostEstimate(flops=flops, bytes_accessed=int(mib * MIB), transcendentals=transcendentals)


def copies_body(count, *refs):
    pieces, out_ref, held, sem = refs[:-3], refs[-3], refs[-2], refs[-1]
    for i, piece in enumerate(pieces):
        held[i] = piece[...]
    copies = [pltpu.make_async_copy(held, out_ref.at[j], sem.at[j]) for j in range(count)]
    for copy in copies:
        copy.start()
    for copy in copies:
        copy.wait()


def copies_of(pieces, count, name):
    shape = (len(pieces), *pieces[0].shape)
    return pl.pallas_call(
        functools.partial(copies_body, count),
        in_specs=[VMEM] * len(pieces),
        out_specs=ANYWHERE,
        out_shape=pltpu.HBM((count, *shape), BF16),
        scratch_shapes=[pltpu.VMEM(shape, BF16), pltpu.SemaphoreType.DMA((count,))],
        compiler_params=limits(4),
        cost_estimate=cost(0, 2),
        name=name,
    )(*pieces)


def stage_body(place_ref, *refs):
    sources, outs = refs[:-2], refs[-2:]
    for j, out in enumerate(outs):
        half = place_ref[1] if j == 0 else 1 - place_ref[1]
        at = pl.ds(pl.multiple_of(half * HD, HD), HD)
        for i, source in enumerate(sources):
            out[0, :, i * HD : (i + 1) * HD] = source[at, :]


def staged(place, weights):
    count, blocks = len(weights), weights[0].shape[0] // (2 * HD)
    block = pl.BlockSpec((1, HD, count * HD), lambda i: (i, 0, 0))
    out = pltpu.HBM((blocks, HD, count * HD), BF16)
    return pl.pallas_call(
        stage_body,
        grid=(blocks,),
        in_specs=[SMEM] + [pl.BlockSpec((2 * HD, HD), lambda i: (i, 0))] * count,
        out_specs=[block] * 2,
        out_shape=[out] * 2,
        compiler_params=limits(8),
        cost_estimate=cost(0, 16),
        name="stage",
    )(place, *[in_hbm(w) for w in weights])


def project_body(pieces, z_ref, gain_ref, *refs):
    xs = refs[: len(pieces)]
    w_refs, refs = refs[len(pieces) : len(pieces) + 2], refs[len(pieces) + 2 :]
    own_ref, sib_ref, scale_ref, normed_ref, held, rows_low, weights, x_sem, w_sem, out_sem = refs
    blocks, segs, part, width = held.shape
    rows = segs * part
    z = z_ref[0]
    copies = []
    for (distance, first, depth), x in zip(pieces, xs):
        for side in range(2):
            place = side * RING + lax.rem(z + distance, RING)
            source = x.at[:, side] if depth is None else x.at[:, side, depth]
            target = held.at[place, pl.ds(first, source.shape[0])]
            copies.append(pltpu.make_async_copy(source, target, x_sem.at[len(copies)]))
    loads = [pltpu.make_async_copy(w, weights.at[i], w_sem.at[i]) for i, w in enumerate(w_refs)]
    for copy in copies + loads:
        copy.start()
    for copy in copies:
        copy.wait()
    squares = jnp.zeros((rows, 128), F32)
    for p in range(blocks):
        wide = held[p].reshape(rows, width).astype(F32)
        wide = wide * wide
        for i in range(width // 128):
            squares += wide[:, i * 128 : (i + 1) * 128]
    scale = lax.rsqrt(jnp.sum(squares, axis=1, keepdims=True) / (blocks * width) + EPS)
    scale_ref[...] = scale
    for p in range(blocks):
        wide = held[p].reshape(rows, width).astype(F32)
        rows_low[:, p * width : (p + 1) * width] = (wide * scale * gain_ref[p]).astype(BF16)
    out = pltpu.make_async_copy(rows_low, normed_ref, out_sem)
    out.start()
    total = 0.0
    for i, load in enumerate(loads):
        load.wait()
        first = z_ref[1] if i == 0 else 1 - z_ref[1]
        columns = beside(*[rows_low[:, pl.ds(pl.multiple_of((2 * p + first) * HD, HD), HD)] for p in range(blocks)])
        total += nn(columns, weights[i].reshape(blocks * HD, 4 * HD))
    own_ref[...] = total[:, : 2 * HD].astype(BF16)
    sib_ref[...] = total[:, 2 * HD :].astype(BF16)
    out.wait()


def project(pieces, xs, z, gain, weights, segs, name):
    part, width = xs[0].shape[-2:]
    blocks = gain.shape[0] // width
    rows = segs * part
    return pl.pallas_call(
        functools.partial(project_body, pieces),
        in_specs=[SMEM, VMEM] + [ANYWHERE] * (len(xs) + 2),
        out_specs=[VMEM, VMEM, VMEM, ANYWHERE],
        out_shape=[
            jax.ShapeDtypeStruct((rows, 2 * HD), BF16),
            jax.ShapeDtypeStruct((rows, 2 * HD), BF16),
            jax.ShapeDtypeStruct((rows, 1), F32),
            jax.ShapeDtypeStruct((rows, blocks * width), BF16),
        ],
        scratch_shapes=[
            pltpu.VMEM((blocks, segs, part, width), BF16),
            pltpu.VMEM((rows, blocks * width), BF16),
            pltpu.VMEM((2, blocks, HD, 4 * HD), BF16),
            pltpu.SemaphoreType.DMA((2 * len(xs),)),
            pltpu.SemaphoreType.DMA((2,)),
            pltpu.SemaphoreType.DMA(()),
        ],
        compiler_params=limits(24),
        cost_estimate=cost(2 * rows * blocks * width * 4 * HD, 12),
        name=name,
    )(z, gain.reshape(blocks, 1, width), *xs, *[in_hbm(w) for w in weights])


def pieces_of(dots):
    high = dots.astype(BF16).astype(F32)
    shape = (EXTRA, dots.shape[1])
    row = lax.broadcasted_iota(jnp.int32, shape, 0)
    low = jnp.broadcast_to(dots - high, shape)
    return jnp.where(row == 0, jnp.broadcast_to(high, shape), jnp.where(row == 1, low, 0.0)).astype(BF16)


def in_four_rows(dots):
    left, right = pieces_of(dots[:, :HD]).astype(F32), pieces_of(dots[:, HD:]).astype(F32)
    row = lax.broadcasted_iota(jnp.int32, left.shape, 0)
    later = jnp.where(row == 2, right[0:1], jnp.where(row == 3, right[1:2], 0.0))
    return jnp.where(row < 2, left, later).astype(BF16)


def dots_of(rows):
    return beside(rows[0:1] + rows[1:2], rows[2:3] + rows[3:4])


def attend_body(tile, q_ref, dc_ref, near_a, near_b, far_a, far_b, ctx_ref, qg_ref, gnear_ref, gfar_ref, near_dots, gkeys, gvalues):
    kv = above(near_a[...], near_b[...], far_a[...], far_b[...])
    k, v = kv[:, :HD], kv[:, HD:]
    half = kv.shape[0] // 2
    scale = HD ** (-0.5)
    row_products = jnp.zeros((8, kv.shape[0]), F32)
    for i in range(q_ref.shape[0] // tile):
        here = slice(i * tile, (i + 1) * tile)
        q, dc = q_ref[here], dc_ref[here]
        scores = nt(q, k) * scale
        expo = jnp.exp(scores - jnp.max(scores, axis=-1, keepdims=True))
        attend = expo * (1.0 / jnp.sum(expo, axis=-1, keepdims=True))
        low = attend.astype(BF16)
        ctx_ref[here] = nn(low, v).astype(BF16)
        gattend = nt(dc, v)
        dots = jnp.sum(gattend * attend, axis=-1, keepdims=True)
        gscores = attend * (gattend - dots)
        both = gscores * scores + attend * gattend
        row_products += jnp.sum(both.reshape(tile // 8, 8, kv.shape[0]), axis=0)
        gscores = (gscores * scale).astype(BF16)
        qg_ref[here] = nn(gscores, k).astype(BF16)
        if i == 0:
            gkeys[...] = tn(gscores, q)
            gvalues[...] = tn(low, dc)
        else:
            gkeys[...] += tn(gscores, q)
            gvalues[...] += tn(low, dc)
    gnear_ref[:, :HD] = gkeys[:half].astype(BF16)
    gnear_ref[:, HD:] = gvalues[:half].astype(BF16)
    gfar_ref[:half, :HD] = gkeys[half:].astype(BF16)
    gfar_ref[:half, HD:] = gvalues[half:].astype(BF16)
    row_products = jnp.sum(row_products, axis=0, keepdims=True)
    near_dots[...] = row_products[:, :half]
    gfar_ref[half:] = pieces_of(row_products[:, half:])


def attention(q, dc, near_a, near_b, far_a, far_b, tile=256):
    targets, half = q.shape[0], 2 * near_a.shape[0]
    return pl.pallas_call(
        functools.partial(attend_body, tile),
        in_specs=[VMEM] * 6,
        out_specs=[VMEM] * 5,
        out_shape=[jax.ShapeDtypeStruct((targets, HD), BF16)] * 2
        + [
            jax.ShapeDtypeStruct((half, 2 * HD), BF16),
            jax.ShapeDtypeStruct((half + EXTRA, 2 * HD), BF16),
            jax.ShapeDtypeStruct((1, half), F32),
        ],
        scratch_shapes=[pltpu.VMEM((2 * half, HD), F32)] * 2,
        compiler_params=limits(20),
        cost_estimate=cost(12 * targets * 2 * half * HD, 4, targets * 2 * half),
        name="attention",
    )(q, dc, near_a, near_b, far_a, far_b)


def feature_block(z, rows, w_ref, distance, side):
    return nt(rows, w_ref[side * RING + lax.rem(z + distance, RING)]).astype(BF16)


def back_b_body(z_ref, own_ref, sib_ref, dots_ref, w_ref, out_ref, stage, out_sem):
    half = own_ref.shape[0]
    segs = out_ref.shape[0]
    part = half // segs // 2
    rows = beside(own_ref[...], sib_ref[:half])
    outs = []
    for distance in range(RING):
        at = distance * 2 * part
        for side in range(2):
            value = feature_block(z_ref[0], rows, w_ref, distance, side).reshape(2, segs, part, HD)
            for k in range(2):
                stage[:, side, at + k * part : at + (k + 1) * part] = value[k]
        size = 2 * part
        if distance == RING - 1:
            extra = sib_ref[half:].astype(F32)
            pieces = in_four_rows(dots_ref[...] + extra[0:1] + extra[1:2])
            stage[:, :, at + size :] = jnp.broadcast_to(pieces, (segs, 2, EXTRA, HD))
            size += EXTRA
        outs.append(pltpu.make_async_copy(stage.at[:, :, pl.ds(at, size)], out_ref.at[:, :, pl.ds(at, size)], out_sem.at[distance]))
        outs[-1].start()
    for out in outs:
        out.wait()


def back_b(z, own, sib, dots, weights, segs):
    rows = own.shape[0]
    shape = (segs, 2, RING * rows // segs + EXTRA, HD)
    return pl.pallas_call(
        back_b_body,
        in_specs=[SMEM] + [VMEM] * 4,
        out_specs=ANYWHERE,
        out_shape=pltpu.HBM(shape, BF16),
        scratch_shapes=[
            pltpu.VMEM(shape, BF16),
            pltpu.SemaphoreType.DMA((RING,)),
        ],
        compiler_params=limits(16),
        cost_estimate=cost(2 * rows * 8 * HD * 4 * HD, 4),
        name="back_b",
    )(z, own, sib, dots, in_vmem(weights))


def back_a_body(z_ref, own_ref, sib_ref, w_ref, *outs):
    rows = beside(own_ref[...], sib_ref[: own_ref.shape[0]])
    segs = outs[-1].shape[0]
    part = rows.shape[0] // segs // 2
    lands = {2: ((0, 0), (1, segs // 2)), 1: ((2, 0), (3, segs // 2)), 3: ((4, 0), (5, segs // 2)), 0: ((6, 0),)}
    for distance in (2, 1, 3, 0):
        for side in range(2):
            value = feature_block(z_ref[0], rows, w_ref, distance, side).reshape(2, segs, part, HD)
            for index, first in lands[distance]:
                for k in range(2):
                    count = outs[index].shape[0]
                    outs[index][:, side, k * part : (k + 1) * part] = value[k, first : first + count]


def back_a(z, own, sib, weights, segs):
    rows = own.shape[0]
    half = jax.ShapeDtypeStruct((segs // 2, 2, rows // segs, HD), BF16)
    full = jax.ShapeDtypeStruct((segs, 2, rows // segs, HD), BF16)
    return pl.pallas_call(
        back_a_body,
        in_specs=[SMEM] + [VMEM] * 3,
        out_specs=[VMEM] * 7,
        out_shape=[half] * 6 + [full],
        compiler_params=limits(16),
        cost_estimate=cost(2 * rows * 8 * HD * 4 * HD, 4),
        name="back_a",
    )(z, own, sib, in_vmem(weights))


def weights_body(near_a, near_b, far_a, far_b, gnear_ref, gfar_ref, out_ref):
    rows = above(near_a[...], near_b[...], far_a[...], far_b[...])
    out_ref[...] = tn(rows, above(gnear_ref[...], gfar_ref[...]))


def weight_grad(normed, gnear, gfar, which, width=1024):
    rows, hidden = normed[0].shape
    block = pl.BlockSpec((rows, width), lambda i: (0, i))
    columns = pl.BlockSpec((2 * rows, HD), lambda i: (0, which))
    return pl.pallas_call(
        weights_body,
        grid=(hidden // width,),
        in_specs=[block] * 4 + [columns, columns],
        out_specs=pl.BlockSpec((width, HD), lambda i: (i, 0)),
        out_shape=jax.ShapeDtypeStruct((hidden, HD), F32),
        compiler_params=limits(24),
        cost_estimate=cost(8 * rows * hidden * HD, 13),
        name=("key_grad", "value_grad")[which],
    )(*normed, gnear, gfar)


def merge_b_body(arrived_ref, kept_ref, dots_ref, *send_refs):
    half = kept_ref.shape[0]
    total = arrived_ref[0].astype(F32)
    for i in range(1, arrived_ref.shape[0]):
        total += arrived_ref[i].astype(F32)
    kept_ref[...] = total[:half]
    both = dots_of(total[RING * half :])
    dots_ref[...] = both
    pieces = in_four_rows(both)
    for i, ref in enumerate(send_refs):
        ref[:half] = total[(i + 1) * half : (i + 2) * half].astype(BF16)
        ref[half:] = pieces


def merge_b(arrived, half):
    send = jax.ShapeDtypeStruct((half + EXTRA, HD), BF16)
    return pl.pallas_call(
        merge_b_body,
        in_specs=[VMEM],
        out_specs=[VMEM] * 5,
        out_shape=[jax.ShapeDtypeStruct((half, HD), F32), jax.ShapeDtypeStruct((1, 2 * HD), F32)] + [send] * 3,
        compiler_params=limits(16),
        cost_estimate=cost(0, 3),
        name="merge_b",
    )(arrived)


def finish_b_body(hidden, place_ref, gain_ref, block_ref, scale_a, scale_b, kept_ref, dots_ref, r1, r2, r3,
                  out_ref, scale_ref, mean_ref):
    core, segment, pair = place_ref[0], place_ref[1], place_ref[2]
    half = block_ref.shape[0]
    part = half // 2
    total, dots = kept_ref[...], dots_ref[...]
    for ref in (r1, r2, r3):
        total += ref[:half].astype(F32)
        dots += dots_of(ref[half:].astype(F32))
    lane = lax.broadcasted_iota(jnp.int32, (part, HD), 1)
    row = lax.broadcasted_iota(jnp.int32, (part, HD), 0)
    mine = lane == row + segment * part
    pick = lambda values: jnp.sum(jnp.where(mine, values, 0.0), axis=1, keepdims=True)
    mean = above(pick(dots[:, :HD]), pick(dots[:, HD:])) / hidden
    rows = pl.ds(pl.multiple_of(segment * part, part), part)
    scale = above(scale_a[rows], scale_b[rows])
    out_ref[...] = finished(core == 1, total, gain_ref[pair], block_ref[...], scale, mean)
    scale_ref[...] = scale
    mean_ref[...] = mean


def finished(first, total, gain, block, scale, mean):
    gain = jnp.where(first, gain[:, :HD], gain[:, HD:])
    centered = jnp.where(first, block[:, :HD].astype(F32), block[:, HD:].astype(F32)) * scale
    return scale * (total * gain - centered * mean)


def finish_b(place, gain, block, scale_a, scale_b, kept, dots, received):
    half, width = block.shape
    hidden = gain.shape[0]
    column = jax.ShapeDtypeStruct((half, 1), F32)
    return pl.pallas_call(
        functools.partial(finish_b_body, hidden),
        in_specs=[SMEM] + [VMEM] * 9,
        out_specs=[VMEM] * 3,
        out_shape=[jax.ShapeDtypeStruct((half, HD), F32), column, column],
        compiler_params=limits(16),
        cost_estimate=cost(0, 1),
        name="finish_b",
    )(place, gain.reshape(hidden // width, 1, width), block, scale_a, scale_b, kept, dots, *received)


def finish_a_body(place_ref, gain_ref, block_ref, scale_ref, mean_ref, came_ref, arrived_ref, out_ref):
    core, pair = place_ref[0], place_ref[2]
    half = block_ref.shape[0]
    total = arrived_ref[0].astype(F32)
    for i in range(1, arrived_ref.shape[0]):
        total += arrived_ref[i].astype(F32)
    kept = finished(core == 0, total, gain_ref[pair], block_ref[...], scale_ref[...], mean_ref[...])
    out_ref[pl.ds(pl.multiple_of(core * half, half), half)] = kept
    out_ref[pl.ds(pl.multiple_of((1 - core) * half, half), half)] = came_ref[...]


def finish_a(place, gain, block, scale, mean, came, arrived):
    half, width = block.shape
    hidden = gain.shape[0]
    return pl.pallas_call(
        finish_a_body,
        in_specs=[SMEM] + [VMEM] * 6,
        out_specs=VMEM,
        out_shape=jax.ShapeDtypeStruct((2 * half, HD), F32),
        compiler_params=limits(16),
        cost_estimate=cost(0, 1),
        name="finish_a",
    )(place, gain.reshape(hidden // width, 1, width), block, scale, mean, came, arrived)


def in_vmem(value):
    return pltpu.with_memory_space_constraint(value, pltpu.VMEM)


def in_hbm(value):
    return pltpu.with_memory_space_constraint(value, pltpu.HBM)


def swapped(value):
    return lax.ppermute(value, "c", [(0, 1), (1, 0)])


def shifted(value, by):
    return lax.ppermute(value, "z", [(i, (i + by) % RING) for i in range(RING)])


def over_plane(value):
    return lax.all_to_all(value, PLANE, 0, 0, tiled=True)


def after(values, *earlier):
    return lax.optimization_barrier((*values, *earlier))[: len(values)]


def local(memory, norm_gain, queries, key_weight, value_weight, context_grad):
    rows_own, cols_own = memory.shape
    half, width = rows_own // 2, 2 * cols_own
    part = half // 2
    core, z = lax.axis_index("c"), lax.axis_index("z")
    segment = lax.axis_index(("y", "xh"))
    pair = lax.axis_index(("xl", "z"))
    segs, plane = lax.axis_size(("y", "xh")), lax.axis_size(PLANE)
    z_array = jnp.stack([z, core]).astype(jnp.int32)
    place = jnp.stack([core, segment, pair]).astype(jnp.int32)
    wide = lambda value: value.astype(F32)

    halves = memory.reshape(2, half, cols_own)
    mine = lax.dynamic_index_in_dim(halves, core, 0, keepdims=False)
    other = swapped(lax.dynamic_index_in_dim(halves, 1 - core, 0, keepdims=False))
    block = jnp.where(core == 0, beside(mine, other), beside(other, mine))
    first_a = over_plane(copies_of([block[:part]], plane, "copies_a").reshape(plane, part, width))
    high = block[part:]
    near_z = [high, shifted(high, -1), shifted(high, 2), shifted(high, 1)]
    all_b = over_plane(copies_of(near_z, plane, "copies_b"))
    all_b = all_b.reshape(segs, 2, RING, part, width)
    low_0, high_0 = first_a[: plane // 2], first_a[plane // 2 :]
    low_3, high_1 = shifted(low_0, 1), shifted(high_0, -1)
    high_3, low_1 = shifted(high_0, 1), shifted(low_0, -1)
    low_2, high_2 = shifted(low_3, 1), shifted(high_1, -1)
    deep = lambda value: value.reshape(segs // 2, 2, part, width)

    key_own, value_own = after((key_weight[0], value_weight[0]), block)
    weights = staged(z_array, (key_own, value_own, swapped(key_own), swapped(value_own)))

    top = segs // 2
    pieces_a = [(0, 0, None), (3, 0, None), (3, top, None), (1, 0, None), (1, top, None), (2, 0, None), (2, top, None)]
    xs_a = [first_a.reshape(segs, 2, part, width)] + [deep(v) for v in (low_3, high_3, low_1, high_1, low_2, high_2)]
    xs_a = [in_hbm(x) for x in xs_a]
    own_a, sib_a, scale_a, normed_a = project(pieces_a, xs_a, z_array, norm_gain, weights, segs, "project_a")
    far_a = swapped(sib_a)
    all_b, = after((all_b,), own_a)
    normed_far_a = swapped(after((normed_a,), all_b, far_a)[0])
    pieces_b = [(d, 0, d) for d in range(RING)]
    own_b, sib_b, scale_b, normed_b = project(pieces_b, [all_b] * RING, z_array, norm_gain, weights, segs, "project_b")
    far_b = swapped(sib_b)
    normed_far_b = swapped(after((normed_b,), far_b)[0])
    context, query_grad, gnear, gfar, near_dots = attention(queries[0], context_grad[0], own_a, own_b, far_a, far_b)
    gsib = swapped(gfar)

    parts_b = back_b(z_array, gnear, gsib, near_dots, weights[1], segs)
    arrived_b = over_plane(parts_b.reshape(plane, RING * half + EXTRA, HD))
    z_later, = after((z_array,), parts_b)
    opp_low, opp_high, up_low, up_high, down_low, down_high, kept = back_a(z_later, gnear, gsib, weights[0], segs)
    from_low, from_high = shifted(opp_low, 1), shifted(opp_high, -1)
    got_high, got_low = shifted(up_high, 1), shifted(down_low, -1)
    all_normed = (normed_a, normed_b, normed_far_a, normed_far_b)
    key_grad = weight_grad(all_normed, gnear, gfar, 0)
    from_low, from_high = after((from_low, from_high), key_grad)
    last_low = shifted((wide(up_low) + wide(from_low)).astype(BF16), 1)
    last_high = shifted((wide(down_high) + wide(from_high)).astype(BF16), -1)
    value_grad = weight_grad(all_normed, gnear, gfar, 1)
    got_low, got_high = after((got_low, got_high), value_grad)
    summed_low = wide(kept[: segs // 2]) + wide(got_low) + wide(last_low)
    summed_high = wide(kept[segs // 2 :]) + wide(got_high) + wide(last_high)
    summed_a = above(summed_low, summed_high).astype(BF16).reshape(plane, half, HD)

    arrived_b, summed_a = lax.optimization_barrier((arrived_b, summed_a))
    arrived_a = over_plane(summed_a)
    kept_b, dots, to_1, to_2, to_3 = merge_b(arrived_b, half)
    received = (shifted(to_1, 1), shifted(to_2, 2), shifted(to_3, -1))
    value_b, own_scale, mean = finish_b(place, norm_gain, block, scale_a, scale_b, kept_b, dots, received)
    result = finish_a(place, norm_gain, block, own_scale, mean, swapped(value_b), arrived_a)
    return context[None], query_grad[None], key_grad[None], value_grad[None], result


def solution(mesh):
    fine = Mesh(mesh.devices.reshape(4, 2, 2, 4, 2), AXES)
    seg, tp = ("y", "xh"), ("xl", "z", "c")
    heads = P(seg, None, tp)
    return jax.shard_map(
        local,
        mesh=fine,
        in_specs=(P(seg, tp), P(), heads, heads, heads, heads),
        out_specs=(heads, heads, heads, heads, P(seg, tp)),
        check_vma=False,
    )
```

```python
import functools

import jax
import jax.numpy as jnp
from jax import lax
from jax.experimental import pallas as pl
from jax.experimental.pallas import tpu as pltpu
from jax.sharding import Mesh
from jax.sharding import PartitionSpec as P

HD = 256
AXES = ("y", "xh", "xl", "z", "c")
PLANE = ("y", "xh", "xl")
RING = 4
EXTRA = 16
EPS = 1e-06
F32 = jnp.float32
BF16 = jnp.bfloat16
MIB = 2**20
VMEM = pl.BlockSpec(memory_space=pltpu.VMEM)
SMEM = pl.BlockSpec(memory_space=pltpu.SMEM)
ANYWHERE = pl.BlockSpec(memory_space=pl.ANY)


def dot(a, b, contract):
    return lax.dot_general(a, b, ((contract[:1], contract[1:]), ((), ())), preferred_element_type=F32)


def nn(a, b):
    return dot(a, b, (1, 0))


def nt(a, b):
    return dot(a, b, (1, 1))


def tn(a, b):
    return dot(a, b, (0, 0))


def beside(*values):
    return jnp.concatenate(values, axis=1)


def above(*values):
    return jnp.concatenate(values, axis=0)


def limits(mib):
    return pltpu.CompilerParams(vmem_limit_bytes=mib * MIB)


def cost(flops, mib, transcendentals=0):
    return pl.CostEstimate(flops=flops, bytes_accessed=int(mib * MIB), transcendentals=transcendentals)


def stage_body(place_ref, *refs):
    sources, outs = refs[:-2], refs[-2:]
    for j, out in enumerate(outs):
        half = place_ref[1] if j == 0 else 1 - place_ref[1]
        at = pl.ds(pl.multiple_of(half * HD, HD), HD)
        for i, source in enumerate(sources):
            out[0, :, i * HD : (i + 1) * HD] = source[at, :]


def staged(place, weights):
    count, blocks = len(weights), weights[0].shape[0] // (2 * HD)
    block = pl.BlockSpec((1, HD, count * HD), lambda i: (i, 0, 0))
    out = pltpu.HBM((blocks, HD, count * HD), BF16)
    return pl.pallas_call(
        stage_body,
        grid=(blocks,),
        in_specs=[SMEM] + [pl.BlockSpec((2 * HD, HD), lambda i: (i, 0))] * count,
        out_specs=[block] * 2,
        out_shape=[out] * 2,
        compiler_params=limits(8),
        cost_estimate=cost(0, 16),
        name="stage",
    )(place, *[in_hbm(w) for w in weights])


def project_body(pieces, z_ref, gain_ref, *refs):
    xs = refs[: len(pieces)]
    w_refs, refs = refs[len(pieces) : len(pieces) + 2], refs[len(pieces) + 2 :]
    own_ref, sib_ref, scale_ref, normed_ref, held, rows_low, weights, x_sem, w_sem, out_sem = refs
    blocks, segs, part, width = held.shape
    rows = segs * part
    z = z_ref[0]
    copies = []
    for (distance, first, depth), x in zip(pieces, xs):
        for side in range(2):
            place = side * RING + lax.rem(z + distance, RING)
            source = x.at[:, side] if depth is None else x.at[:, side, depth]
            target = held.at[place, pl.ds(first, source.shape[0])]
            copies.append(pltpu.make_async_copy(source, target, x_sem.at[len(copies)]))
    loads = [pltpu.make_async_copy(w, weights.at[i], w_sem.at[i]) for i, w in enumerate(w_refs)]
    for copy in copies + loads:
        copy.start()
    for copy in copies:
        copy.wait()
    squares = jnp.zeros((rows, 128), F32)
    for p in range(blocks):
        wide = held[p].reshape(rows, width).astype(F32)
        wide = wide * wide
        for i in range(width // 128):
            squares += wide[:, i * 128 : (i + 1) * 128]
    scale = lax.rsqrt(jnp.sum(squares, axis=1, keepdims=True) / (blocks * width) + EPS)
    scale_ref[...] = scale
    for p in range(blocks):
        wide = held[p].reshape(rows, width).astype(F32)
        rows_low[:, p * width : (p + 1) * width] = (wide * scale * gain_ref[p]).astype(BF16)
    out = pltpu.make_async_copy(rows_low, normed_ref, out_sem)
    out.start()
    total = 0.0
    for i, load in enumerate(loads):
        load.wait()
        first = z_ref[1] if i == 0 else 1 - z_ref[1]
        columns = beside(*[rows_low[:, pl.ds(pl.multiple_of((2 * p + first) * HD, HD), HD)] for p in range(blocks)])
        total += nn(columns, weights[i].reshape(blocks * HD, 4 * HD))
    own_ref[...] = total[:, : 2 * HD].astype(BF16)
    sib_ref[...] = total[:, 2 * HD :].astype(BF16)
    out.wait()


def project(pieces, xs, z, gain, weights, segs, name):
    part, width = xs[0].shape[-2:]
    blocks = gain.shape[0] // width
    rows = segs * part
    return pl.pallas_call(
        functools.partial(project_body, pieces),
        in_specs=[SMEM, VMEM] + [ANYWHERE] * (len(xs) + 2),
        out_specs=[VMEM, VMEM, VMEM, ANYWHERE],
        out_shape=[
            jax.ShapeDtypeStruct((rows, 2 * HD), BF16),
            jax.ShapeDtypeStruct((rows, 2 * HD), BF16),
            jax.ShapeDtypeStruct((rows, 1), F32),
            jax.ShapeDtypeStruct((rows, blocks * width), BF16),
        ],
        scratch_shapes=[
            pltpu.VMEM((blocks, segs, part, width), BF16),
            pltpu.VMEM((rows, blocks * width), BF16),
            pltpu.VMEM((2, blocks, HD, 4 * HD), BF16),
            pltpu.SemaphoreType.DMA((2 * len(xs),)),
            pltpu.SemaphoreType.DMA((2,)),
            pltpu.SemaphoreType.DMA(()),
        ],
        compiler_params=limits(24),
        cost_estimate=cost(2 * rows * blocks * width * 4 * HD, 12),
        name=name,
    )(z, gain.reshape(blocks, 1, width), *xs, *[in_hbm(w) for w in weights])


def pieces_of(dots):
    high = dots.astype(BF16).astype(F32)
    shape = (EXTRA, dots.shape[1])
    row = lax.broadcasted_iota(jnp.int32, shape, 0)
    low = jnp.broadcast_to(dots - high, shape)
    return jnp.where(row == 0, jnp.broadcast_to(high, shape), jnp.where(row == 1, low, 0.0)).astype(BF16)


def in_four_rows(dots):
    left, right = pieces_of(dots[:, :HD]).astype(F32), pieces_of(dots[:, HD:]).astype(F32)
    row = lax.broadcasted_iota(jnp.int32, left.shape, 0)
    later = jnp.where(row == 2, right[0:1], jnp.where(row == 3, right[1:2], 0.0))
    return jnp.where(row < 2, left, later).astype(BF16)


def dots_of(rows):
    return beside(rows[0:1] + rows[1:2], rows[2:3] + rows[3:4])


def attend_body(tile, q_ref, dc_ref, near_a, near_b, far_a, far_b, ctx_ref, qg_ref, gnear_ref, gfar_ref, near_dots, gkeys, gvalues):
    kv = above(near_a[...], near_b[...], far_a[...], far_b[...])
    k, v = kv[:, :HD], kv[:, HD:]
    half = kv.shape[0] // 2
    scale = HD ** (-0.5)
    row_products = jnp.zeros((8, kv.shape[0]), F32)
    for i in range(q_ref.shape[0] // tile):
        here = slice(i * tile, (i + 1) * tile)
        q, dc = q_ref[here], dc_ref[here]
        scores = nt(q, k) * scale
        expo = jnp.exp(scores - jnp.max(scores, axis=-1, keepdims=True))
        attend = expo * (1.0 / jnp.sum(expo, axis=-1, keepdims=True))
        low = attend.astype(BF16)
        ctx_ref[here] = nn(low, v).astype(BF16)
        gattend = nt(dc, v)
        dots = jnp.sum(gattend * attend, axis=-1, keepdims=True)
        gscores = attend * (gattend - dots)
        both = gscores * scores + attend * gattend
        row_products += jnp.sum(both.reshape(tile // 8, 8, kv.shape[0]), axis=0)
        gscores = (gscores * scale).astype(BF16)
        qg_ref[here] = nn(gscores, k).astype(BF16)
        if i == 0:
            gkeys[...] = tn(gscores, q)
            gvalues[...] = tn(low, dc)
        else:
            gkeys[...] += tn(gscores, q)
            gvalues[...] += tn(low, dc)
    gnear_ref[:, :HD] = gkeys[:half].astype(BF16)
    gnear_ref[:, HD:] = gvalues[:half].astype(BF16)
    gfar_ref[:half, :HD] = gkeys[half:].astype(BF16)
    gfar_ref[:half, HD:] = gvalues[half:].astype(BF16)
    row_products = jnp.sum(row_products, axis=0, keepdims=True)
    near_dots[...] = row_products[:, :half]
    gfar_ref[half:] = pieces_of(row_products[:, half:])


def attention(q, dc, near_a, near_b, far_a, far_b, tile=256):
    targets, half = q.shape[0], 2 * near_a.shape[0]
    return pl.pallas_call(
        functools.partial(attend_body, tile),
        in_specs=[VMEM] * 6,
        out_specs=[VMEM] * 5,
        out_shape=[jax.ShapeDtypeStruct((targets, HD), BF16)] * 2
        + [
            jax.ShapeDtypeStruct((half, 2 * HD), BF16),
            jax.ShapeDtypeStruct((half + EXTRA, 2 * HD), BF16),
            jax.ShapeDtypeStruct((1, half), F32),
        ],
        scratch_shapes=[pltpu.VMEM((2 * half, HD), F32)] * 2,
        compiler_params=limits(20),
        cost_estimate=cost(12 * targets * 2 * half * HD, 4, targets * 2 * half),
        name="attention",
    )(q, dc, near_a, near_b, far_a, far_b)


def feature_block(z, rows, w_ref, distance, side):
    return nt(rows, w_ref[side * RING + lax.rem(z + distance, RING)]).astype(BF16)


def back_b_body(z_ref, own_ref, sib_ref, dots_ref, w_ref, out_ref, stage, out_sem):
    half = own_ref.shape[0]
    segs = out_ref.shape[0]
    part = half // segs // 2
    rows = beside(own_ref[...], sib_ref[:half])
    outs = []
    for distance in range(RING):
        at = distance * 2 * part
        for side in range(2):
            value = feature_block(z_ref[0], rows, w_ref, distance, side).reshape(2, segs, part, HD)
            for k in range(2):
                stage[:, side, at + k * part : at + (k + 1) * part] = value[k]
        size = 2 * part
        if distance == RING - 1:
            extra = sib_ref[half:].astype(F32)
            pieces = in_four_rows(dots_ref[...] + extra[0:1] + extra[1:2])
            stage[:, :, at + size :] = jnp.broadcast_to(pieces, (segs, 2, EXTRA, HD))
            size += EXTRA
        outs.append(pltpu.make_async_copy(stage.at[:, :, pl.ds(at, size)], out_ref.at[:, :, pl.ds(at, size)], out_sem.at[distance]))
        outs[-1].start()
    for out in outs:
        out.wait()


def back_b(z, own, sib, dots, weights, segs):
    rows = own.shape[0]
    shape = (segs, 2, RING * rows // segs + EXTRA, HD)
    return pl.pallas_call(
        back_b_body,
        in_specs=[SMEM] + [VMEM] * 4,
        out_specs=ANYWHERE,
        out_shape=pltpu.HBM(shape, BF16),
        scratch_shapes=[
            pltpu.VMEM(shape, BF16),
            pltpu.SemaphoreType.DMA((RING,)),
        ],
        compiler_params=limits(16),
        cost_estimate=cost(2 * rows * 8 * HD * 4 * HD, 4),
        name="back_b",
    )(z, own, sib, dots, in_vmem(weights))


def back_a_body(z_ref, own_ref, sib_ref, w_ref, *outs):
    rows = beside(own_ref[...], sib_ref[: own_ref.shape[0]])
    segs = outs[-1].shape[0]
    part = rows.shape[0] // segs // 2
    lands = {2: ((0, 0), (1, segs // 2)), 1: ((2, 0), (3, segs // 2)), 3: ((4, 0), (5, segs // 2)), 0: ((6, 0),)}
    for distance in (2, 1, 3, 0):
        for side in range(2):
            value = feature_block(z_ref[0], rows, w_ref, distance, side).reshape(2, segs, part, HD)
            for index, first in lands[distance]:
                for k in range(2):
                    count = outs[index].shape[0]
                    outs[index][:, side, k * part : (k + 1) * part] = value[k, first : first + count]


def back_a(z, own, sib, weights, segs):
    rows = own.shape[0]
    half = jax.ShapeDtypeStruct((segs // 2, 2, rows // segs, HD), BF16)
    full = jax.ShapeDtypeStruct((segs, 2, rows // segs, HD), BF16)
    return pl.pallas_call(
        back_a_body,
        in_specs=[SMEM] + [VMEM] * 3,
        out_specs=[VMEM] * 7,
        out_shape=[half] * 6 + [full],
        compiler_params=limits(16),
        cost_estimate=cost(2 * rows * 8 * HD * 4 * HD, 4),
        name="back_a",
    )(z, own, sib, in_vmem(weights))


def weights_body(near_a, near_b, far_a, far_b, gnear_ref, gfar_ref, gk_ref, gv_ref):
    rows = above(near_a[...], near_b[...], far_a[...], far_b[...])
    total = tn(rows, above(gnear_ref[...], gfar_ref[: gnear_ref.shape[0]]))
    gk_ref[...] = total[:, :HD]
    gv_ref[...] = total[:, HD:]


def weight_grads(near_a, near_b, far_a, far_b, gnear, gfar, width=512):
    rows, hidden = near_a.shape
    block = pl.BlockSpec((rows, width), lambda i: (0, i))
    near = pl.BlockSpec(gnear.shape, lambda i: (0, 0))
    far = pl.BlockSpec(gfar.shape, lambda i: (0, 0))
    out = pl.BlockSpec((width, HD), lambda i: (i, 0))
    return pl.pallas_call(
        weights_body,
        grid=(hidden // width,),
        in_specs=[block] * 4 + [near, far],
        out_specs=[out, out],
        out_shape=[jax.ShapeDtypeStruct((hidden, HD), F32)] * 2,
        compiler_params=limits(16),
        cost_estimate=cost(16 * rows * hidden * HD, 17),
        name="weight_grads",
    )(near_a, near_b, far_a, far_b, gnear, gfar)


def merge_b_body(arrived_ref, kept_ref, dots_ref, *send_refs):
    half = kept_ref.shape[0]
    total = arrived_ref[0].astype(F32)
    for i in range(1, arrived_ref.shape[0]):
        total += arrived_ref[i].astype(F32)
    kept_ref[...] = total[:half]
    both = dots_of(total[RING * half :])
    dots_ref[...] = both
    pieces = in_four_rows(both)
    for i, ref in enumerate(send_refs):
        ref[:half] = total[(i + 1) * half : (i + 2) * half].astype(BF16)
        ref[half:] = pieces


def merge_b(arrived, half):
    send = jax.ShapeDtypeStruct((half + EXTRA, HD), BF16)
    return pl.pallas_call(
        merge_b_body,
        in_specs=[VMEM],
        out_specs=[VMEM] * 5,
        out_shape=[jax.ShapeDtypeStruct((half, HD), F32), jax.ShapeDtypeStruct((1, 2 * HD), F32)] + [send] * 3,
        compiler_params=limits(16),
        cost_estimate=cost(0, 3),
        name="merge_b",
    )(arrived)


def finish_b_body(hidden, place_ref, gain_ref, block_ref, scale_a, scale_b, kept_ref, dots_ref, r1, r2, r3,
                  out_ref, scale_ref, mean_ref):
    core, segment, pair = place_ref[0], place_ref[1], place_ref[2]
    half = block_ref.shape[0]
    part = half // 2
    total, dots = kept_ref[...], dots_ref[...]
    for ref in (r1, r2, r3):
        total += ref[:half].astype(F32)
        dots += dots_of(ref[half:].astype(F32))
    lane = lax.broadcasted_iota(jnp.int32, (part, HD), 1)
    row = lax.broadcasted_iota(jnp.int32, (part, HD), 0)
    mine = lane == row + segment * part
    pick = lambda values: jnp.sum(jnp.where(mine, values, 0.0), axis=1, keepdims=True)
    mean = above(pick(dots[:, :HD]), pick(dots[:, HD:])) / hidden
    rows = pl.ds(pl.multiple_of(segment * part, part), part)
    scale = above(scale_a[rows], scale_b[rows])
    out_ref[...] = finished(core == 1, total, gain_ref[pair], block_ref[...], scale, mean)
    scale_ref[...] = scale
    mean_ref[...] = mean


def finished(first, total, gain, block, scale, mean):
    gain = jnp.where(first, gain[:, :HD], gain[:, HD:])
    centered = jnp.where(first, block[:, :HD].astype(F32), block[:, HD:].astype(F32)) * scale
    return scale * (total * gain - centered * mean)


def finish_b(place, gain, block, scale_a, scale_b, kept, dots, received):
    half, width = block.shape
    hidden = gain.shape[0]
    column = jax.ShapeDtypeStruct((half, 1), F32)
    return pl.pallas_call(
        functools.partial(finish_b_body, hidden),
        in_specs=[SMEM] + [VMEM] * 9,
        out_specs=[VMEM] * 3,
        out_shape=[jax.ShapeDtypeStruct((half, HD), F32), column, column],
        compiler_params=limits(16),
        cost_estimate=cost(0, 1),
        name="finish_b",
    )(place, gain.reshape(hidden // width, 1, width), block, scale_a, scale_b, kept, dots, *received)


def finish_a_body(place_ref, gain_ref, block_ref, scale_ref, mean_ref, came_ref, arrived_ref, out_ref):
    core, pair = place_ref[0], place_ref[2]
    half = block_ref.shape[0]
    total = arrived_ref[0].astype(F32)
    for i in range(1, arrived_ref.shape[0]):
        total += arrived_ref[i].astype(F32)
    kept = finished(core == 0, total, gain_ref[pair], block_ref[...], scale_ref[...], mean_ref[...])
    out_ref[pl.ds(pl.multiple_of(core * half, half), half)] = kept
    out_ref[pl.ds(pl.multiple_of((1 - core) * half, half), half)] = came_ref[...]


def finish_a(place, gain, block, scale, mean, came, arrived):
    half, width = block.shape
    hidden = gain.shape[0]
    return pl.pallas_call(
        finish_a_body,
        in_specs=[SMEM] + [VMEM] * 6,
        out_specs=VMEM,
        out_shape=jax.ShapeDtypeStruct((2 * half, HD), F32),
        compiler_params=limits(16),
        cost_estimate=cost(0, 1),
        name="finish_a",
    )(place, gain.reshape(hidden // width, 1, width), block, scale, mean, came, arrived)


def in_vmem(value):
    return pltpu.with_memory_space_constraint(value, pltpu.VMEM)


def in_hbm(value):
    return pltpu.with_memory_space_constraint(value, pltpu.HBM)


def swapped(value):
    return lax.ppermute(value, "c", [(0, 1), (1, 0)])


def shifted(value, by):
    return lax.ppermute(value, "z", [(i, (i + by) % RING) for i in range(RING)])


def over_plane(value):
    return lax.all_to_all(value, PLANE, 0, 0, tiled=True)


def after(values, *earlier):
    return lax.optimization_barrier((*values, *earlier))[: len(values)]


def local(memory, norm_gain, queries, key_weight, value_weight, context_grad):
    rows_own, cols_own = memory.shape
    half, width = rows_own // 2, 2 * cols_own
    part = half // 2
    core, z = lax.axis_index("c"), lax.axis_index("z")
    segment = lax.axis_index(("y", "xh"))
    pair = lax.axis_index(("xl", "z"))
    segs, plane = lax.axis_size(("y", "xh")), lax.axis_size(PLANE)
    z_array = jnp.stack([z, core]).astype(jnp.int32)
    place = jnp.stack([core, segment, pair]).astype(jnp.int32)
    wide = lambda value: value.astype(F32)

    halves = memory.reshape(2, half, cols_own)
    mine = lax.dynamic_index_in_dim(halves, core, 0, keepdims=False)
    other = swapped(lax.dynamic_index_in_dim(halves, 1 - core, 0, keepdims=False))
    block = jnp.where(core == 0, beside(mine, other), beside(other, mine))
    first_a = over_plane(jnp.broadcast_to(block[:part], (plane, part, width)))
    high = block[part:]
    near_z = jnp.stack([high, shifted(high, -1), shifted(high, 2), shifted(high, 1)])
    all_b = over_plane(jnp.broadcast_to(near_z, (plane, RING, part, width)))
    all_b = all_b.reshape(segs, 2, RING, part, width)
    low_0, high_0 = first_a[: plane // 2], first_a[plane // 2 :]
    low_3, high_1 = shifted(low_0, 1), shifted(high_0, -1)
    high_3, low_1 = shifted(high_0, 1), shifted(low_0, -1)
    low_2, high_2 = shifted(low_3, 1), shifted(high_1, -1)
    deep = lambda value: value.reshape(segs // 2, 2, part, width)

    key_own, value_own = after((key_weight[0], value_weight[0]), block)
    weights = staged(z_array, (key_own, value_own, swapped(key_own), swapped(value_own)))

    top = segs // 2
    pieces_a = [(0, 0, None), (3, 0, None), (3, top, None), (1, 0, None), (1, top, None), (2, 0, None), (2, top, None)]
    xs_a = [first_a.reshape(segs, 2, part, width)] + [deep(v) for v in (low_3, high_3, low_1, high_1, low_2, high_2)]
    xs_a = [in_hbm(x) for x in xs_a]
    own_a, sib_a, scale_a, normed_a = project(pieces_a, xs_a, z_array, norm_gain, weights, segs, "project_a")
    far_a = swapped(sib_a)
    all_b, = after((all_b,), own_a)
    normed_far_a = swapped(after((normed_a,), all_b, far_a)[0])
    pieces_b = [(d, 0, d) for d in range(RING)]
    own_b, sib_b, scale_b, normed_b = project(pieces_b, [all_b] * RING, z_array, norm_gain, weights, segs, "project_b")
    far_b = swapped(sib_b)
    normed_far_b = swapped(after((normed_b,), far_b)[0])
    context, query_grad, gnear, gfar, near_dots = attention(queries[0], context_grad[0], own_a, own_b, far_a, far_b)
    gsib = swapped(gfar)

    parts_b = back_b(z_array, gnear, gsib, near_dots, weights[1], segs)
    arrived_b = over_plane(parts_b.reshape(plane, RING * half + EXTRA, HD))
    z_later, = after((z_array,), parts_b)
    opp_low, opp_high, up_low, up_high, down_low, down_high, kept = back_a(z_later, gnear, gsib, weights[0], segs)
    from_low, from_high = shifted(opp_low, 1), shifted(opp_high, -1)
    got_high, got_low = shifted(up_high, 1), shifted(down_low, -1)
    all_normed = (normed_a, normed_b, normed_far_a, normed_far_b)
    key_grad, value_grad = weight_grads(*all_normed, gnear, gfar)
    from_low, from_high = after((from_low, from_high), key_grad, value_grad)
    last_low = shifted((wide(up_low) + wide(from_low)).astype(BF16), 1)
    last_high = shifted((wide(down_high) + wide(from_high)).astype(BF16), -1)
    summed_low = wide(kept[: segs // 2]) + wide(got_low) + wide(last_low)
    summed_high = wide(kept[segs // 2 :]) + wide(got_high) + wide(last_high)
    summed_a = above(summed_low, summed_high).astype(BF16).reshape(plane, half, HD)

    arrived_b, summed_a = lax.optimization_barrier((arrived_b, summed_a))
    arrived_a = over_plane(summed_a)
    kept_b, dots, to_1, to_2, to_3 = merge_b(arrived_b, half)
    received = (shifted(to_1, 1), shifted(to_2, 2), shifted(to_3, -1))
    value_b, own_scale, mean = finish_b(place, norm_gain, block, scale_a, scale_b, kept_b, dots, received)
    result = finish_a(place, norm_gain, block, own_scale, mean, swapped(value_b), arrived_a)
    return context[None], query_grad[None], key_grad[None], value_grad[None], result


def solution(mesh):
    fine = Mesh(mesh.devices.reshape(4, 2, 2, 4, 2), AXES)
    seg, tp = ("y", "xh"), ("xl", "z", "c")
    heads = P(seg, None, tp)
    return jax.shard_map(
        local,
        mesh=fine,
        in_specs=(P(seg, tp), P(), heads, heads, heads, heads),
        out_specs=(heads, heads, heads, heads, P(seg, tp)),
        check_vma=False,
    )
```

```python
import functools

import jax
import jax.numpy as jnp
from jax import lax
from jax.experimental import pallas as pl
from jax.experimental.pallas import tpu as pltpu
from jax.sharding import Mesh
from jax.sharding import PartitionSpec as P

HD = 256
AXES = ("y", "xh", "xl", "z", "c")
PLANE = ("y", "xh", "xl")
RING = 4
EXTRA = 16
EPS = 1e-06
F32 = jnp.float32
BF16 = jnp.bfloat16
MIB = 2**20
VMEM = pl.BlockSpec(memory_space=pltpu.VMEM)
SMEM = pl.BlockSpec(memory_space=pltpu.SMEM)
ANYWHERE = pl.BlockSpec(memory_space=pl.ANY)


def dot(a, b, contract):
    return lax.dot_general(a, b, ((contract[:1], contract[1:]), ((), ())), preferred_element_type=F32)


def nn(a, b):
    return dot(a, b, (1, 0))


def nt(a, b):
    return dot(a, b, (1, 1))


def tn(a, b):
    return dot(a, b, (0, 0))


def beside(*values):
    return jnp.concatenate(values, axis=1)


def above(*values):
    return jnp.concatenate(values, axis=0)


def limits(mib):
    return pltpu.CompilerParams(vmem_limit_bytes=mib * MIB)


def cost(flops, mib, transcendentals=0):
    return pl.CostEstimate(flops=flops, bytes_accessed=int(mib * MIB), transcendentals=transcendentals)


def stage_body(place_ref, *refs):
    sources, outs = refs[:-2], refs[-2:]
    for j, out in enumerate(outs):
        half = place_ref[1] if j == 0 else 1 - place_ref[1]
        at = pl.ds(pl.multiple_of(half * HD, HD), HD)
        for i, source in enumerate(sources):
            out[0, :, i * HD : (i + 1) * HD] = source[at, :]


def staged(place, weights):
    count, blocks = len(weights), weights[0].shape[0] // (2 * HD)
    block = pl.BlockSpec((1, HD, count * HD), lambda i: (i, 0, 0))
    out = pltpu.HBM((blocks, HD, count * HD), BF16)
    return pl.pallas_call(
        stage_body,
        grid=(blocks,),
        in_specs=[SMEM] + [pl.BlockSpec((2 * HD, HD), lambda i: (i, 0))] * count,
        out_specs=[block] * 2,
        out_shape=[out] * 2,
        compiler_params=limits(8),
        cost_estimate=cost(0, 16),
        name="stage",
    )(place, *[in_hbm(w) for w in weights])


def project_body(pieces, z_ref, gain_ref, *refs):
    xs = refs[: len(pieces)]
    w_refs, refs = refs[len(pieces) : len(pieces) + 2], refs[len(pieces) + 2 :]
    own_ref, sib_ref, scale_ref, normed_ref, held, rows_low, weights, x_sem, w_sem, out_sem = refs
    blocks, segs, part, width = held.shape
    rows = segs * part
    z = z_ref[0]
    copies = []
    for (distance, first, depth), x in zip(pieces, xs):
        for side in range(2):
            place = side * RING + lax.rem(z + distance, RING)
            source = x.at[:, side] if depth is None else x.at[:, side, depth]
            target = held.at[place, pl.ds(first, source.shape[0])]
            copies.append(pltpu.make_async_copy(source, target, x_sem.at[len(copies)]))
    loads = [pltpu.make_async_copy(w, weights.at[i], w_sem.at[i]) for i, w in enumerate(w_refs)]
    for copy in copies + loads:
        copy.start()
    for copy in copies:
        copy.wait()
    squares = jnp.zeros((rows, 128), F32)
    for p in range(blocks):
        wide = held[p].reshape(rows, width).astype(F32)
        wide = wide * wide
        for i in range(width // 128):
            squares += wide[:, i * 128 : (i + 1) * 128]
    scale = lax.rsqrt(jnp.sum(squares, axis=1, keepdims=True) / (blocks * width) + EPS)
    scale_ref[...] = scale
    for p in range(blocks):
        wide = held[p].reshape(rows, width).astype(F32)
        rows_low[:, p * width : (p + 1) * width] = (wide * scale * gain_ref[p]).astype(BF16)
    out = pltpu.make_async_copy(rows_low, normed_ref, out_sem)
    out.start()

    def products(core):
        total = 0.0
        for i, load in enumerate(loads):
            load.wait()
            half = core if i == 0 else 1 - core
            columns = beside(*[rows_low[:, (2 * p + half) * HD : (2 * p + half + 1) * HD] for p in range(blocks)])
            total += nn(columns, weights[i].reshape(blocks * HD, 4 * HD))
        own_ref[...] = total[:, : 2 * HD].astype(BF16)
        sib_ref[...] = total[:, 2 * HD :].astype(BF16)

    lax.cond(z_ref[1] == 0, lambda: products(0), lambda: products(1))
    out.wait()


def project(pieces, xs, z, gain, weights, segs, name):
    part, width = xs[0].shape[-2:]
    blocks = gain.shape[0] // width
    rows = segs * part
    return pl.pallas_call(
        functools.partial(project_body, pieces),
        in_specs=[SMEM, VMEM] + [ANYWHERE] * (len(xs) + 2),
        out_specs=[VMEM, VMEM, VMEM, ANYWHERE],
        out_shape=[
            jax.ShapeDtypeStruct((rows, 2 * HD), BF16),
            jax.ShapeDtypeStruct((rows, 2 * HD), BF16),
            jax.ShapeDtypeStruct((rows, 1), F32),
            jax.ShapeDtypeStruct((rows, blocks * width), BF16),
        ],
        scratch_shapes=[
            pltpu.VMEM((blocks, segs, part, width), BF16),
            pltpu.VMEM((rows, blocks * width), BF16),
            pltpu.VMEM((2, blocks, HD, 4 * HD), BF16),
            pltpu.SemaphoreType.DMA((2 * len(xs),)),
            pltpu.SemaphoreType.DMA((2,)),
            pltpu.SemaphoreType.DMA(()),
        ],
        compiler_params=limits(24),
        cost_estimate=cost(2 * rows * blocks * width * 4 * HD, 12),
        name=name,
    )(z, gain.reshape(blocks, 1, width), *xs, *[in_hbm(w) for w in weights])


def pieces_of(dots):
    high = dots.astype(BF16).astype(F32)
    shape = (EXTRA, dots.shape[1])
    row = lax.broadcasted_iota(jnp.int32, shape, 0)
    low = jnp.broadcast_to(dots - high, shape)
    return jnp.where(row == 0, jnp.broadcast_to(high, shape), jnp.where(row == 1, low, 0.0)).astype(BF16)


def in_four_rows(dots):
    left, right = pieces_of(dots[:, :HD]).astype(F32), pieces_of(dots[:, HD:]).astype(F32)
    row = lax.broadcasted_iota(jnp.int32, left.shape, 0)
    later = jnp.where(row == 2, right[0:1], jnp.where(row == 3, right[1:2], 0.0))
    return jnp.where(row < 2, left, later).astype(BF16)


def dots_of(rows):
    return beside(rows[0:1] + rows[1:2], rows[2:3] + rows[3:4])


def attend_body(tile, q_ref, dc_ref, near_a, near_b, far_a, far_b, ctx_ref, qg_ref, gnear_ref, gfar_ref, near_dots, gkeys, gvalues):
    kv = above(near_a[...], near_b[...], far_a[...], far_b[...])
    k, v = kv[:, :HD], kv[:, HD:]
    half = kv.shape[0] // 2
    scale = HD ** (-0.5)
    row_products = jnp.zeros((8, kv.shape[0]), F32)
    for i in range(q_ref.shape[0] // tile):
        here = slice(i * tile, (i + 1) * tile)
        q, dc = q_ref[here], dc_ref[here]
        scores = nt(q, k) * scale
        expo = jnp.exp(scores - jnp.max(scores, axis=-1, keepdims=True))
        attend = expo * (1.0 / jnp.sum(expo, axis=-1, keepdims=True))
        low = attend.astype(BF16)
        ctx_ref[here] = nn(low, v).astype(BF16)
        gattend = nt(dc, v)
        dots = jnp.sum(gattend * attend, axis=-1, keepdims=True)
        gscores = attend * (gattend - dots)
        both = gscores * scores + attend * gattend
        row_products += jnp.sum(both.reshape(tile // 8, 8, kv.shape[0]), axis=0)
        gscores = (gscores * scale).astype(BF16)
        qg_ref[here] = nn(gscores, k).astype(BF16)
        if i == 0:
            gkeys[...] = tn(gscores, q)
            gvalues[...] = tn(low, dc)
        else:
            gkeys[...] += tn(gscores, q)
            gvalues[...] += tn(low, dc)
    gnear_ref[:, :HD] = gkeys[:half].astype(BF16)
    gnear_ref[:, HD:] = gvalues[:half].astype(BF16)
    gfar_ref[:half, :HD] = gkeys[half:].astype(BF16)
    gfar_ref[:half, HD:] = gvalues[half:].astype(BF16)
    row_products = jnp.sum(row_products, axis=0, keepdims=True)
    near_dots[...] = row_products[:, :half]
    gfar_ref[half:] = pieces_of(row_products[:, half:])


def attention(q, dc, near_a, near_b, far_a, far_b, tile=256):
    targets, half = q.shape[0], 2 * near_a.shape[0]
    return pl.pallas_call(
        functools.partial(attend_body, tile),
        in_specs=[VMEM] * 6,
        out_specs=[VMEM] * 5,
        out_shape=[jax.ShapeDtypeStruct((targets, HD), BF16)] * 2
        + [
            jax.ShapeDtypeStruct((half, 2 * HD), BF16),
            jax.ShapeDtypeStruct((half + EXTRA, 2 * HD), BF16),
            jax.ShapeDtypeStruct((1, half), F32),
        ],
        scratch_shapes=[pltpu.VMEM((2 * half, HD), F32)] * 2,
        compiler_params=limits(20),
        cost_estimate=cost(12 * targets * 2 * half * HD, 4, targets * 2 * half),
        name="attention",
    )(q, dc, near_a, near_b, far_a, far_b)


def feature_block(z, rows, w_ref, distance, side):
    return nt(rows, w_ref[side * RING + lax.rem(z + distance, RING)]).astype(BF16)


def back_b_body(z_ref, own_ref, sib_ref, dots_ref, w_ref, out_ref, stage, out_sem):
    half = own_ref.shape[0]
    segs = out_ref.shape[0]
    part = half // segs // 2
    rows = beside(own_ref[...], sib_ref[:half])
    outs = []
    for distance in range(RING):
        at = distance * 2 * part
        for side in range(2):
            value = feature_block(z_ref[0], rows, w_ref, distance, side).reshape(2, segs, part, HD)
            for k in range(2):
                stage[:, side, at + k * part : at + (k + 1) * part] = value[k]
        size = 2 * part
        if distance == RING - 1:
            extra = sib_ref[half:].astype(F32)
            pieces = in_four_rows(dots_ref[...] + extra[0:1] + extra[1:2])
            stage[:, :, at + size :] = jnp.broadcast_to(pieces, (segs, 2, EXTRA, HD))
            size += EXTRA
        outs.append(pltpu.make_async_copy(stage.at[:, :, pl.ds(at, size)], out_ref.at[:, :, pl.ds(at, size)], out_sem.at[distance]))
        outs[-1].start()
    for out in outs:
        out.wait()


def back_b(z, own, sib, dots, weights, segs):
    rows = own.shape[0]
    shape = (segs, 2, RING * rows // segs + EXTRA, HD)
    return pl.pallas_call(
        back_b_body,
        in_specs=[SMEM] + [VMEM] * 4,
        out_specs=ANYWHERE,
        out_shape=pltpu.HBM(shape, BF16),
        scratch_shapes=[
            pltpu.VMEM(shape, BF16),
            pltpu.SemaphoreType.DMA((RING,)),
        ],
        compiler_params=limits(16),
        cost_estimate=cost(2 * rows * 8 * HD * 4 * HD, 4),
        name="back_b",
    )(z, own, sib, dots, in_vmem(weights))


def back_a_body(z_ref, own_ref, sib_ref, w_ref, *outs):
    rows = beside(own_ref[...], sib_ref[: own_ref.shape[0]])
    segs = outs[-1].shape[0]
    part = rows.shape[0] // segs // 2
    lands = {2: ((0, 0), (1, segs // 2)), 1: ((2, 0), (3, segs // 2)), 3: ((4, 0), (5, segs // 2)), 0: ((6, 0),)}
    for distance in (2, 1, 3, 0):
        for side in range(2):
            value = feature_block(z_ref[0], rows, w_ref, distance, side).reshape(2, segs, part, HD)
            for index, first in lands[distance]:
                for k in range(2):
                    count = outs[index].shape[0]
                    outs[index][:, side, k * part : (k + 1) * part] = value[k, first : first + count]


def back_a(z, own, sib, weights, segs):
    rows = own.shape[0]
    half = jax.ShapeDtypeStruct((segs // 2, 2, rows // segs, HD), BF16)
    full = jax.ShapeDtypeStruct((segs, 2, rows // segs, HD), BF16)
    return pl.pallas_call(
        back_a_body,
        in_specs=[SMEM] + [VMEM] * 3,
        out_specs=[VMEM] * 7,
        out_shape=[half] * 6 + [full],
        compiler_params=limits(16),
        cost_estimate=cost(2 * rows * 8 * HD * 4 * HD, 4),
        name="back_a",
    )(z, own, sib, in_vmem(weights))


def weights_body(near_a, near_b, far_a, far_b, gnear_ref, gfar_ref, gk_ref, gv_ref):
    rows = above(near_a[...], near_b[...], far_a[...], far_b[...])
    total = tn(rows, above(gnear_ref[...], gfar_ref[: gnear_ref.shape[0]]))
    gk_ref[...] = total[:, :HD]
    gv_ref[...] = total[:, HD:]


def weight_grads(near_a, near_b, far_a, far_b, gnear, gfar, width=512):
    rows, hidden = near_a.shape
    block = pl.BlockSpec((rows, width), lambda i: (0, i))
    near = pl.BlockSpec(gnear.shape, lambda i: (0, 0))
    far = pl.BlockSpec(gfar.shape, lambda i: (0, 0))
    out = pl.BlockSpec((width, HD), lambda i: (i, 0))
    return pl.pallas_call(
        weights_body,
        grid=(hidden // width,),
        in_specs=[block] * 4 + [near, far],
        out_specs=[out, out],
        out_shape=[jax.ShapeDtypeStruct((hidden, HD), F32)] * 2,
        compiler_params=limits(16),
        cost_estimate=cost(16 * rows * hidden * HD, 17),
        name="weight_grads",
    )(near_a, near_b, far_a, far_b, gnear, gfar)


def merge_b_body(arrived_ref, kept_ref, dots_ref, *send_refs):
    half = kept_ref.shape[0]
    total = arrived_ref[0].astype(F32)
    for i in range(1, arrived_ref.shape[0]):
        total += arrived_ref[i].astype(F32)
    kept_ref[...] = total[:half]
    both = dots_of(total[RING * half :])
    dots_ref[...] = both
    pieces = in_four_rows(both)
    for i, ref in enumerate(send_refs):
        ref[:half] = total[(i + 1) * half : (i + 2) * half].astype(BF16)
        ref[half:] = pieces


def merge_b(arrived, half):
    send = jax.ShapeDtypeStruct((half + EXTRA, HD), BF16)
    return pl.pallas_call(
        merge_b_body,
        in_specs=[VMEM],
        out_specs=[VMEM] * 5,
        out_shape=[jax.ShapeDtypeStruct((half, HD), F32), jax.ShapeDtypeStruct((1, 2 * HD), F32)] + [send] * 3,
        compiler_params=limits(16),
        cost_estimate=cost(0, 3),
        name="merge_b",
    )(arrived)


def finish_b_body(hidden, place_ref, gain_ref, block_ref, scale_a, scale_b, kept_ref, dots_ref, r1, r2, r3,
                  out_ref, scale_ref, mean_ref):
    core, segment, pair = place_ref[0], place_ref[1], place_ref[2]
    half = block_ref.shape[0]
    part = half // 2
    total, dots = kept_ref[...], dots_ref[...]
    for ref in (r1, r2, r3):
        total += ref[:half].astype(F32)
        dots += dots_of(ref[half:].astype(F32))
    lane = lax.broadcasted_iota(jnp.int32, (part, HD), 1)
    row = lax.broadcasted_iota(jnp.int32, (part, HD), 0)
    mine = lane == row + segment * part
    pick = lambda values: jnp.sum(jnp.where(mine, values, 0.0), axis=1, keepdims=True)
    mean = above(pick(dots[:, :HD]), pick(dots[:, HD:])) / hidden
    rows = pl.ds(pl.multiple_of(segment * part, part), part)
    scale = above(scale_a[rows], scale_b[rows])
    out_ref[...] = finished(core == 1, total, gain_ref[pair], block_ref[...], scale, mean)
    scale_ref[...] = scale
    mean_ref[...] = mean


def finished(first, total, gain, block, scale, mean):
    gain = jnp.where(first, gain[:, :HD], gain[:, HD:])
    centered = jnp.where(first, block[:, :HD].astype(F32), block[:, HD:].astype(F32)) * scale
    return scale * (total * gain - centered * mean)


def finish_b(place, gain, block, scale_a, scale_b, kept, dots, received):
    half, width = block.shape
    hidden = gain.shape[0]
    column = jax.ShapeDtypeStruct((half, 1), F32)
    return pl.pallas_call(
        functools.partial(finish_b_body, hidden),
        in_specs=[SMEM] + [VMEM] * 9,
        out_specs=[VMEM] * 3,
        out_shape=[jax.ShapeDtypeStruct((half, HD), F32), column, column],
        compiler_params=limits(16),
        cost_estimate=cost(0, 1),
        name="finish_b",
    )(place, gain.reshape(hidden // width, 1, width), block, scale_a, scale_b, kept, dots, *received)


def finish_a_body(place_ref, gain_ref, block_ref, scale_ref, mean_ref, came_ref, arrived_ref, out_ref):
    core, pair = place_ref[0], place_ref[2]
    half = block_ref.shape[0]
    total = arrived_ref[0].astype(F32)
    for i in range(1, arrived_ref.shape[0]):
        total += arrived_ref[i].astype(F32)
    kept = finished(core == 0, total, gain_ref[pair], block_ref[...], scale_ref[...], mean_ref[...])
    out_ref[pl.ds(pl.multiple_of(core * half, half), half)] = kept
    out_ref[pl.ds(pl.multiple_of((1 - core) * half, half), half)] = came_ref[...]


def finish_a(place, gain, block, scale, mean, came, arrived):
    half, width = block.shape
    hidden = gain.shape[0]
    return pl.pallas_call(
        finish_a_body,
        in_specs=[SMEM] + [VMEM] * 6,
        out_specs=VMEM,
        out_shape=jax.ShapeDtypeStruct((2 * half, HD), F32),
        compiler_params=limits(16),
        cost_estimate=cost(0, 1),
        name="finish_a",
    )(place, gain.reshape(hidden // width, 1, width), block, scale, mean, came, arrived)


def in_vmem(value):
    return pltpu.with_memory_space_constraint(value, pltpu.VMEM)


def in_hbm(value):
    return pltpu.with_memory_space_constraint(value, pltpu.HBM)


def swapped(value):
    return lax.ppermute(value, "c", [(0, 1), (1, 0)])


def shifted(value, by):
    return lax.ppermute(value, "z", [(i, (i + by) % RING) for i in range(RING)])


def over_plane(value):
    return lax.all_to_all(value, PLANE, 0, 0, tiled=True)


def after(values, *earlier):
    return lax.optimization_barrier((*values, *earlier))[: len(values)]


def local(memory, norm_gain, queries, key_weight, value_weight, context_grad):
    rows_own, cols_own = memory.shape
    half, width = rows_own // 2, 2 * cols_own
    part = half // 2
    core, z = lax.axis_index("c"), lax.axis_index("z")
    segment = lax.axis_index(("y", "xh"))
    pair = lax.axis_index(("xl", "z"))
    segs, plane = lax.axis_size(("y", "xh")), lax.axis_size(PLANE)
    z_array = jnp.stack([z, core]).astype(jnp.int32)
    place = jnp.stack([core, segment, pair]).astype(jnp.int32)
    wide = lambda value: value.astype(F32)

    halves = memory.reshape(2, half, cols_own)
    mine = lax.dynamic_index_in_dim(halves, core, 0, keepdims=False)
    other = swapped(lax.dynamic_index_in_dim(halves, 1 - core, 0, keepdims=False))
    block = jnp.where(core == 0, beside(mine, other), beside(other, mine))
    first_a = over_plane(jnp.broadcast_to(block[:part], (plane, part, width)))
    high = block[part:]
    near_z = jnp.stack([high, shifted(high, -1), shifted(high, 2), shifted(high, 1)])
    all_b = over_plane(jnp.broadcast_to(near_z, (plane, RING, part, width)))
    all_b = all_b.reshape(segs, 2, RING, part, width)
    low_0, high_0 = first_a[: plane // 2], first_a[plane // 2 :]
    low_3, high_1 = shifted(low_0, 1), shifted(high_0, -1)
    high_0, low_0 = after((high_0, low_0), low_3, high_1)
    high_3, low_1 = shifted(high_0, 1), shifted(low_0, -1)
    low_2, high_2 = shifted(low_3, 1), shifted(high_1, -1)
    deep = lambda value: value.reshape(segs // 2, 2, part, width)

    key_own, value_own = after((key_weight[0], value_weight[0]), block)
    weights = staged(z_array, (key_own, value_own, swapped(key_own), swapped(value_own)))

    top = segs // 2
    pieces_a = [(0, 0, None), (3, 0, None), (3, top, None), (1, 0, None), (1, top, None), (2, 0, None), (2, top, None)]
    xs_a = [first_a.reshape(segs, 2, part, width)] + [deep(v) for v in (low_3, high_3, low_1, high_1, low_2, high_2)]
    xs_a = [in_hbm(x) for x in xs_a]
    own_a, sib_a, scale_a, normed_a = project(pieces_a, xs_a, z_array, norm_gain, weights, segs, "project_a")
    far_a = swapped(sib_a)
    all_b, = after((all_b,), own_a)
    normed_far_a = swapped(after((normed_a,), all_b, far_a)[0])
    pieces_b = [(d, 0, d) for d in range(RING)]
    own_b, sib_b, scale_b, normed_b = project(pieces_b, [all_b] * RING, z_array, norm_gain, weights, segs, "project_b")
    far_b = swapped(sib_b)
    normed_far_b = swapped(after((normed_b,), far_b)[0])
    context, query_grad, gnear, gfar, near_dots = attention(queries[0], context_grad[0], own_a, own_b, far_a, far_b)
    gsib = swapped(gfar)

    parts_b = back_b(z_array, gnear, gsib, near_dots, weights[1], segs)
    arrived_b = over_plane(parts_b.reshape(plane, RING * half + EXTRA, HD))
    z_later, = after((z_array,), parts_b)
    opp_low, opp_high, up_low, up_high, down_low, down_high, kept = back_a(z_later, gnear, gsib, weights[0], segs)
    from_low, from_high = shifted(opp_low, 1), shifted(opp_high, -1)
    got_high, got_low = shifted(up_high, 1), shifted(down_low, -1)
    all_normed = (normed_a, normed_b, normed_far_a, normed_far_b)
    key_grad, value_grad = weight_grads(*all_normed, gnear, gfar)
    from_low, from_high = after((from_low, from_high), key_grad, value_grad)
    last_low = shifted((wide(up_low) + wide(from_low)).astype(BF16), 1)
    last_high = shifted((wide(down_high) + wide(from_high)).astype(BF16), -1)
    summed_low = wide(kept[: segs // 2]) + wide(got_low) + wide(last_low)
    summed_high = wide(kept[segs // 2 :]) + wide(got_high) + wide(last_high)
    summed_a = above(summed_low, summed_high).astype(BF16).reshape(plane, half, HD)

    arrived_b, summed_a = lax.optimization_barrier((arrived_b, summed_a))
    arrived_a = over_plane(summed_a)
    kept_b, dots, to_1, to_2, to_3 = merge_b(arrived_b, half)
    received = (shifted(to_1, 1), shifted(to_2, 2), shifted(to_3, -1))
    value_b, own_scale, mean = finish_b(place, norm_gain, block, scale_a, scale_b, kept_b, dots, received)
    result = finish_a(place, norm_gain, block, own_scale, mean, swapped(value_b), arrived_a)
    return context[None], query_grad[None], key_grad[None], value_grad[None], result


def solution(mesh):
    fine = Mesh(mesh.devices.reshape(4, 2, 2, 4, 2), AXES)
    seg, tp = ("y", "xh"), ("xl", "z", "c")
    heads = P(seg, None, tp)
    return jax.shard_map(
        local,
        mesh=fine,
        in_specs=(P(seg, tp), P(), heads, heads, heads, heads),
        out_specs=(heads, heads, heads, heads, P(seg, tp)),
        check_vma=False,
    )
```

```python
import functools

import jax
import jax.numpy as jnp
from jax import lax
from jax.experimental import pallas as pl
from jax.experimental.pallas import tpu as pltpu
from jax.sharding import Mesh
from jax.sharding import PartitionSpec as P

HD = 256
AXES = ("y", "xh", "xl", "z", "c")
PLANE = ("y", "xh", "xl")
RING = 4
EXTRA = 16
EPS = 1e-06
F32 = jnp.float32
BF16 = jnp.bfloat16
MIB = 2**20
VMEM = pl.BlockSpec(memory_space=pltpu.VMEM)
SMEM = pl.BlockSpec(memory_space=pltpu.SMEM)
ANYWHERE = pl.BlockSpec(memory_space=pl.ANY)


def dot(a, b, contract):
    return lax.dot_general(a, b, ((contract[:1], contract[1:]), ((), ())), preferred_element_type=F32)


def nn(a, b):
    return dot(a, b, (1, 0))


def nt(a, b):
    return dot(a, b, (1, 1))


def tn(a, b):
    return dot(a, b, (0, 0))


def beside(*values):
    return jnp.concatenate(values, axis=1)


def above(*values):
    return jnp.concatenate(values, axis=0)


def limits(mib):
    return pltpu.CompilerParams(vmem_limit_bytes=mib * MIB)


def cost(flops, mib, transcendentals=0):
    return pl.CostEstimate(flops=flops, bytes_accessed=int(mib * MIB), transcendentals=transcendentals)


def stage_body(*refs):
    sources, (first_ref, second_ref) = refs[:-2], refs[-2:]
    for i, source in enumerate(sources):
        first_ref[0, :, i * HD : (i + 1) * HD] = source[:HD]
        second_ref[0, :, i * HD : (i + 1) * HD] = source[HD:]


def staged(weights):
    count, blocks = len(weights), weights[0].shape[0] // (2 * HD)
    block = pl.BlockSpec((1, HD, count * HD), lambda i: (i, 0, 0))
    out = pltpu.HBM((blocks, HD, count * HD), BF16)
    return pl.pallas_call(
        stage_body,
        grid=(blocks,),
        in_specs=[pl.BlockSpec((2 * HD, HD), lambda i: (i, 0))] * count,
        out_specs=[block] * 2,
        out_shape=[out] * 2,
        compiler_params=limits(8),
        cost_estimate=cost(0, 16),
        name="stage",
    )(*[in_hbm(w) for w in weights])


def project_body(pieces, z_ref, gain_ref, *refs):
    xs = refs[: len(pieces)]
    w_refs, refs = refs[len(pieces) : len(pieces) + 2], refs[len(pieces) + 2 :]
    own_ref, sib_ref, scale_ref, normed_ref, held, rows_low, weights, x_sem, w_sem, out_sem = refs
    blocks, segs, part, width = held.shape
    rows = segs * part
    z = z_ref[0]
    copies = []
    for (distance, first, depth), x in zip(pieces, xs):
        for side in range(2):
            place = side * RING + lax.rem(z + distance, RING)
            source = x.at[:, side] if depth is None else x.at[:, side, depth]
            target = held.at[place, pl.ds(first, source.shape[0])]
            copies.append(pltpu.make_async_copy(source, target, x_sem.at[len(copies)]))
    loads = [pltpu.make_async_copy(w, weights.at[i], w_sem.at[i]) for i, w in enumerate(w_refs)]
    for copy in copies + loads:
        copy.start()
    for copy in copies:
        copy.wait()
    squares = jnp.zeros((rows, 128), F32)
    for p in range(blocks):
        wide = held[p].reshape(rows, width).astype(F32)
        wide = wide * wide
        for i in range(width // 128):
            squares += wide[:, i * 128 : (i + 1) * 128]
    scale = lax.rsqrt(jnp.sum(squares, axis=1, keepdims=True) / (blocks * width) + EPS)
    scale_ref[...] = scale
    for p in range(blocks):
        wide = held[p].reshape(rows, width).astype(F32)
        rows_low[:, p * width : (p + 1) * width] = (wide * scale * gain_ref[p]).astype(BF16)
    out = pltpu.make_async_copy(rows_low, normed_ref, out_sem)
    out.start()
    total = 0.0
    for i, load in enumerate(loads):
        load.wait()
        columns = beside(*[rows_low[:, (2 * p + i) * HD : (2 * p + i + 1) * HD] for p in range(blocks)])
        total += nn(columns, weights[i].reshape(blocks * HD, 4 * HD))
    own_ref[...] = total[:, : 2 * HD].astype(BF16)
    sib_ref[...] = total[:, 2 * HD :].astype(BF16)
    out.wait()


def project(pieces, xs, z, gain, weights, segs, name):
    part, width = xs[0].shape[-2:]
    blocks = gain.shape[0] // width
    rows = segs * part
    return pl.pallas_call(
        functools.partial(project_body, pieces),
        in_specs=[SMEM, VMEM] + [ANYWHERE] * (len(xs) + 2),
        out_specs=[VMEM, VMEM, VMEM, ANYWHERE],
        out_shape=[
            jax.ShapeDtypeStruct((rows, 2 * HD), BF16),
            jax.ShapeDtypeStruct((rows, 2 * HD), BF16),
            jax.ShapeDtypeStruct((rows, 1), F32),
            jax.ShapeDtypeStruct((rows, blocks * width), BF16),
        ],
        scratch_shapes=[
            pltpu.VMEM((blocks, segs, part, width), BF16),
            pltpu.VMEM((rows, blocks * width), BF16),
            pltpu.VMEM((2, blocks, HD, 4 * HD), BF16),
            pltpu.SemaphoreType.DMA((2 * len(xs),)),
            pltpu.SemaphoreType.DMA((2,)),
            pltpu.SemaphoreType.DMA(()),
        ],
        compiler_params=limits(24),
        cost_estimate=cost(2 * rows * blocks * width * 4 * HD, 12),
        name=name,
    )(z, gain.reshape(blocks, 1, width), *xs, *[in_hbm(w) for w in weights])


def pieces_of(dots):
    high = dots.astype(BF16).astype(F32)
    shape = (EXTRA, dots.shape[1])
    row = lax.broadcasted_iota(jnp.int32, shape, 0)
    low = jnp.broadcast_to(dots - high, shape)
    return jnp.where(row == 0, jnp.broadcast_to(high, shape), jnp.where(row == 1, low, 0.0)).astype(BF16)


def in_four_rows(dots):
    left, right = pieces_of(dots[:, :HD]).astype(F32), pieces_of(dots[:, HD:]).astype(F32)
    row = lax.broadcasted_iota(jnp.int32, left.shape, 0)
    later = jnp.where(row == 2, right[0:1], jnp.where(row == 3, right[1:2], 0.0))
    return jnp.where(row < 2, left, later).astype(BF16)


def dots_of(rows):
    return beside(rows[0:1] + rows[1:2], rows[2:3] + rows[3:4])


def attend_body(tile, q_ref, dc_ref, near_a, near_b, far_a, far_b, ctx_ref, qg_ref, gnear_ref, gfar_ref, near_dots, gkeys, gvalues):
    kv = above(near_a[...], near_b[...], far_a[...], far_b[...])
    k, v = kv[:, :HD], kv[:, HD:]
    half = kv.shape[0] // 2
    scale = HD ** (-0.5)
    row_products = jnp.zeros((8, kv.shape[0]), F32)
    for i in range(q_ref.shape[0] // tile):
        here = slice(i * tile, (i + 1) * tile)
        q, dc = q_ref[here], dc_ref[here]
        scores = nt(q, k) * scale
        expo = jnp.exp(scores - jnp.max(scores, axis=-1, keepdims=True))
        attend = expo * (1.0 / jnp.sum(expo, axis=-1, keepdims=True))
        low = attend.astype(BF16)
        ctx_ref[here] = nn(low, v).astype(BF16)
        gattend = nt(dc, v)
        dots = jnp.sum(gattend * attend, axis=-1, keepdims=True)
        gscores = attend * (gattend - dots)
        both = gscores * scores + attend * gattend
        row_products += jnp.sum(both.reshape(tile // 8, 8, kv.shape[0]), axis=0)
        gscores = (gscores * scale).astype(BF16)
        qg_ref[here] = nn(gscores, k).astype(BF16)
        if i == 0:
            gkeys[...] = tn(gscores, q)
            gvalues[...] = tn(low, dc)
        else:
            gkeys[...] += tn(gscores, q)
            gvalues[...] += tn(low, dc)
    gnear_ref[:, :HD] = gkeys[:half].astype(BF16)
    gnear_ref[:, HD:] = gvalues[:half].astype(BF16)
    gfar_ref[:half, :HD] = gkeys[half:].astype(BF16)
    gfar_ref[:half, HD:] = gvalues[half:].astype(BF16)
    row_products = jnp.sum(row_products, axis=0, keepdims=True)
    near_dots[...] = row_products[:, :half]
    gfar_ref[half:] = pieces_of(row_products[:, half:])


def attention(q, dc, near_a, near_b, far_a, far_b, tile=256):
    targets, half = q.shape[0], 2 * near_a.shape[0]
    return pl.pallas_call(
        functools.partial(attend_body, tile),
        in_specs=[VMEM] * 6,
        out_specs=[VMEM] * 5,
        out_shape=[jax.ShapeDtypeStruct((targets, HD), BF16)] * 2
        + [
            jax.ShapeDtypeStruct((half, 2 * HD), BF16),
            jax.ShapeDtypeStruct((half + EXTRA, 2 * HD), BF16),
            jax.ShapeDtypeStruct((1, half), F32),
        ],
        scratch_shapes=[pltpu.VMEM((2 * half, HD), F32)] * 2,
        compiler_params=limits(20),
        cost_estimate=cost(12 * targets * 2 * half * HD, 4, targets * 2 * half),
        name="attention",
    )(q, dc, near_a, near_b, far_a, far_b)


def feature_block(z, rows, w_ref, distance, side):
    return nt(rows, w_ref[side * RING + lax.rem(z + distance, RING)]).astype(BF16)


def back_b_body(z_ref, own_ref, sib_ref, dots_ref, w_ref, out_ref, stage, out_sem):
    half = own_ref.shape[0]
    segs = out_ref.shape[0]
    part = half // segs // 2
    rows = beside(own_ref[...], sib_ref[:half])
    outs = []
    for distance in range(RING):
        at = distance * 2 * part
        for side in range(2):
            value = feature_block(z_ref[0], rows, w_ref, distance, side).reshape(2, segs, part, HD)
            for k in range(2):
                stage[:, side, at + k * part : at + (k + 1) * part] = value[k]
        size = 2 * part
        if distance == RING - 1:
            extra = sib_ref[half:].astype(F32)
            pieces = in_four_rows(dots_ref[...] + extra[0:1] + extra[1:2])
            stage[:, :, at + size :] = jnp.broadcast_to(pieces, (segs, 2, EXTRA, HD))
            size += EXTRA
        outs.append(pltpu.make_async_copy(stage.at[:, :, pl.ds(at, size)], out_ref.at[:, :, pl.ds(at, size)], out_sem.at[distance]))
        outs[-1].start()
    for out in outs:
        out.wait()


def back_b(z, own, sib, dots, weights, segs):
    rows = own.shape[0]
    shape = (segs, 2, RING * rows // segs + EXTRA, HD)
    return pl.pallas_call(
        back_b_body,
        in_specs=[SMEM] + [VMEM] * 4,
        out_specs=ANYWHERE,
        out_shape=pltpu.HBM(shape, BF16),
        scratch_shapes=[
            pltpu.VMEM(shape, BF16),
            pltpu.SemaphoreType.DMA((RING,)),
        ],
        compiler_params=limits(16),
        cost_estimate=cost(2 * rows * 8 * HD * 4 * HD, 4),
        name="back_b",
    )(z, own, sib, dots, in_vmem(weights))


def back_a_body(z_ref, own_ref, sib_ref, w_ref, *outs):
    rows = beside(own_ref[...], sib_ref[: own_ref.shape[0]])
    segs = outs[-1].shape[0]
    part = rows.shape[0] // segs // 2
    lands = {2: ((0, 0), (1, segs // 2)), 1: ((2, 0), (3, segs // 2)), 3: ((4, 0), (5, segs // 2)), 0: ((6, 0),)}
    for distance in (2, 1, 3, 0):
        for side in range(2):
            value = feature_block(z_ref[0], rows, w_ref, distance, side).reshape(2, segs, part, HD)
            for index, first in lands[distance]:
                for k in range(2):
                    count = outs[index].shape[0]
                    outs[index][:, side, k * part : (k + 1) * part] = value[k, first : first + count]


def back_a(z, own, sib, weights, segs):
    rows = own.shape[0]
    half = jax.ShapeDtypeStruct((segs // 2, 2, rows // segs, HD), BF16)
    full = jax.ShapeDtypeStruct((segs, 2, rows // segs, HD), BF16)
    return pl.pallas_call(
        back_a_body,
        in_specs=[SMEM] + [VMEM] * 3,
        out_specs=[VMEM] * 7,
        out_shape=[half] * 6 + [full],
        compiler_params=limits(16),
        cost_estimate=cost(2 * rows * 8 * HD * 4 * HD, 4),
        name="back_a",
    )(z, own, sib, in_vmem(weights))


def weights_body(near_a, near_b, far_a, far_b, gnear_ref, gfar_ref, gk_ref, gv_ref):
    rows = above(near_a[...], near_b[...], far_a[...], far_b[...])
    total = tn(rows, above(gnear_ref[...], gfar_ref[: gnear_ref.shape[0]]))
    gk_ref[...] = total[:, :HD]
    gv_ref[...] = total[:, HD:]


def weight_grads(near_a, near_b, far_a, far_b, gnear, gfar, width=512):
    rows, hidden = near_a.shape
    block = pl.BlockSpec((rows, width), lambda i: (0, i))
    near = pl.BlockSpec(gnear.shape, lambda i: (0, 0))
    far = pl.BlockSpec(gfar.shape, lambda i: (0, 0))
    out = pl.BlockSpec((width, HD), lambda i: (i, 0))
    return pl.pallas_call(
        weights_body,
        grid=(hidden // width,),
        in_specs=[block] * 4 + [near, far],
        out_specs=[out, out],
        out_shape=[jax.ShapeDtypeStruct((hidden, HD), F32)] * 2,
        compiler_params=limits(16),
        cost_estimate=cost(16 * rows * hidden * HD, 17),
        name="weight_grads",
    )(near_a, near_b, far_a, far_b, gnear, gfar)


def merge_b_body(arrived_ref, kept_ref, dots_ref, *send_refs):
    half = kept_ref.shape[0]
    total = arrived_ref[0].astype(F32)
    for i in range(1, arrived_ref.shape[0]):
        total += arrived_ref[i].astype(F32)
    kept_ref[...] = total[:half]
    both = dots_of(total[RING * half :])
    dots_ref[...] = both
    pieces = in_four_rows(both)
    for i, ref in enumerate(send_refs):
        ref[:half] = total[(i + 1) * half : (i + 2) * half].astype(BF16)
        ref[half:] = pieces


def merge_b(arrived, half):
    send = jax.ShapeDtypeStruct((half + EXTRA, HD), BF16)
    return pl.pallas_call(
        merge_b_body,
        in_specs=[VMEM],
        out_specs=[VMEM] * 5,
        out_shape=[jax.ShapeDtypeStruct((half, HD), F32), jax.ShapeDtypeStruct((1, 2 * HD), F32)] + [send] * 3,
        compiler_params=limits(16),
        cost_estimate=cost(0, 3),
        name="merge_b",
    )(arrived)


def finish_body(hidden, place_ref, gain_ref, block_ref, scale_a, scale_b, arrived_ref, kept_ref, dots_ref, r1, r2, r3,
                keep_ref, send_ref):
    core, segment, pair = place_ref[0], place_ref[1], place_ref[2]
    half = block_ref.shape[0]
    part = half // 2
    left = arrived_ref[0].astype(F32)
    for i in range(1, arrived_ref.shape[0]):
        left += arrived_ref[i].astype(F32)
    right, dots = kept_ref[...], dots_ref[...]
    for ref in (r1, r2, r3):
        right += ref[:half].astype(F32)
        dots += dots_of(ref[half:].astype(F32))
    lane = lax.broadcasted_iota(jnp.int32, (part, HD), 1)
    row = lax.broadcasted_iota(jnp.int32, (part, HD), 0)
    mine = lane == row + segment * part
    pick = lambda values: jnp.sum(jnp.where(mine, values, 0.0), axis=1, keepdims=True)
    mean = above(pick(dots[:, :HD]), pick(dots[:, HD:])) / hidden
    rows = pl.ds(pl.multiple_of(segment * part, part), part)
    scale = above(scale_a[rows], scale_b[rows])
    gain = gain_ref[pair]
    for side, total in enumerate((left, right)):
        at = slice(side * HD, (side + 1) * HD)
        value = scale * (total * gain[:, at] - block_ref[:, at].astype(F32) * scale * mean)

        @pl.when(core == side)
        def _():
            keep_ref[...] = value

        @pl.when(core != side)
        def _():
            send_ref[...] = value


def finish(place, gain, block, scale_a, scale_b, arrived, kept, dots, received):
    half, width = block.shape
    hidden = gain.shape[0]
    return pl.pallas_call(
        functools.partial(finish_body, hidden),
        in_specs=[SMEM] + [VMEM] * 10,
        out_specs=[VMEM] * 2,
        out_shape=[jax.ShapeDtypeStruct((half, HD), F32)] * 2,
        compiler_params=limits(16),
        cost_estimate=cost(0, 1),
        name="finish",
    )(place, gain.reshape(hidden // width, 1, width), block, scale_a, scale_b, arrived, kept, dots, *received)


def in_vmem(value):
    return pltpu.with_memory_space_constraint(value, pltpu.VMEM)


def in_hbm(value):
    return pltpu.with_memory_space_constraint(value, pltpu.HBM)


def swapped(value):
    return lax.ppermute(value, "c", [(0, 1), (1, 0)])


def shifted(value, by):
    return lax.ppermute(value, "z", [(i, (i + by) % RING) for i in range(RING)])


def over_plane(value):
    return lax.all_to_all(value, PLANE, 0, 0, tiled=True)


def after(values, *earlier):
    return lax.optimization_barrier((*values, *earlier))[: len(values)]


def local(memory, norm_gain, queries, key_weight, value_weight, context_grad):
    rows_own, cols_own = memory.shape
    half, width = rows_own // 2, 2 * cols_own
    part = half // 2
    core, z = lax.axis_index("c"), lax.axis_index("z")
    segment = lax.axis_index(("y", "xh"))
    pair = lax.axis_index(("xl", "z"))
    segs, plane = lax.axis_size(("y", "xh")), lax.axis_size(PLANE)
    z_array = z.astype(jnp.int32).reshape(1)
    place = jnp.stack([core, segment, pair]).astype(jnp.int32)
    wide = lambda value: value.astype(F32)

    halves = memory.reshape(2, half, cols_own)
    mine = lax.dynamic_index_in_dim(halves, core, 0, keepdims=False)
    other = swapped(lax.dynamic_index_in_dim(halves, 1 - core, 0, keepdims=False))
    block = jnp.where(core == 0, beside(mine, other), beside(other, mine))
    first_a = over_plane(jnp.broadcast_to(block[:part], (plane, part, width)))
    high = block[part:]
    near_z = jnp.stack([high, shifted(high, -1), shifted(high, 2), shifted(high, 1)])
    all_b = over_plane(jnp.broadcast_to(near_z, (plane, RING, part, width)))
    all_b = all_b.reshape(segs, 2, RING, part, width)
    low_0, high_0 = first_a[: plane // 2], first_a[plane // 2 :]
    low_3, high_1 = shifted(low_0, 1), shifted(high_0, -1)
    high_3, low_1 = shifted(high_0, 1), shifted(low_0, -1)
    low_2, high_2 = shifted(low_3, 1), shifted(high_1, -1)
    deep = lambda value: value.reshape(segs // 2, 2, part, width)

    key_own, value_own = after((key_weight[0], value_weight[0]), block)
    weights = staged((key_own, value_own, swapped(key_own), swapped(value_own)))

    top = segs // 2
    pieces_a = [(0, 0, None), (3, 0, None), (3, top, None), (1, 0, None), (1, top, None), (2, 0, None), (2, top, None)]
    xs_a = [first_a.reshape(segs, 2, part, width)] + [deep(v) for v in (low_3, high_3, low_1, high_1, low_2, high_2)]
    xs_a = [in_hbm(x) for x in xs_a]
    own_a, sib_a, scale_a, normed_a = project(pieces_a, xs_a, z_array, norm_gain, weights, segs, "project_a")
    far_a = swapped(sib_a)
    all_b, = after((all_b,), own_a)
    normed_far_a = swapped(after((normed_a,), all_b, far_a)[0])
    pieces_b = [(d, 0, d) for d in range(RING)]
    own_b, sib_b, scale_b, normed_b = project(pieces_b, [all_b] * RING, z_array, norm_gain, weights, segs, "project_b")
    far_b = swapped(sib_b)
    normed_far_b = swapped(after((normed_b,), far_b)[0])
    context, query_grad, gnear, gfar, near_dots = attention(queries[0], context_grad[0], own_a, own_b, far_a, far_b)
    gsib = swapped(gfar)

    parts_b = back_b(z_array, gnear, gsib, near_dots, weights[1], segs)
    arrived_b = over_plane(parts_b.reshape(plane, RING * half + EXTRA, HD))
    z_later, = after((z_array,), parts_b)
    opp_low, opp_high, up_low, up_high, down_low, down_high, kept = back_a(z_later, gnear, gsib, weights[0], segs)
    from_low, from_high = shifted(opp_low, 1), shifted(opp_high, -1)
    got_high, got_low = shifted(up_high, 1), shifted(down_low, -1)
    all_normed = (normed_a, normed_b, normed_far_a, normed_far_b)
    key_grad, value_grad = weight_grads(*all_normed, gnear, gfar)
    from_low, from_high = after((from_low, from_high), key_grad, value_grad)
    last_low = shifted((wide(up_low) + wide(from_low)).astype(BF16), 1)
    last_high = shifted((wide(down_high) + wide(from_high)).astype(BF16), -1)
    summed_low = wide(kept[: segs // 2]) + wide(got_low) + wide(last_low)
    summed_high = wide(kept[segs // 2 :]) + wide(got_high) + wide(last_high)
    summed_a = above(summed_low, summed_high).astype(BF16).reshape(plane, half, HD)

    arrived_b, summed_a = lax.optimization_barrier((arrived_b, summed_a))
    arrived_a = over_plane(summed_a)
    kept_b, dots, to_1, to_2, to_3 = merge_b(arrived_b, half)
    received = (shifted(to_1, 1), shifted(to_2, 2), shifted(to_3, -1))
    keep, send = finish(place, norm_gain, block, scale_a, scale_b, arrived_a, kept_b, dots, received)
    came = swapped(send)
    result = jnp.where(core == 0, above(keep, came), above(came, keep))
    return context[None], query_grad[None], key_grad[None], value_grad[None], result


def solution(mesh):
    fine = Mesh(mesh.devices.reshape(4, 2, 2, 4, 2), AXES)
    seg, tp = ("y", "xh"), ("xl", "z", "c")
    heads = P(seg, None, tp)
    return jax.shard_map(
        local,
        mesh=fine,
        in_specs=(P(seg, tp), P(), heads, heads, heads, heads),
        out_specs=(heads, heads, heads, heads, P(seg, tp)),
        check_vma=False,
    )
```
